32 devices in a mesh: blk: 8 (over z, x), head: 4 (over y, core).
Axes of the slice: x: 2, y: 2, z: 4, core: 2. Of those that a mesh axis runs over, the one named last changes fastest.
Arguments:
- inputs: bfloat16 [16384, 768], P(('blk', 'head')), may hold values from -6 to 6
- segments: int32 [16384], replicated, may hold values from 0 to 15, never falling along the last dimension, each value on 1 to 2048 neighbouring positions
- cotangent: bfloat16 [16384, 768], P(('blk', 'head')), may hold values from -6 to 6
- w_qkv: bfloat16 [768, 2304], P(('blk', 'head')), may hold values from -0.3125 to 0.3125
- q_bias: bfloat16 [768], P(('blk', 'head')), may hold values from -3 to 3
- v_bias: bfloat16 [768], P(('blk', 'head')), may hold values from -3 to 3
- w_out: bfloat16 [768, 768], P(('blk', 'head')), may hold values from -1.25 to 1.25
- out_bias: bfloat16 [768], P(('blk', 'head')), may hold values from -3 to 3
- ln1_gain: bfloat16 [768], P(('blk', 'head')), may hold values from 0.5 to 1.5
- ln1_bias: bfloat16 [768], P(('blk', 'head')), may hold values from -2 to 2
- w_in: bfloat16 [768, 3072], P(('blk', 'head')), may hold values from -0.21875 to 0.21875
- in_bias: bfloat16 [3072], P(('blk', 'head')), may hold values from -3 to 3
- w_down: bfloat16 [3072, 768], P(('blk', 'head')), may hold values from -0.15625 to 0.15625
- down_bias: bfloat16 [768], P(('blk', 'head')), may hold values from -3 to 3
- ln2_gain: bfloat16 [768], P(('blk', 'head')), may hold values from 0.5 to 1.5
- ln2_bias: bfloat16 [768], P(('blk', 'head')), may hold values from -2 to 2
Outputs:
- outputs: bfloat16 [16384, 768], P(('blk', 'head'))
- d_inputs: bfloat16 [16384, 768], P(('blk', 'head'))
- d_w_qkv: float32 [768, 2304], P(('blk', 'head'))
- d_q_bias: float32 [768], P(('blk', 'head'))
- d_v_bias: float32 [768], P(('blk', 'head'))
- d_w_out: float32 [768, 768], P(('blk', 'head'))
- d_out_bias: float32 [768], P(('blk', 'head'))
- d_ln1_gain: float32 [768], P(('blk', 'head'))
- d_ln1_bias: float32 [768], P(('blk', 'head'))
- d_w_in: float32 [768, 3072], P(('blk', 'head'))
- d_in_bias: float32 [3072], P(('blk', 'head'))
- d_w_down: float32 [3072, 768], P(('blk', 'head'))
- d_down_bias: float32 [768], P(('blk', 'head'))
- d_ln2_gain: float32 [768], P(('blk', 'head'))
- d_ln2_bias: float32 [768], P(('blk', 'head'))
The draws below stay inside these ranges and needn't reach their ends.
Inputs may be any that keep to these rules, and one draw needn't show every extreme that they name: `segments`: segment numbers never fall along the tokens; every number from 0 to 15 has 1 to 2048 tokens, and some number has exactly 2048.
All inputs are finite; a program needn't handle non-finite values.
Results may differ from the reference program's by a relative error of at most 0.017.
The reference program's roundings to bfloat16 on the way count: a program that leaves them out, or rounds other values in their place, can miss the bound.
Values may be sent and summed in bfloat16 or wider, within the bound.
A program may use at most 128 MiB of HBM per device.

```python
import math
import jax
import jax.numpy as jnp
import numpy as np
from jax import lax

D = 768
HEADS = 12
HEAD_DIM = 64
FF = 3072
TOK_DEV = 512
TOKENS = 16384
DOC_MOST = 2048
SEGS = 16
N_HEAD = 4


def with_spikes(drawn, rng, source, target, parts, factor):
    owner, partner = [(jnp.arange(drawn.shape[position]) // (drawn.shape[position] // parts)).reshape([-1 if axis == position else 1 for axis in range(drawn.ndim)]) for position in (source, target)]
    chosen = jax.random.permutation(rng, parts)[partner]
    strong = (owner == chosen) | (owner == (partner + parts // 2) % parts)
    return jnp.where(strong, factor * drawn, drawn)


def shard_levels(key, shape, split, low, top_value):
    def one(position, blocks):
        steps = jax.random.uniform(jax.random.fold_in(jax.random.fold_in(key, 6), position), (blocks,), jnp.float32, low / len(split), top_value / len(split))
        return jnp.repeat(jnp.exp(steps), shape[position] // blocks).reshape((-1,) + (1,) * (len(shape) - position - 1))

    level = one(*split[0])
    for cut in split[1:]:
        level = level * one(*cut)
    return level


def split_up(amount, total, reach, lean):
    portions = [(1 << 20) // math.isqrt(rank ** lean) + 1 for rank in range(2, amount + 1)]
    rest, holding = total - reach - (amount - 1), [1] * (amount - 1)
    while rest > 0:
        candidates = [i for i in range(amount - 1) if holding[i] < reach]
        pool, budget = sum([portions[i] for i in candidates]), rest
        for i in candidates:
            more = min(reach - holding[i], max(1, budget * portions[i] // pool), rest)
            holding[i] = holding[i] + more
            rest = rest - more
    return np.array([reach] + holding)


def ragged_sizes(key, count, total, most, skew):
    if count == 2:
        one = jax.random.randint(key, (), max(1, total - most), min(most, total - 1) + 1)
        return jnp.stack([one, total - one])
    lengths = jnp.asarray(split_up(count, total, most, skew), jnp.int32)
    twos = (count - 1) // 2
    source_of, taker = lengths[1:1 + 2 * twos:2], lengths[2:2 + 2 * twos:2]
    margin = jnp.minimum(source_of - 1, most - taker)
    moved = jax.random.randint(jax.random.fold_in(key, 1), (twos,), 0, 1 << 20) % (margin + 1)
    lengths = lengths.at[1:1 + 2 * twos:2].set(source_of - moved).at[2:2 + 2 * twos:2].set(taker + moved)
    return lengths[jax.random.permutation(jax.random.fold_in(key, 2), count)]


def noise(own_key, dims, scale, reach, split=(), kind=jnp.bfloat16):
    array = scale * jax.random.normal(own_key, dims, jnp.float32)
    if split:
        array = array * shard_levels(own_key, dims, split, -0.22, 0.18)
    return jnp.clip(array, -reach, reach).astype(kind)


def heavy_noise(rng, dims, width, limit, shards, heavy, held_as=jnp.bfloat16):
    values = width * jax.random.normal(rng, dims, jnp.float32)
    if shards:
        values = values * shard_levels(rng, dims, shards, -0.22, 0.18)
    return jnp.clip(with_spikes(values, jax.random.fold_in(rng, 3), *heavy), -limit, limit).astype(held_as)


def setup_inputs(seed: int = 0) -> dict:
    arg_keys = jax.random.split(jax.random.key(seed), 17)
    return {
        "inputs": noise(arg_keys[0], (TOKENS, D), 1.0, 6.0, ((0, 32),)),
        "segments": jnp.searchsorted(jnp.cumsum(ragged_sizes(arg_keys[1], SEGS, TOKENS, DOC_MOST, 2)), jnp.arange(TOKENS), side="right").astype(jnp.int32),
        "cotangent": heavy_noise(arg_keys[2], (TOKENS, D), 1.0, 6.0, ((0, 32),), (0, 1, 32, 2.75)),
        "w_qkv": noise(arg_keys[3], (D, 3 * D), (D // 2) ** -0.5, 0.3125, ((0, 32),)),
        "q_bias": noise(arg_keys[4], (D,), 0.5, 3.0, ((0, 32),)),
        "v_bias": noise(arg_keys[5], (D,), 0.5, 3.0, ((0, 32),)),
        "w_out": noise(arg_keys[6], (D, D), (D // 32) ** -0.5, 1.25, ((0, 32),)),
        "out_bias": noise(arg_keys[7], (D,), 0.5, 3.0, ((0, 32),)),
        "ln1_gain": jnp.clip(1.0 + 0.1 * jax.random.normal(arg_keys[8], (D,), jnp.float32), 0.5, 1.5).astype(jnp.bfloat16),
        "ln1_bias": noise(arg_keys[9], (D,), 0.3, 2.0, ((0, 32),)),
        "w_in": noise(arg_keys[10], (D, FF), D ** -0.5, 0.21875, ((0, 32),)),
        "in_bias": noise(arg_keys[11], (FF,), 0.5, 3.0, ((0, 32),)),
        "w_down": noise(arg_keys[12], (FF, D), (FF // 2) ** -0.5, 0.15625, ((0, 32),)),
        "down_bias": noise(arg_keys[13], (D,), 0.5, 3.0, ((0, 32),)),
        "ln2_gain": jnp.clip(1.0 + 0.1 * jax.random.normal(arg_keys[14], (D,), jnp.float32), 0.5, 1.5).astype(jnp.bfloat16),
        "ln2_bias": noise(arg_keys[15], (D,), 0.3, 2.0, ((0, 32),)),
    }


@jax.custom_vjp
def low(v):
    return lax.optimization_barrier(v.astype(jnp.bfloat16)).astype(jnp.float32)

@jax.custom_vjp
def low_back(v):
    return v

def low_keep(v):
    return (low(v), None)

def low_pass(kept, grad):
    return (grad,)

def back_keep(v):
    return (v, None)

def back_low(kept, grad):
    return (low(grad),)
low.defvjp(low_keep, low_pass)
low_back.defvjp(back_keep, back_low)

def matmul(left, right):
    return jnp.dot(left, right, precision=lax.Precision.HIGHEST)

def layer_norm(values, gain, shift_vec):
    centre = lax.optimization_barrier(jnp.mean(values, axis=-1, keepdims=True))
    centered = values - centre
    spread = lax.optimization_barrier(jnp.mean(centered * centered, axis=-1, keepdims=True))
    return centered * lax.rsqrt(spread + 1e-05) * gain + shift_vec

def attention(queries, key_rows, values, segments):
    block_len = N_HEAD * TOK_DEV
    tile_rows = min(512, block_len)
    pad_spec = ((block_len, block_len), (0, 0), (0, 0))
    keys_pad = jnp.pad(key_rows, pad_spec)
    values_pad = jnp.pad(values, pad_spec)
    labels = jnp.concatenate([jnp.full((block_len,), -1, jnp.int32), segments.astype(jnp.int32), jnp.full((block_len,), 1073741824, jnp.int32)])
    score_scale = HEAD_DIM ** (-0.5)
    window = tile_rows + 2 * block_len

    def one_tile(first_row):
        q_tile = lax.dynamic_slice_in_dim(queries, first_row, tile_rows, 0)
        k_tile = lax.dynamic_slice_in_dim(keys_pad, first_row, window, 0)
        v_tile = lax.dynamic_slice_in_dim(values_pad, first_row, window, 0)
        q_label = lax.dynamic_slice_in_dim(segments.astype(jnp.int32), first_row, tile_rows, 0)
        k_label = lax.dynamic_slice_in_dim(labels, first_row, window, 0)
        scores = low_back(jnp.einsum('qhd,khd->hqk', q_tile, k_tile, precision=lax.Precision.HIGHEST) * score_scale)
        same_doc = (q_label[:, None] == k_label[None, :])[None]
        softmax_w = jax.nn.softmax(jnp.where(same_doc, scores, -1e+30), axis=-1)
        return jnp.einsum('hqk,khd->qhd', low(softmax_w), v_tile, precision=lax.Precision.HIGHEST)
    first_rows = jnp.arange(TOKENS // tile_rows, dtype=jnp.int32) * tile_rows
    tile_out = lax.map(jax.checkpoint(one_tile), first_rows)
    return tile_out.reshape(TOKENS, HEADS * HEAD_DIM)

def layer_forward(x_in, w_qkv, q_bias, v_bias, w_out, out_bias, ln1_gain, ln1_bias, w_in, in_bias, w_down, down_bias, ln2_gain, ln2_bias, segments):
    qkv_bias = jnp.concatenate([q_bias, jnp.zeros_like(q_bias), v_bias])
    mixed_qkv = low(low_back(matmul(x_in, w_qkv) + qkv_bias))
    queries = mixed_qkv[:, :D].reshape(TOKENS, HEADS, HEAD_DIM)
    key_rows = mixed_qkv[:, D:2 * D].reshape(TOKENS, HEADS, HEAD_DIM)
    values = mixed_qkv[:, 2 * D:].reshape(TOKENS, HEADS, HEAD_DIM)
    attended = low(low_back(attention(queries, key_rows, values, segments)))
    branch = low_back(matmul(attended, w_out) + out_bias)
    first_sum = x_in + branch
    normed = layer_norm(first_sum, ln1_gain, ln1_bias)
    hidden_pre = low_back(matmul(low(normed), w_in) + in_bias)
    activated = low(jax.nn.gelu(hidden_pre, approximate=False))
    second_sum = normed + low_back(matmul(activated, w_down) + down_bias)
    return layer_norm(second_sum, ln2_gain, ln2_bias)

def reference(inputs, segments, cotangent, w_qkv, q_bias, v_bias, w_out, out_bias, ln1_gain, ln1_bias, w_in, in_bias, w_down, down_bias, ln2_gain, ln2_bias):
    weights = tuple((member.astype(jnp.float32) for member in (w_qkv, q_bias, v_bias, w_out, out_bias, ln1_gain, ln1_bias, w_in, in_bias, w_down, down_bias, ln2_gain, ln2_bias)))

    def layer_fn(x_in, *params):
        return layer_forward(x_in, *params, segments)
    outputs, pullback = jax.vjp(layer_fn, inputs.astype(jnp.float32), *weights)
    grads_all = pullback(cotangent.astype(jnp.float32))
    return (outputs.astype(jnp.bfloat16), grads_all[0].astype(jnp.bfloat16), grads_all[1], grads_all[2], grads_all[3], grads_all[4], grads_all[5], grads_all[6], grads_all[7], grads_all[8], grads_all[9], grads_all[10], grads_all[11], grads_all[12], grads_all[13])
```

```python
import functools

import jax
import jax.numpy as jnp
from jax import lax
from jax.experimental import pallas as pl
from jax.experimental.pallas import tpu as pltpu
from jax.sharding import PartitionSpec as P

HEAD_DIM = 64
HD = 64


def padded(block, sides, width):
    for axis, dim in sides:
        count = lax.axis_size(axis)
        forward = [(i, i + 1) for i in range(count - 1)]
        backward = [(target, source) for source, target in forward]
        low = lax.ppermute(
            lax.slice_in_dim(block, block.shape[dim] - width, None, axis=dim), axis, forward
        )
        high = lax.ppermute(lax.slice_in_dim(block, 0, width, axis=dim), axis, backward)
        block = jnp.concatenate([low, block, high], axis=dim)
    return block


def from_behind(value, axis, steps):
    count = lax.axis_size(axis)
    first, last = (max(0, -steps), min(count, count - steps))
    return lax.ppermute(value, axis, [(source, source + steps) for source in range(first, last)])


def layer_norm(values, gain, shift_vec):
    centre = jnp.mean(values, axis=-1, keepdims=True)
    centered = values - centre
    spread = jnp.mean(centered * centered, axis=-1, keepdims=True)
    return centered * lax.rsqrt(spread + 1e-05) * gain + shift_vec


def gelu_exact(values):
    return jax.nn.gelu(values, approximate=False)


F32=jnp.float32; BF=jnp.bfloat16
NEG=-1e30

def dot(a,b): return jnp.dot(a,b,preferred_element_type=F32)

def fwd_body(lo_ref,hi_ref,qT_ref,k_ref,vT_ref,qs_ref,qe_ref,oT_ref,lse_ref,*,TQ,TK,H):
    nq=qT_ref.shape[2]//TQ
    def qloop(i,_):
        qsl=pl.ds(pl.multiple_of(i*TQ,TQ),TQ)
        qs=qs_ref[:,qsl]; qe=qe_ref[:,qsl]
        qts=[qT_ref[h,:,qsl]*BF(HD**-0.5) for h in range(H)]
        def kloop(j,c):
            ksl=pl.ds(pl.multiple_of(j*TK,TK),TK)
            pos=lax.broadcasted_iota(jnp.int32,(TK,TQ),0)+j*TK
            mask=(pos>=qs)&(pos<qe)
            out=[]
            for h in range(H):
                m,l,acc=c[h]
                s=jnp.where(mask,dot(k_ref[h,ksl,:],qts[h]),NEG)
                mn=jnp.maximum(m,jnp.max(s,axis=0,keepdims=True))
                p=jnp.exp(s-mn)
                al=jnp.exp(m-mn)
                l=l*al+jnp.sum(p,axis=0,keepdims=True)
                acc=acc*al+dot(vT_ref[h,:,ksl],p.astype(BF))
                out.append((mn,l,acc))
            return tuple(out)
        init=tuple((jnp.full((1,TQ),NEG,F32),jnp.zeros((1,TQ),F32),jnp.zeros((HD,TQ),F32)) for _ in range(H))
        res=lax.fori_loop(lo_ref[i],hi_ref[i],kloop,init)
        for h in range(H):
            m,l,acc=res[h]
            oT_ref[h,:,qsl]=acc/l
            lse_ref[h:h+1,qsl]=m+jnp.log(l)
        return 0
    lax.fori_loop(0,nq,qloop,0)

def attn_fwd(qT,k,vT,lo,hi,qs,qe,TQ=256,TK=256):
    H,_,N=qT.shape
    V=pl.BlockSpec(memory_space=pltpu.VMEM); S=pl.BlockSpec(memory_space=pltpu.SMEM)
    return pl.pallas_call(functools.partial(fwd_body,TQ=TQ,TK=TK,H=H),
        out_shape=(jax.ShapeDtypeStruct((H,HD,N),F32),jax.ShapeDtypeStruct((H,N),F32)),
        in_specs=[S,S,V,V,V,V,V],out_specs=(V,V),
        compiler_params=pltpu.CompilerParams(vmem_limit_bytes=48<<20),name="attn_fwd",
        cost_estimate=pl.CostEstimate(flops=int(4e9),bytes_accessed=int(2e7),transcendentals=int(1.5e7)))(lo,hi,qT,k,vT,qs,qe)

def bwdA_body(lo_ref,hi_ref,qT_ref,q_ref,doT_ref,do_ref,lse_ref,dl_ref,k_ref,kT_ref,v_ref,qs_ref,qe_ref,
              dqT_ref,dk_ref,dv_ref,*,T,H,nb):
    dqT_ref[...]=jnp.zeros_like(dqT_ref)
    dk_ref[...]=jnp.zeros_like(dk_ref)
    dv_ref[...]=jnp.zeros_like(dv_ref)
    def qloop(i,_):
        qsl=pl.ds(pl.multiple_of(i*T,T),T)
        qs=qs_ref[:,qsl]; qe=qe_ref[:,qsl]
        def pair(j,own):
            ksl=pl.ds(pl.multiple_of(j*T,T),T)
            osl=pl.ds(pl.multiple_of((j-nb)*T,T),T)
            pos=lax.broadcasted_iota(jnp.int32,(T,T),0)+j*T
            mask=(pos>=qs)&(pos<qe)
            for h in range(H):
                qT=qT_ref[h,:,qsl]*BF(HD**-0.5)
                s=dot(k_ref[h,ksl,:],qT)
                p=jnp.where(mask,jnp.exp(s-lse_ref[h:h+1,qsl]),0.0)
                dp=dot(v_ref[h,ksl,:],doT_ref[h,:,qsl])
                ds=(p*(dp-dl_ref[h:h+1,qsl])).astype(BF)
                dqT_ref[h,:,qsl]+=dot(kT_ref[h,:,ksl],ds)
                if own:
                    dv_ref[h,osl,:]+=dot(p.astype(BF),do_ref[h,qsl,:])
                    dk_ref[h,osl,:]+=dot(ds,q_ref[h,qsl,:])
        lo=lo_ref[i]; hi=hi_ref[i]
        lax.fori_loop(jnp.maximum(lo,nb),jnp.minimum(hi,2*nb),lambda j,_:(pair(j,True),0)[1],0)
        lax.fori_loop(lo,jnp.minimum(hi,nb),lambda j,_:(pair(j,False),0)[1],0)
        lax.fori_loop(jnp.maximum(lo,2*nb),hi,lambda j,_:(pair(j,False),0)[1],0)
        return 0
    lax.fori_loop(0,nb,qloop,0)
    dqT_ref[...]=dqT_ref[...]*(HD**-0.5)

def attn_bwdA(qT,q,doT,do,lse,dl,k,kT,v,lo,hi,qs,qe,T=256):
    H,_,N=qT.shape
    V=pl.BlockSpec(memory_space=pltpu.VMEM); S=pl.BlockSpec(memory_space=pltpu.SMEM)
    return pl.pallas_call(functools.partial(bwdA_body,T=T,H=H,nb=N//T),
        out_shape=(jax.ShapeDtypeStruct((H,HD,N),F32),jax.ShapeDtypeStruct((H,N,HD),F32),jax.ShapeDtypeStruct((H,N,HD),F32)),
        in_specs=[S,S]+[V]*11,out_specs=(V,V,V),
        compiler_params=pltpu.CompilerParams(vmem_limit_bytes=56<<20),name="attn_bwdA",
        cost_estimate=pl.CostEstimate(flops=int(1e10),bytes_accessed=int(4e7),transcendentals=int(1.5e7)))(lo,hi,qT,q,doT,do,lse,dl,k,kT,v,qs,qe)


def bwdB_body(lo_ref,hi_ref,qT_ref,q_ref,doT_ref,do_ref,lse_ref,dl_ref,k_ref,v_ref,dk0_ref,dv0_ref,qs_ref,qe_ref,
              dk_ref,dv_ref,*,T,H,nb):
    dk_ref[...]=dk0_ref[...]
    dv_ref[...]=dv0_ref[...]
    def kloop(j,_):
        osl=pl.ds(pl.multiple_of(j*T,T),T)
        def pair(i):
            qsl=pl.ds(pl.multiple_of(i*T,T),T)
            pos=lax.broadcasted_iota(jnp.int32,(T,T),0)+(j+nb)*T
            mask=(pos>=qs_ref[:,qsl])&(pos<qe_ref[:,qsl])
            for h in range(H):
                qT=qT_ref[h,:,qsl]*BF(HD**-0.5)
                s=dot(k_ref[h,osl,:],qT)
                p=jnp.where(mask,jnp.exp(s-lse_ref[h:h+1,qsl]),0.0)
                dp=dot(v_ref[h,osl,:],doT_ref[h,:,qsl])
                ds=(p*(dp-dl_ref[h:h+1,qsl])).astype(BF)
                dv_ref[h,osl,:]+=dot(p.astype(BF),do_ref[h,qsl,:])
                dk_ref[h,osl,:]+=dot(ds,q_ref[h,qsl,:])
        lo=lo_ref[j]; hi=hi_ref[j]
        lax.fori_loop(lo,jnp.minimum(hi,nb),lambda i,_:(pair(i),0)[1],0)
        lax.fori_loop(jnp.maximum(lo,2*nb),hi,lambda i,_:(pair(i-nb),0)[1],0)
        return 0
    lax.fori_loop(0,nb,kloop,0)
    dk_ref[...]=dk_ref[...]*(HD**-0.5)

def attn_bwdB(qT,q,doT,do,lse,dl,k,v,dk0,dv0,lo,hi,qs,qe,T=256):
    H,N,_=k.shape
    V=pl.BlockSpec(memory_space=pltpu.VMEM); S=pl.BlockSpec(memory_space=pltpu.SMEM)
    return pl.pallas_call(functools.partial(bwdB_body,T=T,H=H,nb=N//T),
        out_shape=(jax.ShapeDtypeStruct((H,N,HD),F32),jax.ShapeDtypeStruct((H,N,HD),F32)),
        in_specs=[S,S]+[V]*12,out_specs=(V,V),
        compiler_params=pltpu.CompilerParams(vmem_limit_bytes=56<<20),name="attn_bwdB",
        cost_estimate=pl.CostEstimate(flops=int(4e9),bytes_accessed=int(4e7),transcendentals=int(5e6)))(lo,hi,qT,q,doT,do,lse,dl,k,v,dk0,dv0,qs,qe)

def tile_ranges(segments, first, block, tile):
    tok=jnp.arange(segments.shape[0],dtype=jnp.int32)
    return tok


def body(
    inputs,
    segments,
    cotangent,
    w_qkv,
    q_bias,
    v_bias,
    w_out,
    out_bias,
    ln1_gain,
    ln1_bias,
    w_in,
    in_bias,
    w_down,
    down_bias,
    ln2_gain,
    ln2_bias,
):
    gathered = (
        lax.all_gather(w_qkv, ("blk", "head"), axis=0, tiled=True),
        lax.all_gather(q_bias, ("blk", "head"), axis=0, tiled=True),
        lax.all_gather(v_bias, ("blk", "head"), axis=0, tiled=True),
        lax.all_gather(w_out, ("blk", "head"), axis=0, tiled=True),
        lax.all_gather(out_bias, ("blk", "head"), axis=0, tiled=True),
        lax.all_gather(ln1_gain, ("blk", "head"), axis=0, tiled=True),
        lax.all_gather(ln1_bias, ("blk", "head"), axis=0, tiled=True),
        lax.all_gather(w_in, ("blk", "head"), axis=0, tiled=True),
        lax.all_gather(in_bias, ("blk", "head"), axis=0, tiled=True),
        lax.all_gather(w_down, ("blk", "head"), axis=0, tiled=True),
        lax.all_gather(down_bias, ("blk", "head"), axis=0, tiled=True),
        lax.all_gather(ln2_gain, ("blk", "head"), axis=0, tiled=True),
        lax.all_gather(ln2_bias, ("blk", "head"), axis=0, tiled=True),
    )
    (
        g_qkv,
        g_q_bias,
        g_v_bias,
        g_out,
        g_out_bias,
        g_ln1_gain,
        g_ln1_bias,
        g_in,
        g_in_bias,
        g_down,
        g_down_bias,
        g_ln2_gain,
        g_ln2_bias,
    ) = gathered
    tok_rows, model_width = inputs.shape
    qkv_bias = jnp.concatenate(
        [
            g_q_bias.astype(jnp.float32),
            jnp.zeros((model_width,), jnp.float32),
            g_v_bias.astype(jnp.float32),
        ]
    )
    mixed_qkv = (
        (jnp.dot(inputs, g_qkv, preferred_element_type=jnp.float32) + qkv_bias)
        .astype(jnp.bfloat16)
        .reshape(tok_rows, 3, model_width)
    )
    head_rows = lax.all_to_all(mixed_qkv, "head", split_axis=2, concat_axis=0, tiled=True)
    block_rows = head_rows.shape[0]
    group_width = head_rows.shape[2]
    groups = group_width // HEAD_DIM
    kv_width = groups
    def heads_of(rows):
        return rows.reshape(rows.shape[0], groups, HEAD_DIM).transpose(1, 0, 2)
    neighbours = padded(head_rows, (("blk", 0),), block_rows)
    q_win, k_win, v_win = (heads_of(neighbours[:, n]) for n in range(3))
    q_own = q_win[:, block_rows : 2 * block_rows]
    swap = lambda a: a.transpose(0, 2, 1)
    block_index = lax.axis_index("blk")
    TILE = 512
    total = segments.shape[0]
    first = (block_index - 1) * block_rows
    padded_seg = jnp.concatenate(
        [jnp.full((block_rows,), -1, jnp.int32), segments, jnp.full((block_rows,), 1 << 30, jnp.int32)]
    )
    win_seg = lax.dynamic_slice_in_dim(padded_seg, block_index * block_rows, 3 * block_rows, 0)
    below = jnp.sum((win_seg[None, :] < win_seg[::TILE][:, None]).astype(jnp.int32), axis=1)
    upto = jnp.sum((win_seg[None, :] <= win_seg[TILE - 1 :: TILE][:, None]).astype(jnp.int32), axis=1)
    pos = jnp.arange(3 * block_rows, dtype=jnp.int32)
    newdoc = jnp.concatenate([jnp.ones((1,), bool), win_seg[1:] != win_seg[:-1]])
    qs = lax.cummax(jnp.where(newdoc, pos, 0))
    enddoc = jnp.concatenate([win_seg[1:] != win_seg[:-1], jnp.ones((1,), bool)])
    qe = lax.cummin(jnp.where(enddoc, pos + 1, 3 * block_rows), reverse=True)
    nb = block_rows // TILE
    t_lo = (below // TILE)[nb : 2 * nb]
    t_hi = ((upto - 1) // TILE + 1)[nb : 2 * nb]
    qs, qe = qs[None], qe[None]
    qs_own, qe_own = (a[:, block_rows : 2 * block_rows] for a in (qs, qe))
    qT_own = swap(q_own)
    oT, lse = attn_fwd(qT_own, k_win, swap(v_win), t_lo, t_hi, qs_own, qe_own, TILE, TILE)
    attended = oT.reshape(group_width, block_rows).T
    attended_low = attended.astype(jnp.bfloat16).reshape(block_rows, group_width)
    attended_seq = lax.all_to_all(attended_low, "head", split_axis=0, concat_axis=1, tiled=True)
    first_sum = (
        inputs.astype(jnp.float32)
        + jnp.dot(attended_seq, g_out, preferred_element_type=jnp.float32)
        + g_out_bias.astype(jnp.float32)
    )
    normed, ln1_pull = jax.vjp(
        layer_norm, first_sum, g_ln1_gain.astype(jnp.float32), g_ln1_bias.astype(jnp.float32)
    )
    normed_low = normed.astype(jnp.bfloat16)
    hidden_pre = jnp.dot(normed_low, g_in, preferred_element_type=jnp.float32) + g_in_bias.astype(
        jnp.float32
    )
    gelu_value, gelu_pull = jax.vjp(gelu_exact, hidden_pre)
    activated = gelu_value.astype(jnp.bfloat16)
    second_sum = (
        normed
        + jnp.dot(activated, g_down, preferred_element_type=jnp.float32)
        + g_down_bias.astype(jnp.float32)
    )
    outputs, ln2_pull = jax.vjp(
        layer_norm, second_sum, g_ln2_gain.astype(jnp.float32), g_ln2_bias.astype(jnp.float32)
    )
    b_qkv, b_out, b_in, b_down = g_qkv, g_out, g_in, g_down
    d_second, d_ln2_gain, d_ln2_bias = ln2_pull(cotangent.astype(jnp.float32))
    e_second = d_second.astype(jnp.bfloat16)
    d_down_bias = jnp.sum(e_second.astype(jnp.float32), axis=0)
    d_w_down = jnp.dot(activated.T, e_second, preferred_element_type=jnp.float32)
    d_activated = jnp.dot(e_second, b_down.T, preferred_element_type=jnp.float32)
    d_hidden = gelu_pull(d_activated)[0].astype(jnp.bfloat16)
    d_in_bias = jnp.sum(d_hidden.astype(jnp.float32), axis=0)
    d_w_in = jnp.dot(normed_low.T, d_hidden, preferred_element_type=jnp.float32)
    d_normed = d_second + jnp.dot(d_hidden, b_in.T, preferred_element_type=jnp.float32)
    d_first, d_ln1_gain, d_ln1_bias = ln1_pull(d_normed)
    e_first = d_first.astype(jnp.bfloat16)
    d_out_bias = jnp.sum(e_first.astype(jnp.float32), axis=0)
    d_w_out = jnp.dot(attended_seq.T, e_first, preferred_element_type=jnp.float32)
    d_attended_seq = jnp.dot(e_first, b_out.T, preferred_element_type=jnp.float32).astype(
        jnp.bfloat16
    )
    d_attended = lax.all_to_all(
        d_attended_seq, "head", split_axis=1, concat_axis=0, tiled=True
    )
    doT = d_attended.T.reshape(groups, HEAD_DIM, block_rows)
    delta = jnp.sum(doT.astype(jnp.float32) * oT, axis=1)
    stats = jnp.concatenate([lse, delta], axis=0).T
    do_win = padded(d_attended, (("blk", 0),), block_rows)
    stats_win = padded(stats, (("blk", 0),), block_rows).T
    do_own = heads_of(d_attended)
    dqT, dk0, dv0 = attn_bwdA(
        qT_own, q_own, doT, do_own, lse, delta, k_win, swap(k_win), v_win, t_lo, t_hi, qs_own, qe_own, TILE
    )
    outer = lambda a, ax: jnp.concatenate(
        [lax.slice_in_dim(a, 0, block_rows, axis=ax), lax.slice_in_dim(a, 2 * block_rows, None, axis=ax)], axis=ax
    )
    do_out = heads_of(outer(do_win, 0))
    q_out = outer(q_win, 1)
    st_out = outer(stats_win, 1)
    dk, dv = attn_bwdB(
        swap(q_out), q_out, swap(do_out), do_out, st_out[:groups], st_out[groups:],
        k_win[:, block_rows : 2 * block_rows], v_win[:, block_rows : 2 * block_rows], dk0, dv0,
        t_lo, t_hi, outer(qs, 1), outer(qe, 1), TILE
    )
    rows_of = lambda a: a.astype(jnp.bfloat16).transpose(1, 0, 2).reshape(block_rows, group_width)
    d_heads = jnp.stack([dqT.astype(jnp.bfloat16).reshape(group_width, block_rows).T, rows_of(dk), rows_of(dv)], axis=1)
    d_qkv = lax.all_to_all(d_heads, "head", split_axis=0, concat_axis=2, tiled=True).reshape(
        tok_rows, 3 * model_width
    )
    d_q_bias = jnp.sum(d_qkv[:, :model_width].astype(jnp.float32), axis=0)
    d_v_bias = jnp.sum(d_qkv[:, 2 * model_width :].astype(jnp.float32), axis=0)
    d_w_qkv = jnp.dot(inputs.T, d_qkv, preferred_element_type=jnp.float32)
    d_inputs = (d_first + jnp.dot(d_qkv, b_qkv.T, preferred_element_type=jnp.float32)).astype(
        jnp.bfloat16
    )
    summed = (
        lax.psum_scatter(d_w_qkv, ("blk", "head"), scatter_dimension=0, tiled=True),
        lax.psum_scatter(d_q_bias, ("blk", "head"), scatter_dimension=0, tiled=True),
        lax.psum_scatter(d_v_bias, ("blk", "head"), scatter_dimension=0, tiled=True),
        lax.psum_scatter(d_w_out, ("blk", "head"), scatter_dimension=0, tiled=True),
        lax.psum_scatter(d_out_bias, ("blk", "head"), scatter_dimension=0, tiled=True),
        lax.psum_scatter(d_ln1_gain, ("blk", "head"), scatter_dimension=0, tiled=True),
        lax.psum_scatter(d_ln1_bias, ("blk", "head"), scatter_dimension=0, tiled=True),
        lax.psum_scatter(d_w_in, ("blk", "head"), scatter_dimension=0, tiled=True),
        lax.psum_scatter(d_in_bias, ("blk", "head"), scatter_dimension=0, tiled=True),
        lax.psum_scatter(d_w_down, ("blk", "head"), scatter_dimension=0, tiled=True),
        lax.psum_scatter(d_down_bias, ("blk", "head"), scatter_dimension=0, tiled=True),
        lax.psum_scatter(d_ln2_gain, ("blk", "head"), scatter_dimension=0, tiled=True),
        lax.psum_scatter(d_ln2_bias, ("blk", "head"), scatter_dimension=0, tiled=True),
    )
    return (
        outputs.astype(jnp.bfloat16),
        d_inputs,
        summed[0],
        summed[1],
        summed[2],
        summed[3],
        summed[4],
        summed[5],
        summed[6],
        summed[7],
        summed[8],
        summed[9],
        summed[10],
        summed[11],
        summed[12],
    )


def solution(mesh):
    placed = (
        P(("blk", "head"), None),
        P(),
        P(("blk", "head"), None),
        P(("blk", "head"), None),
        P(("blk", "head")),
        P(("blk", "head")),
        P(("blk", "head"), None),
        P(("blk", "head")),
        P(("blk", "head")),
        P(("blk", "head")),
        P(("blk", "head"), None),
        P(("blk", "head")),
        P(("blk", "head"), None),
        P(("blk", "head")),
        P(("blk", "head")),
        P(("blk", "head")),
    )
    return jax.shard_map(
        body,
        mesh=mesh,
        in_specs=placed,
        out_specs=(
            P(("blk", "head"), None),
            P(("blk", "head"), None),
            P(("blk", "head"), None),
            P(("blk", "head")),
            P(("blk", "head")),
            P(("blk", "head"), None),
            P(("blk", "head")),
            P(("blk", "head")),
            P(("blk", "head")),
            P(("blk", "head"), None),
            P(("blk", "head")),
            P(("blk", "head"), None),
            P(("blk", "head")),
            P(("blk", "head")),
            P(("blk", "head")),
        ),
        check_vma=False,
    )
```

```python
import functools

import jax
import jax.numpy as jnp
from jax import lax
from jax.experimental import pallas as pl
from jax.experimental.pallas import tpu as pltpu
from jax.sharding import PartitionSpec as P

HEAD_DIM = 64
F32, BF16 = jnp.float32, jnp.bfloat16
NEG = -1e30
SCALE = HEAD_DIM**-0.5
MESH = pl.DeviceIdType.MESH
BOTH = ("blk", "head")
TILE = 512
BIAS_ROWS = 8

VMEM = pl.BlockSpec(memory_space=pltpu.VMEM)
SMEM = pl.BlockSpec(memory_space=pltpu.SMEM)
ANY = pl.BlockSpec(memory_space=pl.ANY)


def mm(a, b):
    return jnp.dot(a, b, preferred_element_type=F32)


def mm_tn(a, b):
    return lax.dot_general(a, b, (((0,), (0,)), ((), ())), preferred_element_type=F32)


def mm_nt(a, b):
    return lax.dot_general(a, b, (((1,), (1,)), ((), ())), preferred_element_type=F32)


def attend_body(lo_ref, hi_ref, qkv_ref, start_ref, end_ref, out_ref, lse_ref, *, groups, rows, tile):
    def one_query(i, _):
        at = pl.ds(pl.multiple_of(i * tile, tile), tile)
        win = pl.ds(pl.multiple_of(rows + i * tile, tile), tile)
        first, last = start_ref[:, win], end_ref[:, win]
        queries = [qkv_ref[h, :, win] * BF16(SCALE) for h in range(groups)]

        def one_key(j, state):
            keys = pl.ds(pl.multiple_of(j * tile, tile), tile)
            pos = lax.broadcasted_iota(jnp.int32, (tile, tile), 0) + j * tile
            same = (pos >= first) & (pos < last)
            new = []
            for h in range(groups):
                top, total, acc = state[h]
                scores = jnp.where(same, mm_tn(qkv_ref[groups + h, :, keys], queries[h]), NEG)
                peak = jnp.maximum(top, jnp.max(scores, axis=0, keepdims=True))
                weights = jnp.exp(scores - peak)
                fade = jnp.exp(top - peak)
                total = total * fade + jnp.sum(weights, axis=0, keepdims=True)
                acc = acc * fade + mm(qkv_ref[2 * groups + h, :, keys], weights.astype(BF16))
                new.append((peak, total, acc))
            return tuple(new)

        zero = tuple(
            (jnp.full((1, tile), NEG, F32), jnp.zeros((1, tile), F32), jnp.zeros((HEAD_DIM, tile), F32))
            for _ in range(groups)
        )
        state = lax.fori_loop(lo_ref[i], hi_ref[i], one_key, zero)
        for h in range(groups):
            top, total, acc = state[h]
            out_ref[h, :, at] = acc / total
            lse_ref[h : h + 1, at] = top + jnp.log(total)
        return 0

    lax.fori_loop(0, rows // tile, one_query, 0)


def attend(qkv, start, end, lo, hi, groups, rows, tile):
    return pl.pallas_call(
        functools.partial(attend_body, groups=groups, rows=rows, tile=tile),
        out_shape=(
            jax.ShapeDtypeStruct((groups, HEAD_DIM, rows), F32),
            jax.ShapeDtypeStruct((groups, rows), F32),
        ),
        in_specs=[SMEM, SMEM, VMEM, VMEM, VMEM],
        out_specs=(VMEM, VMEM),
        compiler_params=pltpu.CompilerParams(vmem_limit_bytes=48 << 20),
        cost_estimate=pl.CostEstimate(flops=30_000_000_000, bytes_accessed=12_000_000, transcendentals=15_000_000),
        name="attend",
    )(lo, hi, qkv, start, end)


def score_grads(query, key, value, d_out, lse, delta, same):
    weights = jnp.where(same, jnp.exp(mm_tn(key, query) - lse), 0.0)
    d_scores = (weights * (mm_tn(value, d_out) - delta)).astype(BF16)
    return weights.astype(BF16), d_scores


def own_grads_body(
    lo_ref, hi_ref, qkv_ref, do_ref, stat_ref, start_ref, end_ref, dq_ref, dk_ref, dv_ref, acc_ref, *, groups, rows, tile
):
    count = rows // tile
    dk_ref[...] = jnp.zeros_like(dk_ref)
    dv_ref[...] = jnp.zeros_like(dv_ref)

    def one_query(i, _):
        at = pl.ds(pl.multiple_of(i * tile, tile), tile)
        win = pl.ds(pl.multiple_of(rows + i * tile, tile), tile)
        first, last = start_ref[:, win], end_ref[:, win]
        acc_ref[...] = jnp.zeros_like(acc_ref)

        def pair(j, own):
            keys = pl.ds(pl.multiple_of(j * tile, tile), tile)
            mine = pl.ds(pl.multiple_of((j - count) * tile, tile), tile)
            pos = lax.broadcasted_iota(jnp.int32, (tile, tile), 0) + j * tile
            same = (pos >= first) & (pos < last)
            for h in range(groups):
                query = qkv_ref[h, :, win] * BF16(SCALE)
                key = qkv_ref[groups + h, :, keys]
                d_out = do_ref[h, :, at]
                weights, d_scores = score_grads(
                    query, key, qkv_ref[2 * groups + h, :, keys], d_out,
                    stat_ref[h : h + 1, at], stat_ref[groups + h : groups + h + 1, at], same,
                )
                acc_ref[h] += mm(key, d_scores)
                if own:
                    dv_ref[h, mine, :] += mm_nt(weights, d_out)
                    dk_ref[h, mine, :] += mm_nt(d_scores, query)

        def inside(j, c):
            pair(j, True)
            return c

        def outside(j, c):
            pair(j, False)
            return c

        lo, hi = lo_ref[i], hi_ref[i]
        lax.fori_loop(jnp.maximum(lo, count), jnp.minimum(hi, 2 * count), inside, 0)
        lax.fori_loop(lo, jnp.minimum(hi, count), outside, 0)
        lax.fori_loop(jnp.maximum(lo, 2 * count), hi, outside, 0)
        dq_ref[:, :, at] = (acc_ref[...] * SCALE).astype(BF16)
        return 0

    lax.fori_loop(0, count, one_query, 0)


def own_grads(qkv, d_out, stats, start, end, lo, hi, groups, rows, tile):
    return pl.pallas_call(
        functools.partial(own_grads_body, groups=groups, rows=rows, tile=tile),
        out_shape=(
            jax.ShapeDtypeStruct((groups, HEAD_DIM, rows), BF16),
            jax.ShapeDtypeStruct((groups, rows, HEAD_DIM), F32),
            jax.ShapeDtypeStruct((groups, rows, HEAD_DIM), F32),
        ),
        in_specs=[SMEM, SMEM] + [VMEM] * 5,
        out_specs=(VMEM,) * 3,
        scratch_shapes=[pltpu.VMEM((groups, HEAD_DIM, tile), F32)],
        compiler_params=pltpu.CompilerParams(vmem_limit_bytes=52 << 20),
        cost_estimate=pl.CostEstimate(flops=60_000_000_000, bytes_accessed=20_000_000, transcendentals=15_000_000),
        name="own_grads",
    )(lo, hi, qkv, d_out, stats, start, end)


def outer_grads_body(
    lo_ref, hi_ref, qkv_ref, do_lo_ref, do_hi_ref, stat_lo_ref, stat_hi_ref, start_ref, end_ref, dq_ref, dk_ref, dv_ref,
    out_ref, dk_acc, dv_acc, *, groups, rows, tile
):
    count = rows // tile
    out_ref[:groups] = dq_ref[...]

    def one_key(j, _):
        mine = pl.ds(pl.multiple_of(j * tile, tile), tile)
        keys = pl.ds(pl.multiple_of(rows + j * tile, tile), tile)
        dk_acc[...] = dk_ref[:, mine, :]
        dv_acc[...] = dv_ref[:, mine, :]

        def pair(i, base, do_ref, stat_ref):
            at = pl.ds(pl.multiple_of((i - base) * tile, tile), tile)
            win = pl.ds(pl.multiple_of(i * tile, tile), tile)
            pos = lax.broadcasted_iota(jnp.int32, (tile, tile), 0) + (j + count) * tile
            same = (pos >= start_ref[:, win]) & (pos < end_ref[:, win])
            for h in range(groups):
                query = qkv_ref[h, :, win] * BF16(SCALE)
                d_out = do_ref[h, :, at]
                weights, d_scores = score_grads(
                    query, qkv_ref[groups + h, :, keys], qkv_ref[2 * groups + h, :, keys], d_out,
                    stat_ref[h : h + 1, at], stat_ref[groups + h : groups + h + 1, at], same,
                )
                dv_acc[h] += mm_nt(weights, d_out)
                dk_acc[h] += mm_nt(d_scores, query)

        def before(i, c):
            pair(i, 0, do_lo_ref, stat_lo_ref)
            return c

        def after(i, c):
            pair(i, 2 * count, do_hi_ref, stat_hi_ref)
            return c

        lo, hi = lo_ref[j], hi_ref[j]
        lax.fori_loop(lo, jnp.minimum(hi, count), before, 0)
        lax.fori_loop(jnp.maximum(lo, 2 * count), hi, after, 0)
        for h in range(groups):
            out_ref[groups + h, :, mine] = dk_acc[h].T.astype(BF16)
            out_ref[2 * groups + h, :, mine] = dv_acc[h].T.astype(BF16)
        return 0

    lax.fori_loop(0, count, one_key, 0)


def outer_grads(qkv, do_lo, do_hi, stat_lo, stat_hi, start, end, dq, dk, dv, lo, hi, groups, rows, tile):
    return pl.pallas_call(
        functools.partial(outer_grads_body, groups=groups, rows=rows, tile=tile),
        out_shape=jax.ShapeDtypeStruct((3 * groups, HEAD_DIM, rows), BF16),
        in_specs=[SMEM, SMEM] + [VMEM] * 10,
        out_specs=VMEM,
        scratch_shapes=[pltpu.VMEM((groups, tile, HEAD_DIM), F32)] * 2,
        compiler_params=pltpu.CompilerParams(vmem_limit_bytes=52 << 20),
        cost_estimate=pl.CostEstimate(flops=20_000_000_000, bytes_accessed=20_000_000, transcendentals=5_000_000),
        name="outer_grads",
    )(lo, hi, qkv, do_lo, do_hi, stat_lo, stat_hi, start, end, dq, dk, dv)


def place():
    return lax.axis_index("blk"), lax.axis_index("head")


def greet_all(n_blk, n_head):
    blk, head = place()
    me = blk * n_head + head
    count = n_blk * n_head
    barrier = pltpu.get_barrier_semaphore()

    def say(step, c):
        to = lax.rem(me + step, count)
        pl.semaphore_signal(
            barrier, inc=1, device_id=(to // n_head, lax.rem(to, n_head)), device_id_type=MESH
        )
        return c

    lax.fori_loop(1, count, say, 0)
    pl.semaphore_wait(barrier, count - 1)


def scatter_rows(src_of, dst, send_sems, recv_sems, n_blk, n_head):
    blk, head = place()
    me = blk * n_head + head
    count = n_blk * n_head

    def copy(step):
        to = lax.rem(me + step, count)
        return pltpu.make_async_remote_copy(
            src_ref=src_of(to // n_head, lax.rem(to, n_head)),
            dst_ref=dst.at[me],
            send_sem=send_sems.at[step],
            recv_sem=recv_sems.at[step],
            device_id=(to // n_head, lax.rem(to, n_head)),
            device_id_type=MESH,
        )

    def begin(step, c):
        copy(step).start()
        return c

    def end(step, c):
        copy(step).wait()
        return c

    lax.fori_loop(1, count, begin, 0)
    return lambda: lax.fori_loop(1, count, end, 0)


def collect_body(n_blk, n_head, chunks, x_ref, w_ref, xw_ref, wr_ref, local_sem, w_send, w_recv, x_send, x_recv):
    blk, head = place()
    me = blk * n_head + head
    rows = x_ref.shape[0] // chunks
    core, row, far = head ^ 1, head ^ 2, head ^ 3
    greet_all(n_blk, n_head)

    def part(c):
        return pl.ds(c * rows, rows)

    def send(src, slot, owner, c, n, to):
        return pltpu.make_async_remote_copy(
            src_ref=src,
            dst_ref=xw_ref.at[slot, owner, part(c)],
            send_sem=x_send.at[n, c],
            recv_sem=x_recv.at[slot, owner, c],
            device_id=to,
            device_id_type=MESH,
        )

    def arrived(slot, owner, c):
        here = xw_ref.at[slot, owner, part(c)]
        pltpu.make_async_copy(here, here, x_recv.at[slot, owner, c]).wait()

    own = [x_ref.at[part(c)] for c in range(chunks)]
    started = []

    def go(copy):
        copy.start()
        started.append(copy)

    has_before, has_after = blk > 0, blk < n_blk - 1
    to_row = [send(own[c], 1, head, c, 0, (blk, row)) for c in range(chunks)]
    to_core = [send(own[c], 1, head, c, 1, (blk, core)) for c in range(chunks)]
    to_after = [send(own[c], 0, head, c, 2, (blk + 1, head)) for c in range(chunks)]
    to_before = [send(own[c], 2, head, c, 3, (blk - 1, head)) for c in range(chunks)]
    for c in range(chunks):
        go(to_row[c])

        @pl.when(has_after)
        def _():
            to_after[c].start()

        @pl.when(has_before)
        def _():
            to_before[c].start()

        go(to_core[c])
    keep_x = pltpu.make_async_copy(x_ref, xw_ref.at[1, head], local_sem.at[0])
    keep_w = pltpu.make_async_copy(w_ref.at[head], wr_ref.at[me], local_sem.at[1])
    keep_x.start()
    keep_w.start()
    wait_w = scatter_rows(lambda b, h: w_ref.at[h], wr_ref, w_send, w_recv, n_blk, n_head)

    for c in range(chunks):
        arrived(1, row, c)
        go(send(xw_ref.at[1, row, part(c)], 1, row, c, 4, (blk, core)))
    halo = []
    for c in range(chunks):
        for slot, there, n in ((0, has_before, 5), (2, has_after, 8)):
            on_row = send(xw_ref.at[slot, head, part(c)], slot, head, c, n, (blk, row))
            on_core = send(xw_ref.at[slot, head, part(c)], slot, head, c, n + 1, (blk, core))
            halo.append((there, on_row))
            halo.append((there, on_core))

            @pl.when(there)
            def _():
                arrived(slot, head, c)
                on_row.start()
                on_core.start()

    for c in range(chunks):
        for slot, there, n in ((0, has_before, 7), (2, has_after, 10)):
            relay = send(xw_ref.at[slot, row, part(c)], slot, row, c, n, (blk, core))
            halo.append((there, relay))

            @pl.when(there)
            def _():
                arrived(slot, row, c)
                relay.start()

    for c in range(chunks):
        arrived(1, core, c)
        arrived(1, far, c)
        for slot, there in ((0, has_before), (2, has_after)):

            @pl.when(there)
            def _():
                arrived(slot, core, c)
                arrived(slot, far, c)

    keep_x.wait()
    keep_w.wait()
    wait_w()
    for copy in started:
        copy.wait_send()
    for there, copies in ((has_after, to_after), (has_before, to_before)):

        @pl.when(there)
        def _():
            for copy in copies:
                copy.wait_send()

    for there, copy in halo:

        @pl.when(there)
        def _():
            copy.wait_send()


def collect(x, w, n_blk, n_head):
    chunks = 2
    return pl.pallas_call(
        functools.partial(collect_body, n_blk, n_head, chunks),
        out_shape=(
            jax.ShapeDtypeStruct((3, n_head, *x.shape), x.dtype),
            jax.ShapeDtypeStruct((n_blk * n_head, *w.shape[1:]), w.dtype),
        ),
        in_specs=[ANY, ANY],
        out_specs=(ANY, ANY),
        scratch_shapes=[
            pltpu.SemaphoreType.DMA((2,)),
            pltpu.SemaphoreType.DMA((n_blk * n_head,)),
            pltpu.SemaphoreType.DMA((n_blk * n_head,)),
            pltpu.SemaphoreType.DMA((11, chunks)),
            pltpu.SemaphoreType.DMA((3, n_head, chunks)),
        ],
        compiler_params=pltpu.CompilerParams(collective_id=0, has_side_effects=True),
        name="collect",
    )(x, w)


def finish_body(
    n_blk, n_head, part_ref, first_ref, w_ref, b_ref, out_ref, wr_ref, br_ref, near, mine, far_in, local_sem, w_send, w_recv,
    b_send, b_recv, x_send, x_recv
):
    blk, head = place()
    me = blk * n_head + head
    core, row, far = head ^ 1, head ^ 2, head ^ 3
    greet_all(n_blk, n_head)

    def send(src, dst, n, to):
        return pltpu.make_async_remote_copy(
            src_ref=src, dst_ref=dst, send_sem=x_send.at[n], recv_sem=x_recv.at[n], device_id=to, device_id_type=MESH
        )

    for_far = send(part_ref.at[far], near.at[1], 1, (blk, core))
    for_core = send(part_ref.at[core], near.at[0], 0, (blk, core))
    for_far.start()
    for_core.start()
    wait_w = scatter_rows(lambda b, h: w_ref.at[b * n_head + h], wr_ref, w_send, w_recv, n_blk, n_head)
    wait_b = scatter_rows(lambda b, h: b_ref.at[b * n_head + h], br_ref, b_send, b_recv, n_blk, n_head)
    keep_w = pltpu.make_async_copy(w_ref.at[me], wr_ref.at[me], local_sem.at[0])
    keep_b = pltpu.make_async_copy(b_ref.at[me], br_ref.at[me], local_sem.at[1])
    keep_w.start()
    keep_b.start()
    for_far.wait()
    mine[...] = (part_ref[row].astype(F32) + near[1].astype(F32)).astype(BF16)
    for_row = send(mine, far_in, 2, (blk, row))
    for_row.start()
    for_core.wait()
    for_row.wait()
    out_ref[...] = (
        first_ref[...] + part_ref[head].astype(F32) + near[0].astype(F32) + far_in[...].astype(F32)
    ).astype(BF16)
    keep_w.wait()
    keep_b.wait()
    wait_w()
    wait_b()


def finish(part, d_first, w, b, n_blk, n_head):
    count = n_blk * n_head
    rows, width = d_first.shape
    return pl.pallas_call(
        functools.partial(finish_body, n_blk, n_head),
        out_shape=(
            jax.ShapeDtypeStruct((rows, width), BF16),
            jax.ShapeDtypeStruct(w.shape, w.dtype),
            jax.ShapeDtypeStruct(b.shape, b.dtype),
        ),
        in_specs=[VMEM, VMEM, ANY, ANY],
        out_specs=(VMEM, ANY, ANY),
        scratch_shapes=[
            pltpu.VMEM((2, rows, width), BF16),
            pltpu.VMEM((rows, width), BF16),
            pltpu.VMEM((rows, width), BF16),
            pltpu.SemaphoreType.DMA((2,)),
            pltpu.SemaphoreType.DMA((count,)),
            pltpu.SemaphoreType.DMA((count,)),
            pltpu.SemaphoreType.DMA((count,)),
            pltpu.SemaphoreType.DMA((count,)),
            pltpu.SemaphoreType.DMA((3,)),
            pltpu.SemaphoreType.DMA((3,)),
        ],
        compiler_params=pltpu.CompilerParams(collective_id=1, has_side_effects=True, vmem_limit_bytes=40 << 20),
        name="finish",
    )(part, d_first, w, b)


def layer_norm(values, gain, shift_vec):
    centre = jnp.mean(values, axis=-1, keepdims=True)
    centered = values - centre
    spread = jnp.mean(centered * centered, axis=-1, keepdims=True)
    return centered * lax.rsqrt(spread + 1e-05) * gain + shift_vec


def gelu_exact(values):
    return jax.nn.gelu(values, approximate=False)


def window_of(segments, blk, rows, tile):
    padded = jnp.concatenate(
        [jnp.full((rows,), -1, jnp.int32), segments, jnp.full((rows,), 1 << 30, jnp.int32)]
    )
    seg = lax.dynamic_slice_in_dim(padded, blk * rows, 3 * rows, 0)
    own = seg[rows : 2 * rows]
    below = jnp.sum((seg[None, :] < own[::tile][:, None]).astype(jnp.int32), axis=1)
    upto = jnp.sum((seg[None, :] <= own[tile - 1 :: tile][:, None]).astype(jnp.int32), axis=1)
    pos = jnp.arange(3 * rows, dtype=jnp.int32)
    change = seg[1:] != seg[:-1]
    edge = jnp.ones((1,), bool)
    start = lax.cummax(jnp.where(jnp.concatenate([edge, change]), pos, 0))
    end = lax.cummin(jnp.where(jnp.concatenate([change, edge]), pos + 1, 3 * rows), reverse=True)
    return start[None], end[None], below // tile, (upto - 1) // tile + 1


def shift(value, steps):
    count = lax.axis_size("blk")
    first, last = max(0, -steps), min(count, count - steps)
    return lax.ppermute(value, "blk", [(source, source + steps) for source in range(first, last)])


def body(
    inputs, segments, cotangent, w_qkv, q_bias, v_bias, w_out, out_bias, ln1_gain, ln1_bias, w_in, in_bias, w_down,
    down_bias, ln2_gain, ln2_bias
):
    n_blk, n_head = lax.axis_size("blk"), lax.axis_size("head")
    count = n_blk * n_head
    blk, head = place()
    tok, width = inputs.shape
    rows = tok * n_head
    per = w_qkv.shape[0]
    ff = w_in.shape[1]
    blocks = ff // width
    cut = width // n_head
    groups = cut // HEAD_DIM
    down_per = w_down.shape[0]

    packed = jnp.concatenate(
        [w_out, w_in.reshape(per, blocks, width).transpose(1, 0, 2).reshape(per * blocks, width), w_down], axis=0
    )
    whole = lax.all_gather(packed, BOTH, axis=0, tiled=True).reshape(count, packed.shape[0], width)
    g_out = whole[:, :per].reshape(width, width)
    g_in = (
        whole[:, per : per + per * blocks].reshape(count, blocks, per, width).transpose(0, 2, 1, 3).reshape(width, ff)
    )
    g_down = whole[:, per + per * blocks :].reshape(ff, width)

    small = (q_bias, v_bias, out_bias, ln1_gain, ln1_bias, down_bias, ln2_gain, ln2_bias, in_bias)
    bias_row = jnp.concatenate(small)
    small_cols = 3 * cut
    bias_pad = jnp.zeros((BIAS_ROWS, small_cols), BF16).at[0, : bias_row.shape[0]].set(bias_row)
    columns = w_qkv.reshape(per, 3, n_head, cut).transpose(2, 0, 1, 3).reshape(n_head, per, 3 * cut)
    to_send = jnp.concatenate([columns, jnp.broadcast_to(bias_pad[None], (n_head, BIAS_ROWS, small_cols))], axis=1)
    x_win, got = collect(inputs, to_send, n_blk, n_head)
    x_win = x_win.reshape(3 * rows, width)
    w_mine = got[:, :per].reshape(width, 3 * cut)
    all_small = got[:, per, : bias_row.shape[0]].astype(F32)
    offsets = [0]
    for vec in small:
        offsets.append(offsets[-1] + vec.shape[0])
    (f_q_bias, f_v_bias, f_out_bias, f_ln1_gain, f_ln1_bias, f_down_bias, f_ln2_gain, f_ln2_bias, f_in_bias) = (
        all_small[:, a:b].reshape(-1) for a, b in zip(offsets[:-1], offsets[1:])
    )
    mine = lambda vec: lax.dynamic_slice_in_dim(vec, head * cut, cut, 0)
    qkv_bias = jnp.concatenate([mine(f_q_bias), jnp.zeros((cut,), F32), mine(f_v_bias)])

    qkv = (
        lax.dot_general(w_mine, x_win, (((0,), (1,)), ((), ())), preferred_element_type=F32) + qkv_bias[:, None]
    ).astype(BF16)
    qkv = qkv.reshape(3 * groups, HEAD_DIM, 3 * rows)
    start, end, lo, hi = window_of(segments, blk, rows, TILE)
    attended, lse = attend(qkv, start, end, lo, hi, groups, rows, TILE)
    seq_t = lax.all_to_all(
        attended.astype(BF16).reshape(cut, rows), "head", split_axis=1, concat_axis=0, tiled=True
    )

    first_sum = inputs.astype(F32) + mm_tn(seq_t, g_out) + f_out_bias
    normed, ln1_pull = jax.vjp(layer_norm, first_sum, f_ln1_gain, f_ln1_bias)
    normed_low = normed.astype(BF16)
    hidden_pre = mm(normed_low, g_in) + f_in_bias
    gelu_value, gelu_pull = jax.vjp(gelu_exact, hidden_pre)
    activated = gelu_value.astype(BF16)
    second_sum = normed + mm(activated, g_down) + f_down_bias
    outputs, ln2_pull = jax.vjp(layer_norm, second_sum, f_ln2_gain, f_ln2_bias)

    d_second, d_ln2_gain, d_ln2_bias = ln2_pull(cotangent.astype(F32))
    e_second = d_second.astype(BF16)
    d_down_bias = jnp.sum(e_second.astype(F32), axis=0)
    d_w_down = mm_tn(activated, e_second)
    d_hidden = gelu_pull(mm_nt(e_second, g_down))[0].astype(BF16)
    d_in_bias = jnp.sum(d_hidden.astype(F32), axis=0)
    d_w_in = mm_tn(normed_low, d_hidden)
    d_normed = d_second + mm_nt(d_hidden, g_in)
    d_first, d_ln1_gain, d_ln1_bias = ln1_pull(d_normed)
    e_first = d_first.astype(BF16)
    d_out_bias = jnp.sum(e_first.astype(F32), axis=0)
    d_w_out = mm(seq_t, e_first)
    d_seq_t = mm_nt(g_out, e_first).astype(BF16)
    d_out = lax.all_to_all(d_seq_t, "head", split_axis=0, concat_axis=1, tiled=True)

    grads = jnp.concatenate(
        [
            d_w_out.astype(BF16).reshape(count, per, width),
            d_w_in.astype(BF16).reshape(count, per, blocks, width).transpose(0, 2, 1, 3).reshape(count, -1, width),
            d_w_down.astype(BF16).reshape(count, down_per, width),
        ],
        axis=1,
    )
    owned = lax.psum_scatter(grads.reshape(-1, width), BOTH, scatter_dimension=0, tiled=True)

    d_out = d_out.reshape(groups, HEAD_DIM, rows)
    delta = jnp.sum(d_out.astype(F32) * attended, axis=1)
    stats = jnp.concatenate([lse, delta], axis=0)
    do_lo, do_hi = shift(d_out, 1), shift(d_out, -1)
    stat_lo, stat_hi = shift(stats, 1), shift(stats, -1)
    dq, dk, dv = own_grads(qkv, d_out, stats, start, end, lo, hi, groups, rows, TILE)
    d_qkv = outer_grads(
        qkv, do_lo, do_hi, stat_lo, stat_hi, start, end, dq, dk, dv, lo, hi, groups, rows, TILE
    ).reshape(3 * cut, rows)

    x_own = x_win[rows : 2 * rows]
    d_w_qkv = lax.dot_general(x_own, d_qkv, (((0,), (1,)), ((), ())), preferred_element_type=F32)
    d_part = lax.dot_general(d_qkv, w_mine, (((0,), (1,)), ((), ())), preferred_element_type=F32)
    d_biases = jnp.sum(d_qkv.astype(F32), axis=1)
    spread = lambda vec: lax.dynamic_update_slice_in_dim(jnp.zeros((width,), F32), vec, head * cut, 0)
    vectors = (
        spread(d_biases[:cut]), spread(d_biases[2 * cut :]), d_out_bias, d_ln1_gain, d_ln1_bias, d_down_bias, d_ln2_gain,
        d_ln2_bias, d_in_bias,
    )
    table = jnp.concatenate([vec.reshape(count, -1) for vec in vectors], axis=1)
    lanes = 128
    table_rows = -(-table.shape[1] // (8 * lanes)) * 8
    table = jnp.pad(table, ((0, 0), (0, table_rows * lanes - table.shape[1]))).reshape(count, table_rows, lanes)
    d_inputs, w_parts, b_parts = finish(
        d_part.astype(BF16).reshape(n_head, tok, width), d_first, d_w_qkv.astype(BF16).reshape(count, per, 3 * cut), table,
        n_blk, n_head,
    )
    own_w_qkv = (
        jnp.sum(w_parts.astype(F32).reshape(n_blk, n_head, per, 3, cut), axis=0).transpose(1, 2, 0, 3).reshape(per, -1)
    )
    sums = jnp.sum(b_parts, axis=0).reshape(-1)
    (o_q_bias, o_v_bias, o_out_bias, o_ln1_gain, o_ln1_bias, o_down_bias, o_ln2_gain, o_ln2_bias, o_in_bias) = (
        sums[a:b] for a, b in zip(offsets[:-1], offsets[1:])
    )
    owned = owned.astype(F32)
    own_w_in = owned[per : per + per * blocks].reshape(blocks, per, width).transpose(1, 0, 2).reshape(per, ff)
    return (
        outputs.astype(BF16), d_inputs, own_w_qkv, o_q_bias, o_v_bias, owned[:per], o_out_bias, o_ln1_gain, o_ln1_bias,
        own_w_in, o_in_bias, owned[per + per * blocks :], o_down_bias, o_ln2_gain, o_ln2_bias,
    )


def solution(mesh):
    rows, vec = P(BOTH, None), P(BOTH)
    placed = (rows, P(), rows, rows, vec, vec, rows, vec, vec, vec, rows, vec, rows, vec, vec, vec)
    return jax.shard_map(
        body,
        mesh=mesh,
        in_specs=placed,
        out_specs=(rows, rows, rows, vec, vec, rows, vec, vec, vec, rows, vec, rows, vec, vec, vec),
        check_vma=False,
    )
```

```python
import functools
import math

import jax
import jax.numpy as jnp
from jax import lax
from jax.experimental import pallas as pl
from jax.experimental.pallas import tpu as pltpu
from jax.sharding import PartitionSpec as P

HEAD_DIM = 64
F32, BF16 = jnp.float32, jnp.bfloat16
NEG = -1e30
MILD = 60.0
SCALE = HEAD_DIM**-0.5
MESH = pl.DeviceIdType.MESH
BOTH = ("blk", "head")
BIAS_ROWS = 8

VMEM = pl.BlockSpec(memory_space=pltpu.VMEM)
SMEM = pl.BlockSpec(memory_space=pltpu.SMEM)
ANY = pl.BlockSpec(memory_space=pl.ANY)


def mm(a, b):
    return jnp.dot(a, b, preferred_element_type=F32)


def mm_tn(a, b):
    return lax.dot_general(a, b, (((0,), (0,)), ((), ())), preferred_element_type=F32)


def mm_nt(a, b):
    return lax.dot_general(a, b, (((1,), (1,)), ((), ())), preferred_element_type=F32)


def column(row):
    return jnp.broadcast_to(row, (8, row.shape[1])).T[:, :1]


def same_document(seg_ref, keys, queries):
    return column(seg_ref[:, keys]) == seg_ref[:, queries]


def attend_body(lo_ref, hi_ref, qkv_ref, seg_ref, out_ref, lse_ref, *, groups, rows, tile):
    def one_query(i, mild):
        at = pl.ds(pl.multiple_of(i * tile, tile), tile)
        win = pl.ds(pl.multiple_of(rows + i * tile, tile), tile)
        queries = [qkv_ref[h, :, win] * BF16(SCALE) for h in range(groups)]

        def one_key(j, state):
            keys = pl.ds(pl.multiple_of(j * tile, tile), tile)
            same = same_document(seg_ref, keys, win)
            new = []
            ahead = mm_tn(qkv_ref[groups, :, keys], queries[0])
            for h in range(groups):
                scores = jnp.where(same, ahead, NEG)
                if h + 1 < groups:
                    ahead = mm_tn(qkv_ref[groups + h + 1, :, keys], queries[h + 1])
                value = qkv_ref[2 * groups + h, :, keys]
                top, total, acc = state[h]
                if mild:
                    weights = jnp.exp(scores)
                else:
                    peak = jnp.maximum(top, jnp.max(scores, axis=0, keepdims=True))
                    weights = jnp.exp(scores - peak)
                    fade = jnp.exp(top - peak)
                    total, acc, top = total * fade, acc * fade, peak
                total = total + jnp.sum(weights, axis=0, keepdims=True)
                new.append((top, total, acc + mm(value, weights.astype(BF16))))
            return tuple(new)

        zero = tuple(
            (jnp.full((1, tile), 0.0 if mild else NEG, F32), jnp.zeros((1, tile), F32), jnp.zeros((HEAD_DIM, tile), F32))
            for _ in range(groups)
        )
        state = lax.fori_loop(lo_ref[i], hi_ref[i], one_key, zero)
        for h in range(groups):
            top, total, acc = state[h]
            out_ref[i, h * HEAD_DIM : (h + 1) * HEAD_DIM, :] = (acc / total).astype(BF16)
            lse_ref[h : h + 1, at] = top + jnp.log(total)

    def longest(part, first, last):
        def grow(j, best):
            at = pl.ds(pl.multiple_of(j * tile, tile), tile)
            for h in range(groups):
                values = qkv_ref[part * groups + h, :, at].astype(F32)
                best = jnp.maximum(best, jnp.sum(values * values, axis=0, keepdims=True))
            return best

        return jnp.max(lax.fori_loop(first, last, grow, jnp.zeros((1, tile), F32)))

    count = rows // tile
    reach = longest(0, count, 2 * count) * longest(1, lo_ref[0], hi_ref[count - 1])
    is_mild = reach <= (MILD / SCALE) ** 2
    for mild in (True, False):

        @pl.when(is_mild == mild)
        def _():
            @pl.loop(0, rows // tile)
            def _(i):
                one_query(i, mild)


def attend(qkv, seg, lo, hi, groups, rows, tile):
    return pl.pallas_call(
        functools.partial(attend_body, groups=groups, rows=rows, tile=tile),
        out_shape=(
            jax.ShapeDtypeStruct((rows // tile, groups * HEAD_DIM, tile), BF16),
            jax.ShapeDtypeStruct((groups, rows), F32),
        ),
        in_specs=[SMEM, SMEM, VMEM, VMEM],
        out_specs=(VMEM, VMEM),
        compiler_params=pltpu.CompilerParams(vmem_limit_bytes=48 << 20),
        cost_estimate=pl.CostEstimate(flops=30_000_000_000, bytes_accessed=12_000_000, transcendentals=15_000_000),
        name="attend",
    )(lo, hi, qkv, seg)


def own_grads_body(
    lo_ref, hi_ref, qkv_ref, do_ref, lse_ref, delta_ref, seg_ref, dq_ref, dk_ref, dv_ref, acc_ref, *, groups, rows, tile
):
    count = rows // tile
    dk_ref[...] = jnp.zeros_like(dk_ref)
    dv_ref[...] = jnp.zeros_like(dv_ref)

    def one_query(i, _):
        at = pl.ds(pl.multiple_of(i * tile, tile), tile)
        win = pl.ds(pl.multiple_of(rows + i * tile, tile), tile)
        acc_ref[...] = jnp.zeros_like(acc_ref)

        def pair(j, own):
            keys = pl.ds(pl.multiple_of(j * tile, tile), tile)
            mine = pl.ds(pl.multiple_of((j - count) * tile, tile), tile)
            same = same_document(seg_ref, keys, win)

            def products(h):
                query = qkv_ref[h, :, win] * BF16(SCALE)
                return query, mm_tn(qkv_ref[groups + h, :, keys], query), mm_tn(qkv_ref[2 * groups + h, :, keys], do_ref[h * HEAD_DIM : (h + 1) * HEAD_DIM, at])

            ahead = products(0)
            for h in range(groups):
                query, scores, d_weights = ahead
                if h + 1 < groups:
                    ahead = products(h + 1)
                weights = jnp.exp(jnp.where(same, scores - lse_ref[h : h + 1, at], NEG))
                d_scores = (weights * (d_weights - delta_ref[h : h + 1, at])).astype(BF16)
                acc_ref[h] += mm(qkv_ref[groups + h, :, keys], d_scores)
                if own:
                    dv_ref[h, mine, :] += mm_nt(weights.astype(BF16), do_ref[h * HEAD_DIM : (h + 1) * HEAD_DIM, at])
                    dk_ref[h, mine, :] += mm_nt(d_scores, query)

        def inside(j, c):
            pair(j, True)
            return c

        def outside(j, c):
            pair(j, False)
            return c

        lo, hi = lo_ref[i], hi_ref[i]
        lax.fori_loop(jnp.maximum(lo, count), jnp.minimum(hi, 2 * count), inside, 0)
        lax.fori_loop(lo, jnp.minimum(hi, count), outside, 0)
        lax.fori_loop(jnp.maximum(lo, 2 * count), hi, outside, 0)
        dq_ref[:, :, at] = (acc_ref[...] * SCALE).astype(BF16)
        return 0

    lax.fori_loop(0, count, one_query, 0)


def own_grads(qkv, d_out, lse, delta, seg, lo, hi, groups, rows, tile):
    return pl.pallas_call(
        functools.partial(own_grads_body, groups=groups, rows=rows, tile=tile),
        out_shape=(
            jax.ShapeDtypeStruct((groups, HEAD_DIM, rows), BF16),
            jax.ShapeDtypeStruct((groups, rows, HEAD_DIM), F32),
            jax.ShapeDtypeStruct((groups, rows, HEAD_DIM), F32),
        ),
        in_specs=[SMEM, SMEM] + [VMEM] * 5,
        out_specs=(VMEM,) * 3,
        scratch_shapes=[pltpu.VMEM((groups, HEAD_DIM, tile), F32)],
        compiler_params=pltpu.CompilerParams(vmem_limit_bytes=52 << 20),
        cost_estimate=pl.CostEstimate(flops=60_000_000_000, bytes_accessed=20_000_000, transcendentals=15_000_000),
        name="own_grads",
    )(lo, hi, qkv, d_out, lse, delta, seg)


def outer_grads_body(
    lo_ref, hi_ref, qkv_ref, do_lo_ref, do_hi_ref, lse_lo_ref, lse_hi_ref, delta_lo_ref, delta_hi_ref, seg_ref, dq_ref, dk_ref, dv_ref, out_ref, dk_acc,
    dv_acc, *, groups, rows, tile
):
    count = rows // tile
    out_ref[:groups] = dq_ref[...]

    def one_key(j, _):
        mine = pl.ds(pl.multiple_of(j * tile, tile), tile)
        keys = pl.ds(pl.multiple_of(rows + j * tile, tile), tile)
        dk_acc[...] = dk_ref[:, mine, :]
        dv_acc[...] = dv_ref[:, mine, :]

        def pair(i, base, do_ref, lse_ref, delta_ref):
            at = pl.ds(pl.multiple_of((i - base) * tile, tile), tile)
            win = pl.ds(pl.multiple_of(i * tile, tile), tile)
            same = same_document(seg_ref, keys, win)

            def products(h):
                query = qkv_ref[h, :, win] * BF16(SCALE)
                return query, mm_tn(qkv_ref[groups + h, :, keys], query), mm_tn(qkv_ref[2 * groups + h, :, keys], do_ref[h * HEAD_DIM : (h + 1) * HEAD_DIM, at])

            ahead = products(0)
            for h in range(groups):
                query, scores, d_weights = ahead
                if h + 1 < groups:
                    ahead = products(h + 1)
                weights = jnp.exp(jnp.where(same, scores - lse_ref[h : h + 1, at], NEG))
                d_scores = (weights * (d_weights - delta_ref[h : h + 1, at])).astype(BF16)
                dv_acc[h] += mm_nt(weights.astype(BF16), do_ref[h * HEAD_DIM : (h + 1) * HEAD_DIM, at])
                dk_acc[h] += mm_nt(d_scores, query)

        def before(i, c):
            pair(i, 0, do_lo_ref, lse_lo_ref, delta_lo_ref)
            return c

        def after(i, c):
            pair(i, 2 * count, do_hi_ref, lse_hi_ref, delta_hi_ref)
            return c

        lo, hi = lo_ref[j], hi_ref[j]
        lax.fori_loop(lo, jnp.minimum(hi, count), before, 0)
        lax.fori_loop(jnp.maximum(lo, 2 * count), hi, after, 0)
        for h in range(groups):
            out_ref[groups + h, :, mine] = dk_acc[h].T.astype(BF16)
            out_ref[2 * groups + h, :, mine] = dv_acc[h].T.astype(BF16)
        return 0

    lax.fori_loop(0, count, one_key, 0)


def outer_grads(qkv, do_lo, do_hi, lse_lo, lse_hi, delta_lo, delta_hi, seg, dq, dk, dv, lo, hi, groups, rows, tile):
    return pl.pallas_call(
        functools.partial(outer_grads_body, groups=groups, rows=rows, tile=tile),
        out_shape=jax.ShapeDtypeStruct((3 * groups, HEAD_DIM, rows), BF16),
        in_specs=[SMEM, SMEM] + [VMEM] * 11,
        out_specs=VMEM,
        scratch_shapes=[pltpu.VMEM((groups, tile, HEAD_DIM), F32)] * 2,
        compiler_params=pltpu.CompilerParams(vmem_limit_bytes=52 << 20),
        cost_estimate=pl.CostEstimate(flops=20_000_000_000, bytes_accessed=20_000_000, transcendentals=5_000_000),
        name="outer_grads",
    )(lo, hi, qkv, do_lo, do_hi, lse_lo, lse_hi, delta_lo, delta_hi, seg, dq, dk, dv)


def place():
    return lax.axis_index("blk"), lax.axis_index("head")


def greet_cross(n_blk, n_head):
    blk, head = place()
    barrier = pltpu.get_barrier_semaphore()

    def say_head(step, c):
        to = lax.rem(head + step, n_head)
        pl.semaphore_signal(barrier, inc=1, device_id=(blk, to), device_id_type=MESH)
        return c

    def say_blk(step, c):
        to = lax.rem(blk + step, n_blk)
        pl.semaphore_signal(barrier, inc=1, device_id=(to, head), device_id_type=MESH)
        return c

    lax.fori_loop(1, n_head, say_head, 0)
    lax.fori_loop(1, n_blk, say_blk, 0)
    pl.semaphore_wait(barrier, n_blk + n_head - 2)


def spread(axis, count, src_of, dst, send_sems, recv_sems):
    blk, head = place()
    me = blk if axis == 0 else head

    def copy(step):
        to = lax.rem(me + step, count)
        return pltpu.make_async_remote_copy(
            src_ref=src_of(to),
            dst_ref=dst,
            send_sem=send_sems.at[step],
            recv_sem=recv_sems.at[step],
            device_id=(to, head) if axis == 0 else (blk, to),
            device_id_type=MESH,
        )

    def begin(step, c):
        copy(step).start()
        return c

    def end(step, c):
        copy(step).wait()
        return c

    lax.fori_loop(1, count, begin, 0)
    return lambda: lax.fori_loop(1, count, end, 0)


def collect_body(
    n_blk, n_head, chunks, x_ref, w_ref, xw_ref, wr_ref, local_sem, near_send, near_recv, w_send, w_recv, x_send, x_recv
):
    blk, head = place()
    rows = x_ref.shape[0] // chunks
    core, row, far = head ^ 1, head ^ 2, head ^ 3
    greet_cross(n_blk, n_head)
    keep_w = pltpu.make_async_copy(w_ref.at[head], wr_ref.at[blk, head], local_sem.at[1])
    keep_w.start()
    wait_near = spread(1, n_head, lambda h: w_ref.at[h], wr_ref.at[blk, head], near_send, near_recv)

    def part(c):
        return pl.ds(c * rows, rows)

    def send(src, slot, owner, c, n, to):
        return pltpu.make_async_remote_copy(
            src_ref=src,
            dst_ref=xw_ref.at[slot, owner, part(c)],
            send_sem=x_send.at[n, c],
            recv_sem=x_recv.at[slot, owner, c],
            device_id=to,
            device_id_type=MESH,
        )

    def arrived(slot, owner, c):
        here = xw_ref.at[slot, owner, part(c)]
        pltpu.make_async_copy(here, here, x_recv.at[slot, owner, c]).wait()

    own = [x_ref.at[part(c)] for c in range(chunks)]
    started = []

    def go(copy):
        copy.start()
        started.append(copy)

    has_before, has_after = blk > 0, blk < n_blk - 1
    to_row = [send(own[c], 1, head, c, 0, (blk, row)) for c in range(chunks)]
    to_core = [send(own[c], 1, head, c, 1, (blk, core)) for c in range(chunks)]
    to_after = [send(own[c], 0, head, c, 2, (blk + 1, head)) for c in range(chunks)]
    to_before = [send(own[c], 2, head, c, 3, (blk - 1, head)) for c in range(chunks)]
    for c in range(chunks):
        go(to_row[c])

        @pl.when(has_after)
        def _():
            to_after[c].start()

        @pl.when(has_before)
        def _():
            to_before[c].start()

        go(to_core[c])
    keep_x = pltpu.make_async_copy(x_ref, xw_ref.at[1, head], local_sem.at[0])
    keep_x.start()
    keep_w.wait()
    wait_near()
    wait_w = spread(0, n_blk, lambda b: wr_ref.at[blk], wr_ref.at[blk], w_send, w_recv)

    for c in range(chunks):
        arrived(1, row, c)
        go(send(xw_ref.at[1, row, part(c)], 1, row, c, 4, (blk, core)))
    halo = []
    for c in range(chunks):
        for slot, there, n in ((0, has_before, 5), (2, has_after, 8)):
            on_row = send(xw_ref.at[slot, head, part(c)], slot, head, c, n, (blk, row))
            on_core = send(xw_ref.at[slot, head, part(c)], slot, head, c, n + 1, (blk, core))
            halo.append((there, on_row))
            halo.append((there, on_core))

            @pl.when(there)
            def _():
                arrived(slot, head, c)
                on_row.start()
                on_core.start()

    for c in range(chunks):
        for slot, there, n in ((0, has_before, 7), (2, has_after, 10)):
            relay = send(xw_ref.at[slot, row, part(c)], slot, row, c, n, (blk, core))
            halo.append((there, relay))

            @pl.when(there)
            def _():
                arrived(slot, row, c)
                relay.start()

    for c in range(chunks):
        arrived(1, core, c)
        arrived(1, far, c)
        for slot, there in ((0, has_before), (2, has_after)):

            @pl.when(there)
            def _():
                arrived(slot, core, c)
                arrived(slot, far, c)

    keep_x.wait()
    wait_w()
    for copy in started:
        copy.wait_send()
    for there, copies in ((has_after, to_after), (has_before, to_before)):

        @pl.when(there)
        def _():
            for copy in copies:
                copy.wait_send()

    for there, copy in halo:

        @pl.when(there)
        def _():
            copy.wait_send()


def collect(x, w, n_blk, n_head):
    chunks = 2
    return pl.pallas_call(
        functools.partial(collect_body, n_blk, n_head, chunks),
        out_shape=(
            jax.ShapeDtypeStruct((3, n_head, *x.shape), x.dtype),
            jax.ShapeDtypeStruct((n_blk, *w.shape), w.dtype),
        ),
        in_specs=[ANY, ANY],
        out_specs=(ANY, ANY),
        scratch_shapes=[
            pltpu.SemaphoreType.DMA((2,)),
            pltpu.SemaphoreType.DMA((n_head,)),
            pltpu.SemaphoreType.DMA((n_head,)),
            pltpu.SemaphoreType.DMA((n_blk,)),
            pltpu.SemaphoreType.DMA((n_blk,)),
            pltpu.SemaphoreType.DMA((11, chunks)),
            pltpu.SemaphoreType.DMA((3, n_head, chunks)),
        ],
        compiler_params=pltpu.CompilerParams(collective_id=0, has_side_effects=True),
        name="collect",
    )(x, w)


def finish_body(
    n_blk, n_head, part_ref, first_ref, w_ref, t_ref, out_ref, dw_ref, dt_ref, near, mine, far_in, w_in, t_in, w_sum, t_sum, w_end,
    t_end, x_send, x_recv, w_send, w_recv, t_send, t_recv, w_send2, w_recv2, t_send2, t_recv2
):
    blk, head = place()
    core, row, far = head ^ 1, head ^ 2, head ^ 3
    greet_cross(n_blk, n_head)

    def send(src, dst, n, to):
        return pltpu.make_async_remote_copy(
            src_ref=src, dst_ref=dst, send_sem=x_send.at[n], recv_sem=x_recv.at[n], device_id=to, device_id_type=MESH
        )

    for_far = send(part_ref.at[far], near.at[1], 1, (blk, core))
    for_core = send(part_ref.at[core], near.at[0], 0, (blk, core))
    for_far.start()
    for_core.start()
    wait_w = spread(0, n_blk, lambda b: w_ref.at[b], w_in.at[blk], w_send, w_recv)
    wait_t = spread(0, n_blk, lambda b: t_ref.at[b], t_in.at[blk], t_send, t_recv)
    for_far.wait()
    mine[...] = (part_ref[row].astype(F32) + near[1].astype(F32)).astype(BF16)
    for_row = send(mine, far_in, 2, (blk, row))
    for_row.start()
    wait_w()
    wait_t()
    w_sum[...] = w_ref[blk].astype(F32)
    t_sum[...] = t_ref[blk]

    def add(step, c):
        other = lax.rem(blk + step, n_blk)
        w_sum[...] += w_in[other].astype(F32)
        t_sum[...] += t_in[other]
        return c

    lax.fori_loop(1, n_blk, add, 0)
    wait_w2 = spread(1, n_head, lambda h: w_sum.at[h], w_end.at[head], w_send2, w_recv2)
    wait_t2 = spread(1, n_head, lambda h: t_sum.at[h], t_end.at[head], t_send2, t_recv2)
    w_end[head] = w_sum[head]
    t_end[head] = t_sum[head]
    for_core.wait()
    wait_w2()
    wait_t2()
    dt_ref[...] = jnp.sum(t_end[...], axis=0)
    parts, cut = dw_ref.shape[0], dw_ref.shape[2] // n_head
    for h in range(n_head):
        for p in range(parts):
            dw_ref[p, :, h * cut : (h + 1) * cut] = w_end[h, :, p * cut : (p + 1) * cut]
    for_row.wait()
    out_ref[...] = (
        first_ref[...] + part_ref[head].astype(F32) + near[0].astype(F32) + far_in[...].astype(F32)
    ).astype(BF16)


def finish(part, d_first, w, table, n_blk, n_head):
    rows, width = d_first.shape
    _, _, per, wide = w.shape
    return pl.pallas_call(
        functools.partial(finish_body, n_blk, n_head),
        out_shape=(
            jax.ShapeDtypeStruct((rows, width), BF16),
            jax.ShapeDtypeStruct((3, per, width), F32),
            jax.ShapeDtypeStruct(table.shape[2:], F32),
        ),
        in_specs=[VMEM] * 4,
        out_specs=(VMEM,) * 3,
        scratch_shapes=[
            pltpu.VMEM((2, rows, width), BF16),
            pltpu.VMEM((rows, width), BF16),
            pltpu.VMEM((rows, width), BF16),
            pltpu.VMEM(w.shape, w.dtype),
            pltpu.VMEM(table.shape, F32),
            pltpu.VMEM(w.shape[1:], F32),
            pltpu.VMEM(table.shape[1:], F32),
            pltpu.VMEM(w.shape[1:], F32),
            pltpu.VMEM(table.shape[1:], F32),
            pltpu.SemaphoreType.DMA((3,)),
            pltpu.SemaphoreType.DMA((3,)),
        ]
        + [pltpu.SemaphoreType.DMA((n_blk,))] * 4
        + [pltpu.SemaphoreType.DMA((n_head,))] * 4,
        compiler_params=pltpu.CompilerParams(collective_id=1, has_side_effects=True, vmem_limit_bytes=40 << 20),
        name="finish",
    )(part, d_first, w, table)


def greet(n_blk, n_head):
    blk, head = place()
    barrier = pltpu.get_barrier_semaphore()
    for step in range(1, n_head):
        pl.semaphore_signal(barrier, inc=1, device_id=(blk, lax.rem(head + step, n_head)), device_id_type=MESH)

    @pl.when(blk > 0)
    def _():
        pl.semaphore_signal(barrier, inc=1, device_id=(blk - 1, head), device_id_type=MESH)

    @pl.when(blk < n_blk - 1)
    def _():
        pl.semaphore_signal(barrier, inc=1, device_id=(blk + 1, head), device_id_type=MESH)

    pl.semaphore_wait(barrier, n_head - 1 + jnp.where(blk > 0, 1, 0) + jnp.where(blk < n_blk - 1, 1, 0))


def to_neighbours(n_blk, n_head, src, lo, hi, send_sem, recv_sem):
    blk, head = place()
    cases = (
        (blk > 0, blk < n_blk - 1, hi, (blk - 1, head)),
        (blk < n_blk - 1, blk > 0, lo, (blk + 1, head)),
    )

    def copy(n):
        return pltpu.make_async_remote_copy(
            src_ref=src, dst_ref=cases[n][2], send_sem=send_sem.at[n], recv_sem=recv_sem.at[n], device_id=cases[n][3],
            device_id_type=MESH,
        )

    for n in range(2):

        @pl.when(cases[n][0])
        def _():
            copy(n).start()

    def wait():
        for n in range(2):

            @pl.when(cases[n][0])
            def _():
                copy(n).wait_send()

            @pl.when(cases[n][1])
            def _():
                copy(n).wait_recv()

    return wait


def to_tokens_body(
    n_blk, n_head, out_ref, lse_ref, seq_ref, lse_lo_ref, lse_hi_ref, keep_sem, send_sem, recv_sem, lse_send, lse_recv
):
    blk, head = place()
    greet(n_blk, n_head)

    def part(h):
        return out_ref.at[h]

    def copy(step):
        to = lax.rem(head + step, n_head)
        return pltpu.make_async_remote_copy(
            src_ref=part(to), dst_ref=seq_ref.at[head], send_sem=send_sem.at[step], recv_sem=recv_sem.at[step],
            device_id=(blk, to), device_id_type=MESH,
        )

    for step in range(n_head - 1, 0, -1):
        copy(step).start()
    keep = pltpu.make_async_copy(part(head), seq_ref.at[head], keep_sem)
    keep.start()
    wait = to_neighbours(n_blk, n_head, lse_ref, lse_lo_ref, lse_hi_ref, lse_send, lse_recv)
    for step in range(1, n_head):
        copy(step).wait()
    wait()
    keep.wait()


def to_tokens(out, lse, n_blk, n_head):
    stat = jax.ShapeDtypeStruct(lse.shape, lse.dtype)
    return pl.pallas_call(
        functools.partial(to_tokens_body, n_blk, n_head),
        out_shape=(jax.ShapeDtypeStruct(out.shape, out.dtype), stat, stat),
        in_specs=[ANY, ANY],
        out_specs=(ANY,) * 3,
        scratch_shapes=[
            pltpu.SemaphoreType.DMA,
            pltpu.SemaphoreType.DMA((n_head,)),
            pltpu.SemaphoreType.DMA((n_head,)),
            pltpu.SemaphoreType.DMA((2,)),
            pltpu.SemaphoreType.DMA((2,)),
        ],
        compiler_params=pltpu.CompilerParams(collective_id=2, has_side_effects=True),
        name="to_tokens",
    )(out, lse)


def to_heads_body(
    n_blk, n_head, dseq_ref, dpart_ref, do_ref, delta_ref, delta_lo_ref, delta_hi_ref, keep_sem, send_sem, recv_sem, d_send,
    d_recv, n_send, n_recv
):
    blk, head = place()
    tok = dseq_ref.shape[2]
    greet(n_blk, n_head)
    at = pl.ds(pl.multiple_of(head * tok, tok), tok)

    def copy(step):
        to = lax.rem(head + step, n_head)
        return pltpu.make_async_remote_copy(
            src_ref=dseq_ref.at[to], dst_ref=do_ref.at[:, at], send_sem=send_sem.at[step], recv_sem=recv_sem.at[step],
            device_id=(blk, to), device_id_type=MESH,
        )

    def small_copy(step):
        to = lax.rem(head + step, n_head)
        return pltpu.make_async_remote_copy(
            src_ref=dpart_ref.at[to], dst_ref=delta_ref.at[head], send_sem=d_send.at[step], recv_sem=d_recv.at[step],
            device_id=(blk, to), device_id_type=MESH,
        )

    keep = (
        pltpu.make_async_copy(dseq_ref.at[head], do_ref.at[:, at], keep_sem.at[0]),
        pltpu.make_async_copy(dpart_ref.at[head], delta_ref.at[head], keep_sem.at[1]),
    )
    for step in range(n_head - 1, 0, -1):
        small_copy(step).start()
        copy(step).start()
    for local in keep:
        local.start()
    for step in range(1, n_head):
        small_copy(step).wait()
    keep[1].wait()
    wait = to_neighbours(n_blk, n_head, delta_ref, delta_lo_ref, delta_hi_ref, n_send, n_recv)
    for step in range(1, n_head):
        copy(step).wait()
    keep[0].wait()
    wait()


def to_heads(d_seq, d_part, n_blk, n_head):
    _, cut, tok = d_seq.shape
    stat = jax.ShapeDtypeStruct(d_part.shape, F32)
    return pl.pallas_call(
        functools.partial(to_heads_body, n_blk, n_head),
        out_shape=(jax.ShapeDtypeStruct((cut, n_head * tok), BF16), stat, stat, stat),
        in_specs=[ANY, ANY],
        out_specs=(ANY,) * 4,
        scratch_shapes=[
            pltpu.SemaphoreType.DMA((2,)),
            pltpu.SemaphoreType.DMA((n_head,)),
            pltpu.SemaphoreType.DMA((n_head,)),
            pltpu.SemaphoreType.DMA((n_head,)),
            pltpu.SemaphoreType.DMA((n_head,)),
            pltpu.SemaphoreType.DMA((2,)),
            pltpu.SemaphoreType.DMA((2,)),
        ],
        compiler_params=pltpu.CompilerParams(collective_id=3, has_side_effects=True),
        name="to_heads",
    )(d_seq, d_part)


def project_body(x_ref, w_ref, bias_ref, out_ref, turned_ref):
    @pl.when(pl.program_id(0) == 0)
    def _():
        turned_ref[...] = w_ref[...].T

    out_ref[...] = (mm_nt(turned_ref[...], x_ref[...]) + bias_ref[...]).astype(BF16)


def project(x, w, bias, tile):
    rows, width = x.shape
    wide = w.shape[1]
    whole = lambda i: (0, 0)
    return pl.pallas_call(
        project_body,
        grid=(rows // tile,),
        out_shape=(jax.ShapeDtypeStruct((wide, rows), BF16), jax.ShapeDtypeStruct((wide, width), BF16)),
        in_specs=[
            pl.BlockSpec((tile, width), lambda i: (i, 0)),
            pl.BlockSpec((width, wide), whole),
            pl.BlockSpec((wide, 1), whole),
        ],
        out_specs=(pl.BlockSpec((wide, tile), lambda i: (0, i)), pl.BlockSpec((wide, width), whole)),
        compiler_params=pltpu.CompilerParams(vmem_limit_bytes=32 << 20),
        cost_estimate=pl.CostEstimate(flops=2 * rows * width * wide, bytes_accessed=20_000_000, transcendentals=0),
        name="project",
    )(x, w, bias)


def project_back_body(d_ref, x_ref, turned_ref, dw_ref, part_ref, sum_ref, acc_ref):
    step = pl.program_id(0)
    d = d_ref[...]
    part_ref[...] = mm_tn(d, turned_ref[...]).astype(BF16)
    product = mm(d, x_ref[...])
    total = jnp.sum(d.astype(F32), axis=1, keepdims=True)

    @pl.when(step == 0)
    def _():
        acc_ref[...] = product
        sum_ref[...] = total

    @pl.when(step > 0)
    def _():
        acc_ref[...] += product
        sum_ref[...] += total

    @pl.when(step == pl.num_programs(0) - 1)
    def _():
        dw_ref[...] = acc_ref[...].T.astype(BF16)


def project_back(d_qkv, x_win, turned, tile):
    wide, rows = d_qkv.shape
    width = x_win.shape[1]
    whole = lambda i: (0, 0)
    return pl.pallas_call(
        project_back_body,
        grid=(rows // tile,),
        out_shape=(
            jax.ShapeDtypeStruct((width, wide), BF16),
            jax.ShapeDtypeStruct((rows, width), BF16),
            jax.ShapeDtypeStruct((wide, 1), F32),
        ),
        in_specs=[
            pl.BlockSpec((wide, tile), lambda i: (0, i)),
            pl.BlockSpec((tile, width), lambda i: (rows // tile + i, 0)),
            pl.BlockSpec((wide, width), whole),
        ],
        out_specs=(
            pl.BlockSpec((width, wide), whole),
            pl.BlockSpec((tile, width), lambda i: (i, 0)),
            pl.BlockSpec((wide, 1), whole),
        ),
        scratch_shapes=[pltpu.VMEM((wide, width), F32)],
        compiler_params=pltpu.CompilerParams(vmem_limit_bytes=32 << 20),
        cost_estimate=pl.CostEstimate(flops=4 * rows * width * wide, bytes_accessed=12_000_000, transcendentals=0),
        name="project_back",
    )(d_qkv, x_win, turned)


def normalize(values):
    centre = jnp.mean(values, axis=-1, keepdims=True)
    centered = values - centre
    r = lax.rsqrt(jnp.mean(centered * centered, axis=-1, keepdims=True) + 1e-05)
    return centered * r, r


def normalize_back(d_values, unit, r, gain):
    scaled = d_values * gain
    return r * (
        scaled - jnp.mean(scaled, axis=-1, keepdims=True) - unit * jnp.mean(scaled * unit, axis=-1, keepdims=True)
    )


def over_rows(values):
    return jnp.sum(values, axis=0, keepdims=True)


def dense_body(
    x_ref, seq_ref, cot_ref, vec_ref, inb_ref, w_hbm, out_ref, first_ref, dseq_ref, delta_ref, dvec_ref, dinb_ref, grad_hbm, w, grad,
    unit_ref, r_ref, normed_ref, low_ref, acc_ref, slope_ref, act_ref, e_ref, w_sem, grad_sem, *, blocks
):
    width = x_ref.shape[1]
    out_at, down_at = blocks * width, (blocks + 1) * width

    def fetch(first, size, n):
        at = pl.ds(first, size)
        copy = pltpu.make_async_copy(w_hbm.at[:, at], w.at[:, at], w_sem.at[n])
        copy.start()
        return copy

    def cols(first, c):
        return pl.ds(pl.multiple_of(first + c * width, 128), width)

    def put(first, c, n):
        at = cols(first, c)
        return pltpu.make_async_copy(grad.at[:, at], grad_hbm.at[:, at], grad_sem.at[n])

    w_out_here = fetch(out_at, width, 0)
    w_in_here = fetch(0, out_at, 1)
    w_down_here = fetch(down_at, blocks * width, 2)
    out_bias, ln1_gain, ln1_bias, down_bias, ln2_gain, ln2_bias = (vec_ref[n : n + 1] for n in range(6))
    w_out_here.wait()
    unit, r = normalize(x_ref[...].astype(F32) + mm_tn(seq_ref[...], w[:, out_at:down_at]) + out_bias)
    unit_ref[...] = unit
    r_ref[...] = r
    normed = unit * ln1_gain + ln1_bias
    normed_ref[...] = normed
    low_ref[...] = normed.astype(BF16)
    acc_ref[...] = normed + down_bias
    w_in_here.wait()
    w_down_here.wait()

    def up_down(c, carry):
        at = cols(0, c)
        hidden = mm(low_ref[...], w[:, at]) + inb_ref[:, at]
        phi = 0.5 + 0.5 * lax.erf(hidden * (2.0**-0.5))
        act = (hidden * phi).astype(BF16)
        act_ref[:, at] = act
        slope_ref[:, at] = phi + hidden * (jnp.exp(-0.5 * hidden * hidden) * ((2.0 * math.pi) ** -0.5))
        acc_ref[...] += mm(act, w[:, cols(down_at, c)])
        return carry

    lax.fori_loop(0, blocks, up_down, 0)
    unit2, r2 = normalize(acc_ref[...])
    out_ref[...] = (unit2 * ln2_gain + ln2_bias).astype(BF16)
    dy = cot_ref[...].astype(F32)
    dvec_ref[4:5] = over_rows(dy * unit2)
    dvec_ref[5:6] = over_rows(dy)
    d_second = normalize_back(dy, unit2, r2, ln2_gain)
    e_ref[...] = d_second.astype(BF16)
    dvec_ref[3:4] = over_rows(e_ref[...].astype(F32))
    acc_ref[...] = d_second

    def back(c, carry):
        at, down = cols(0, c), cols(down_at, c)
        e = e_ref[...]
        d_hidden = (mm_nt(e, w[:, down]) * slope_ref[:, at]).astype(BF16)
        dinb_ref[:, at] = over_rows(d_hidden.astype(F32))
        acc_ref[...] += mm_nt(d_hidden, w[:, at])
        grad[:, at] = mm_tn(low_ref[...], d_hidden).astype(BF16)
        put(0, c, c).start()
        grad[:, down] = mm_tn(act_ref[:, at], e).astype(BF16)
        put(down_at, c, blocks + c).start()
        return carry

    lax.fori_loop(0, blocks, back, 0)
    d_normed = acc_ref[...]
    unit = unit_ref[...]
    dvec_ref[1:2] = over_rows(d_normed * unit)
    dvec_ref[2:3] = over_rows(d_normed)
    d_first = normalize_back(d_normed, unit, r_ref[...], ln1_gain)
    first_ref[...] = d_first
    e_first = d_first.astype(BF16)
    dvec_ref[0:1] = over_rows(e_first.astype(F32))
    grad[:, out_at:down_at] = mm(seq_ref[...], e_first).astype(BF16)
    put(out_at, 0, 2 * blocks).start()
    d_seq = mm_nt(w[:, out_at:down_at], e_first).astype(BF16)
    dseq_ref[...] = d_seq
    product = d_seq.astype(F32) * seq_ref[...].astype(F32)
    n_head, groups, _ = delta_ref.shape
    for n in range(n_head):
        for g in range(groups):
            first = (n * groups + g) * HEAD_DIM
            delta_ref[n, g : g + 1] = over_rows(product[first : first + HEAD_DIM])

    def done(c, carry):
        put(0, c, c).wait()
        put(down_at, c, blocks + c).wait()
        return carry

    lax.fori_loop(0, blocks, done, 0)
    put(out_at, 0, 2 * blocks).wait()


def dense(x, seq_t, cotangent, vectors, in_bias, weights, blocks, n_head):
    tok, width = x.shape
    ff = blocks * width
    return pl.pallas_call(
        functools.partial(dense_body, blocks=blocks),
        out_shape=(
            jax.ShapeDtypeStruct((tok, width), BF16),
            jax.ShapeDtypeStruct((tok, width), F32),
            jax.ShapeDtypeStruct((width, tok), BF16),
            jax.ShapeDtypeStruct((n_head, width // n_head // HEAD_DIM, tok), F32),
            jax.ShapeDtypeStruct((8, width), F32),
            jax.ShapeDtypeStruct((1, ff), F32),
            jax.ShapeDtypeStruct(weights.shape, BF16),
        ),
        in_specs=[VMEM] * 5 + [ANY],
        out_specs=(VMEM,) * 6 + (ANY,),
        scratch_shapes=[
            pltpu.VMEM(weights.shape, BF16),
            pltpu.VMEM(weights.shape, BF16),
            pltpu.VMEM((tok, width), F32),
            pltpu.VMEM((tok, 1), F32),
            pltpu.VMEM((tok, width), F32),
            pltpu.VMEM((tok, width), BF16),
            pltpu.VMEM((tok, width), F32),
            pltpu.VMEM((tok, ff), F32),
            pltpu.VMEM((tok, ff), BF16),
            pltpu.VMEM((tok, width), BF16),
            pltpu.SemaphoreType.DMA((3,)),
            pltpu.SemaphoreType.DMA((2 * blocks + 1,)),
        ],
        compiler_params=pltpu.CompilerParams(vmem_limit_bytes=58 << 20),
        cost_estimate=pl.CostEstimate(flops=17_000_000_000, bytes_accessed=30_000_000, transcendentals=3_000_000),
        name="dense",
    )(x, seq_t, cotangent, vectors, in_bias, weights)


def window_of(segments, blk, rows, tile):
    padded = jnp.concatenate(
        [jnp.full((rows,), -1, jnp.int32), segments, jnp.full((rows,), 1 << 30, jnp.int32)]
    )
    seg = lax.dynamic_slice_in_dim(padded, blk * rows, 3 * rows, 0)
    own = seg[rows : 2 * rows]
    below = jnp.sum((seg[None, :] < own[::tile][:, None]).astype(jnp.int32), axis=1)
    upto = jnp.sum((seg[None, :] <= own[tile - 1 :: tile][:, None]).astype(jnp.int32), axis=1)
    return seg[None], below // tile, (upto - 1) // tile + 1


def shift(value, steps):
    count = lax.axis_size("blk")
    first, last = max(0, -steps), min(count, count - steps)
    return lax.ppermute(value, "blk", [(source, source + steps) for source in range(first, last)])


def body(
    inputs, segments, cotangent, w_qkv, q_bias, v_bias, w_out, out_bias, ln1_gain, ln1_bias, w_in, in_bias, w_down,
    down_bias, ln2_gain, ln2_bias
):
    n_blk, n_head = lax.axis_size("blk"), lax.axis_size("head")
    count = n_blk * n_head
    blk, head = place()
    tok, width = inputs.shape
    rows = tok * n_head
    per = w_qkv.shape[0]
    ff = w_in.shape[1]
    blocks = ff // width
    cut = width // n_head
    groups = cut // HEAD_DIM
    down_per = w_down.shape[0]

    unit = down_per // blocks

    def reorder(values):
        return values.reshape(-1, count, blocks, unit).transpose(0, 2, 1, 3).reshape(values.shape)

    def restore(values):
        return values.reshape(-1, blocks, count, unit).transpose(0, 2, 1, 3).reshape(values.shape)

    down = w_down.reshape(blocks, unit, width).transpose(1, 0, 2).reshape(unit, ff)
    whole = lax.all_gather(jnp.concatenate([reorder(w_in), w_out, down], axis=1), BOTH, axis=0, tiled=True)

    small = (q_bias, v_bias, out_bias, ln1_gain, ln1_bias, down_bias, ln2_gain, ln2_bias, in_bias)
    bias_row = jnp.concatenate(small)
    small_cols = 3 * cut
    bias_pad = jnp.zeros((BIAS_ROWS, small_cols), BF16).at[0, : bias_row.shape[0]].set(bias_row)
    columns = w_qkv.reshape(per, 3, n_head, cut).transpose(2, 0, 1, 3).reshape(n_head, per, 3 * cut)
    to_send = jnp.concatenate([columns, jnp.broadcast_to(bias_pad[None], (n_head, BIAS_ROWS, small_cols))], axis=1)
    x_win, got = collect(inputs, to_send, n_blk, n_head)
    x_win = x_win.reshape(3 * rows, width)
    got = got.reshape(count, *got.shape[2:])
    w_mine = got[:, :per].reshape(width, 3 * cut)
    all_small = got[:, per, : bias_row.shape[0]].astype(F32)
    offsets = [0]
    for vec in small:
        offsets.append(offsets[-1] + vec.shape[0])
    (f_q_bias, f_v_bias, f_out_bias, f_ln1_gain, f_ln1_bias, f_down_bias, f_ln2_gain, f_ln2_bias, f_in_bias) = (
        all_small[:, a:b].reshape(-1) for a, b in zip(offsets[:-1], offsets[1:])
    )
    mine = lambda vec: lax.dynamic_slice_in_dim(vec, head * cut, cut, 0)
    qkv_bias = jnp.concatenate([mine(f_q_bias), jnp.zeros((cut,), F32), mine(f_v_bias)])

    qkv, turned = project(x_win, w_mine, qkv_bias[:, None], tok)
    qkv = qkv.reshape(3 * groups, HEAD_DIM, 3 * rows)
    seg, lo, hi = window_of(segments, blk, rows, tok)
    attended, lse = attend(qkv, seg, lo, hi, groups, rows, tok)
    seq_t, lse_lo, lse_hi = to_tokens(attended, lse, n_blk, n_head)
    seq_t = seq_t.reshape(width, tok)

    vectors = jnp.stack([f_out_bias, f_ln1_gain, f_ln1_bias, f_down_bias, f_ln2_gain, f_ln2_bias] + [f_out_bias] * 2)
    outputs, d_first, d_seq_t, d_part, d_vectors, d_in_bias, grads = dense(
        inputs, seq_t, cotangent, vectors, reorder(f_in_bias)[None], whole, blocks, n_head
    )
    d_out_bias, d_ln1_gain, d_ln1_bias, d_down_bias, d_ln2_gain, d_ln2_bias = (d_vectors[n] for n in range(6))
    d_in_bias = restore(d_in_bias[0])
    d_out, delta, delta_lo, delta_hi = to_heads(d_seq_t.reshape(n_head, cut, tok), d_part, n_blk, n_head)
    delta, delta_lo, delta_hi = (a.transpose(1, 0, 2).reshape(groups, rows) for a in (delta, delta_lo, delta_hi))

    owned = lax.psum_scatter(grads, BOTH, scatter_dimension=0, tiled=True).astype(F32)

    do_lo, do_hi = shift(d_out, 1), shift(d_out, -1)
    dq, dk, dv = own_grads(qkv, d_out, lse, delta, seg, lo, hi, groups, rows, tok)
    d_qkv = outer_grads(
        qkv, do_lo, do_hi, lse_lo, lse_hi, delta_lo, delta_hi, seg, dq, dk, dv, lo, hi, groups, rows, tok
    ).reshape(3 * cut, rows)

    d_w_qkv, d_part, d_biases = project_back(d_qkv, x_win, turned, tok)
    d_biases = d_biases[:, 0]
    place_own = lambda vec: lax.dynamic_update_slice_in_dim(jnp.zeros((width,), F32), vec, head * cut, 0)
    vectors = (
        place_own(d_biases[:cut]), place_own(d_biases[2 * cut :]), d_out_bias, d_ln1_gain, d_ln1_bias, d_down_bias, d_ln2_gain,
        d_ln2_bias, d_in_bias,
    )
    table = jnp.concatenate([vec.reshape(count, -1) for vec in vectors], axis=1)
    lanes = 128
    table_rows = -(-table.shape[1] // (8 * lanes)) * 8
    table = jnp.pad(table, ((0, 0), (0, table_rows * lanes - table.shape[1])))
    d_inputs, w_rows, sums = finish(
        d_part.reshape(n_head, tok, width), d_first, d_w_qkv.reshape(n_blk, n_head, per, 3 * cut),
        table.reshape(n_blk, n_head, table_rows, lanes), n_blk, n_head,
    )
    own_w_qkv = w_rows.transpose(1, 0, 2).reshape(per, 3 * width)
    sums = sums.reshape(-1)
    (o_q_bias, o_v_bias, o_out_bias, o_ln1_gain, o_ln1_bias, o_down_bias, o_ln2_gain, o_ln2_bias, o_in_bias) = (
        sums[a:b] for a, b in zip(offsets[:-1], offsets[1:])
    )
    own_w_in = restore(owned[:, :ff])
    own_w_out = owned[:, ff : ff + width]
    own_w_down = owned[:, ff + width :].reshape(unit, blocks, width).transpose(1, 0, 2).reshape(down_per, width)
    return (
        outputs, d_inputs, own_w_qkv, o_q_bias, o_v_bias, own_w_out, o_out_bias, o_ln1_gain, o_ln1_bias,
        own_w_in, o_in_bias, own_w_down, o_down_bias, o_ln2_gain, o_ln2_bias,
    )


def solution(mesh):
    rows, vec = P(BOTH, None), P(BOTH)
    placed = (rows, P(), rows, rows, vec, vec, rows, vec, vec, vec, rows, vec, rows, vec, vec, vec)
    return jax.shard_map(
        body,
        mesh=mesh,
        in_specs=placed,
        out_specs=(rows, rows, rows, vec, vec, rows, vec, vec, vec, rows, vec, rows, vec, vec, vec),
        check_vma=False,
    )
```

```python
import functools
import math

import jax
import jax.numpy as jnp
from jax import lax
from jax.experimental import pallas as pl
from jax.experimental.pallas import tpu as pltpu
from jax.sharding import PartitionSpec as P

HEAD_DIM = 64
F32, BF16 = jnp.float32, jnp.bfloat16
NEG = -1e30
MILD = 60.0
SCALE = HEAD_DIM**-0.5
MESH = pl.DeviceIdType.MESH
BOTH = ("blk", "head")
BIAS_ROWS = 8

VMEM = pl.BlockSpec(memory_space=pltpu.VMEM)
SMEM = pl.BlockSpec(memory_space=pltpu.SMEM)
ANY = pl.BlockSpec(memory_space=pl.ANY)


def mm(a, b):
    return jnp.dot(a, b, preferred_element_type=F32)


def mm_tn(a, b):
    return lax.dot_general(a, b, (((0,), (0,)), ((), ())), preferred_element_type=F32)


def mm_nt(a, b):
    return lax.dot_general(a, b, (((1,), (1,)), ((), ())), preferred_element_type=F32)


def feature_rows(n):
    return slice(n * HEAD_DIM, (n + 1) * HEAD_DIM)


def column(row):
    return jnp.broadcast_to(row, (8, row.shape[1])).T[:, :1]


def same_document(seg_ref, keys, queries):
    return column(seg_ref[:, keys]) == seg_ref[:, queries]


def project_window(first, last, per, got_ref, x_hbm, qkv_ref, qkv_hbm, turned_ref, w_ref, x_buf, x_sem, out_sem, tile):
    def fetch(j):
        slot = lax.rem(j, 2)
        at = pl.ds(pl.multiple_of(j * tile, tile), tile)
        return pltpu.make_async_copy(x_hbm.at[at], x_buf.at[slot], x_sem.at[slot])

    fetch(first).start()
    for n in range(got_ref.shape[0]):
        w_ref[n * per : (n + 1) * per] = got_ref[n, :per].astype(F32)
    turned_ref[...] = w_ref[...].T.astype(BF16)
    bias = column(jnp.sum(got_ref[:, per + 1 : per + 2].astype(F32), axis=0))

    def keep(j):
        at = pl.ds(pl.multiple_of(j * tile, tile), tile)
        return pltpu.make_async_copy(qkv_ref.at[:, at], qkv_hbm.at[:, at], out_sem.at[j])

    def one(j, c):
        @pl.when(j + 1 < last)
        def _():
            fetch(j + 1).start()

        fetch(j).wait()
        at = pl.ds(pl.multiple_of(j * tile, tile), tile)
        qkv_ref[:, at] = (mm_nt(turned_ref[...], x_buf[lax.rem(j, 2)]) + bias).astype(BF16)
        keep(j).start()
        return c

    def done(j, c):
        keep(j).wait()
        return c

    lax.fori_loop(first, last, one, 0)
    return lambda: lax.fori_loop(first, last, done, 0)


def attend_body(
    lo_ref, hi_ref, seg_ref, got_ref, x_hbm, out_ref, lse_ref, turned_ref, qkv_hbm, qkv_ref, w_ref, x_buf, x_sem, out_sem, *,
    groups, rows, tile, per
):
    count = rows // tile
    wait_kept = project_window(
        lo_ref[0], hi_ref[count - 1], per, got_ref, x_hbm, qkv_ref, qkv_hbm, turned_ref, w_ref, x_buf, x_sem, out_sem, tile
    )

    def one_query(i, mild):
        at = pl.ds(pl.multiple_of(i * tile, tile), tile)
        win = pl.ds(pl.multiple_of(rows + i * tile, tile), tile)
        queries = [qkv_ref[feature_rows(h), win] * BF16(SCALE) for h in range(groups)]

        def one_key(j, state):
            keys = pl.ds(pl.multiple_of(j * tile, tile), tile)
            same = same_document(seg_ref, keys, win)
            new = []
            ahead = mm_tn(qkv_ref[feature_rows(groups), keys], queries[0])
            for h in range(groups):
                scores = jnp.where(same, ahead, NEG)
                if h + 1 < groups:
                    ahead = mm_tn(qkv_ref[feature_rows(groups + h + 1), keys], queries[h + 1])
                value = qkv_ref[feature_rows(2 * groups + h), keys]
                top, total, acc = state[h]
                if mild:
                    weights = jnp.exp(scores)
                else:
                    peak = jnp.maximum(top, jnp.max(scores, axis=0, keepdims=True))
                    weights = jnp.exp(scores - peak)
                    fade = jnp.exp(top - peak)
                    total, acc, top = total * fade, acc * fade, peak
                total = total + jnp.sum(weights, axis=0, keepdims=True)
                new.append((top, total, acc + mm(value, weights.astype(BF16))))
            return tuple(new)

        zero = tuple(
            (jnp.full((1, tile), 0.0 if mild else NEG, F32), jnp.zeros((1, tile), F32), jnp.zeros((HEAD_DIM, tile), F32))
            for _ in range(groups)
        )
        state = lax.fori_loop(lo_ref[i], hi_ref[i], one_key, zero)
        for h in range(groups):
            top, total, acc = state[h]
            out_ref[i, h * HEAD_DIM : (h + 1) * HEAD_DIM, :] = (acc / total).astype(BF16)
            lse_ref[h : h + 1, at] = top + jnp.log(total)

    def longest(part, first, last):
        def grow(j, best):
            at = pl.ds(pl.multiple_of(j * tile, tile), tile)
            for h in range(groups):
                values = qkv_ref[feature_rows(part * groups + h), at].astype(F32)
                best = jnp.maximum(best, jnp.sum(values * values, axis=0, keepdims=True))
            return best

        return jnp.max(lax.fori_loop(first, last, grow, jnp.zeros((1, tile), F32)))

    reach = longest(0, count, 2 * count) * longest(1, lo_ref[0], hi_ref[count - 1])
    is_mild = reach <= (MILD / SCALE) ** 2
    for mild in (True, False):

        @pl.when(is_mild == mild)
        def _():
            @pl.loop(0, count)
            def _(i):
                one_query(i, mild)

    wait_kept()


def attend(x_win, got, seg, lo, hi, groups, rows, tile, per):
    width = x_win.shape[1]
    wide = got.shape[2]
    return pl.pallas_call(
        functools.partial(attend_body, groups=groups, rows=rows, tile=tile, per=per),
        out_shape=(
            jax.ShapeDtypeStruct((rows // tile, groups * HEAD_DIM, tile), BF16),
            jax.ShapeDtypeStruct((groups, rows), F32),
            jax.ShapeDtypeStruct((wide, width), BF16),
            jax.ShapeDtypeStruct((wide, 3 * rows), BF16),
        ),
        in_specs=[SMEM, SMEM, VMEM, VMEM, ANY],
        out_specs=(VMEM, VMEM, VMEM, ANY),
        scratch_shapes=[
            pltpu.VMEM((wide, 3 * rows), BF16),
            pltpu.VMEM((width, wide), F32),
            pltpu.VMEM((2, tile, width), BF16),
            pltpu.SemaphoreType.DMA((2,)),
            pltpu.SemaphoreType.DMA((3 * rows // tile,)),
        ],
        compiler_params=pltpu.CompilerParams(vmem_limit_bytes=48 << 20),
        cost_estimate=pl.CostEstimate(flops=36_000_000_000, bytes_accessed=24_000_000, transcendentals=15_000_000),
        name="attend",
    )(lo, hi, seg, got, x_win)


def own_grads_body(
    lo_ref, hi_ref, qkv_ref, do_ref, lse_ref, delta_ref, seg_ref, dq_ref, dk_ref, dv_ref, acc_ref, *, groups, rows, tile
):
    count = rows // tile
    dk_ref[...] = jnp.zeros_like(dk_ref)
    dv_ref[...] = jnp.zeros_like(dv_ref)

    def one_query(i, _):
        at = pl.ds(pl.multiple_of(i * tile, tile), tile)
        win = pl.ds(pl.multiple_of(rows + i * tile, tile), tile)
        acc_ref[...] = jnp.zeros_like(acc_ref)

        def pair(j, own):
            keys = pl.ds(pl.multiple_of(j * tile, tile), tile)
            mine = pl.ds(pl.multiple_of((j - count) * tile, tile), tile)
            same = same_document(seg_ref, keys, win)

            def products(h):
                query = qkv_ref[feature_rows(h), win] * BF16(SCALE)
                return query, mm_tn(qkv_ref[feature_rows(groups + h), keys], query), mm_tn(qkv_ref[feature_rows(2 * groups + h), keys], do_ref[feature_rows(h), at])

            ahead = products(0)
            for h in range(groups):
                query, scores, d_weights = ahead
                if h + 1 < groups:
                    ahead = products(h + 1)
                weights = jnp.exp(jnp.where(same, scores - lse_ref[h : h + 1, at], NEG))
                d_scores = (weights * (d_weights - delta_ref[h : h + 1, at])).astype(BF16)
                acc_ref[h] += mm(qkv_ref[feature_rows(groups + h), keys], d_scores)
                if own:
                    dv_ref[h, mine, :] += mm_nt(weights.astype(BF16), do_ref[feature_rows(h), at])
                    dk_ref[h, mine, :] += mm_nt(d_scores, query)

        def inside(j, c):
            pair(j, True)
            return c

        def outside(j, c):
            pair(j, False)
            return c

        lo, hi = lo_ref[i], hi_ref[i]
        lax.fori_loop(jnp.maximum(lo, count), jnp.minimum(hi, 2 * count), inside, 0)
        lax.fori_loop(lo, jnp.minimum(hi, count), outside, 0)
        lax.fori_loop(jnp.maximum(lo, 2 * count), hi, outside, 0)
        dq_ref[:, :, at] = (acc_ref[...] * SCALE).astype(BF16)
        return 0

    lax.fori_loop(0, count, one_query, 0)


def own_grads(qkv, d_out, lse, delta, seg, lo, hi, groups, rows, tile):
    return pl.pallas_call(
        functools.partial(own_grads_body, groups=groups, rows=rows, tile=tile),
        out_shape=(
            jax.ShapeDtypeStruct((groups, HEAD_DIM, rows), BF16),
            jax.ShapeDtypeStruct((groups, rows, HEAD_DIM), F32),
            jax.ShapeDtypeStruct((groups, rows, HEAD_DIM), F32),
        ),
        in_specs=[SMEM, SMEM] + [VMEM] * 5,
        out_specs=(VMEM,) * 3,
        scratch_shapes=[pltpu.VMEM((groups, HEAD_DIM, tile), F32)],
        compiler_params=pltpu.CompilerParams(vmem_limit_bytes=52 << 20),
        cost_estimate=pl.CostEstimate(flops=60_000_000_000, bytes_accessed=20_000_000, transcendentals=15_000_000),
        name="own_grads",
    )(lo, hi, qkv, d_out, lse, delta, seg)


def outer_grads_body(
    lo_ref, hi_ref, qkv_ref, do_lo_ref, do_hi_ref, lse_lo_ref, lse_hi_ref, delta_lo_ref, delta_hi_ref, seg_ref, dq_ref, dk_ref,
    dv_ref, turned_ref, x_hbm, dw_ref, part_ref, sum_ref, out_ref, dk_acc, dv_acc, dw_acc, x_buf, x_sem, *, groups, rows, tile
):
    fetch = pltpu.make_async_copy(x_hbm.at[pl.ds(rows, rows)], x_buf, x_sem)
    fetch.start()
    count = rows // tile
    for h in range(groups):
        out_ref[feature_rows(h)] = dq_ref[h]

    def one_key(j, _):
        mine = pl.ds(pl.multiple_of(j * tile, tile), tile)
        keys = pl.ds(pl.multiple_of(rows + j * tile, tile), tile)
        dk_acc[...] = dk_ref[:, mine, :]
        dv_acc[...] = dv_ref[:, mine, :]

        def pair(i, base, do_ref, lse_ref, delta_ref):
            at = pl.ds(pl.multiple_of((i - base) * tile, tile), tile)
            win = pl.ds(pl.multiple_of(i * tile, tile), tile)
            same = same_document(seg_ref, keys, win)

            def products(h):
                query = qkv_ref[feature_rows(h), win] * BF16(SCALE)
                return query, mm_tn(qkv_ref[feature_rows(groups + h), keys], query), mm_tn(qkv_ref[feature_rows(2 * groups + h), keys], do_ref[feature_rows(h), at])

            ahead = products(0)
            for h in range(groups):
                query, scores, d_weights = ahead
                if h + 1 < groups:
                    ahead = products(h + 1)
                weights = jnp.exp(jnp.where(same, scores - lse_ref[h : h + 1, at], NEG))
                d_scores = (weights * (d_weights - delta_ref[h : h + 1, at])).astype(BF16)
                dv_acc[h] += mm_nt(weights.astype(BF16), do_ref[feature_rows(h), at])
                dk_acc[h] += mm_nt(d_scores, query)

        def before(i, c):
            pair(i, 0, do_lo_ref, lse_lo_ref, delta_lo_ref)
            return c

        def after(i, c):
            pair(i, 2 * count, do_hi_ref, lse_hi_ref, delta_hi_ref)
            return c

        lo, hi = lo_ref[j], hi_ref[j]
        lax.fori_loop(lo, jnp.minimum(hi, count), before, 0)
        lax.fori_loop(jnp.maximum(lo, 2 * count), hi, after, 0)
        for h in range(groups):
            out_ref[feature_rows(groups + h), mine] = dk_acc[h].T.astype(BF16)
            out_ref[feature_rows(2 * groups + h), mine] = dv_acc[h].T.astype(BF16)
        return 0

    lax.fori_loop(0, count, one_key, 0)
    fetch.wait()
    dw_acc[...] = jnp.zeros_like(dw_acc)
    sum_ref[...] = jnp.zeros_like(sum_ref)

    def back(j, _):
        mine = pl.ds(pl.multiple_of(j * tile, tile), tile)
        d = out_ref[:, mine]
        part_ref[mine, :] = mm_tn(d, turned_ref[...]).astype(BF16)
        dw_acc[...] += mm(d, x_buf[mine, :])
        sum_ref[...] += jnp.sum(d.astype(F32), axis=1, keepdims=True)
        return 0

    lax.fori_loop(0, count, back, 0)
    dw_ref[...] = dw_acc[...].T.astype(BF16)


def outer_grads(
    qkv, do_lo, do_hi, lse_lo, lse_hi, delta_lo, delta_hi, seg, dq, dk, dv, turned, x_win, lo, hi, groups, rows, tile
):
    wide, width = turned.shape
    return pl.pallas_call(
        functools.partial(outer_grads_body, groups=groups, rows=rows, tile=tile),
        out_shape=(
            jax.ShapeDtypeStruct((width, wide), BF16),
            jax.ShapeDtypeStruct((rows, width), BF16),
            jax.ShapeDtypeStruct((wide, 1), F32),
        ),
        in_specs=[SMEM, SMEM] + [VMEM] * 12 + [ANY],
        out_specs=(VMEM,) * 3,
        scratch_shapes=[
            pltpu.VMEM((wide, rows), BF16),
            pltpu.VMEM((groups, tile, HEAD_DIM), F32),
            pltpu.VMEM((groups, tile, HEAD_DIM), F32),
            pltpu.VMEM((wide, width), F32),
            pltpu.VMEM((rows, width), BF16),
            pltpu.SemaphoreType.DMA,
        ],
        compiler_params=pltpu.CompilerParams(vmem_limit_bytes=54 << 20),
        cost_estimate=pl.CostEstimate(flops=24_000_000_000, bytes_accessed=24_000_000, transcendentals=5_000_000),
        name="outer_grads",
    )(lo, hi, qkv, do_lo, do_hi, lse_lo, lse_hi, delta_lo, delta_hi, seg, dq, dk, dv, turned, x_win)


def place():
    return lax.axis_index("blk"), lax.axis_index("head")


def greet_cross(n_blk, n_head):
    blk, head = place()
    barrier = pltpu.get_barrier_semaphore()

    def say_head(step, c):
        to = lax.rem(head + step, n_head)
        pl.semaphore_signal(barrier, inc=1, device_id=(blk, to), device_id_type=MESH)
        return c

    def say_blk(step, c):
        to = lax.rem(blk + step, n_blk)
        pl.semaphore_signal(barrier, inc=1, device_id=(to, head), device_id_type=MESH)
        return c

    lax.fori_loop(1, n_head, say_head, 0)
    lax.fori_loop(1, n_blk, say_blk, 0)
    pl.semaphore_wait(barrier, n_blk + n_head - 2)


def spread(axis, count, src_of, dst, send_sems, recv_sems):
    blk, head = place()
    me = blk if axis == 0 else head

    def copy(step):
        to = lax.rem(me + step, count)
        return pltpu.make_async_remote_copy(
            src_ref=src_of(to),
            dst_ref=dst,
            send_sem=send_sems.at[step],
            recv_sem=recv_sems.at[step],
            device_id=(to, head) if axis == 0 else (blk, to),
            device_id_type=MESH,
        )

    def begin(step, c):
        copy(step).start()
        return c

    def end(step, c):
        copy(step).wait()
        return c

    lax.fori_loop(1, count, begin, 0)
    return lambda: lax.fori_loop(1, count, end, 0)


def collect_body(
    n_blk, n_head, chunks, x_ref, w_ref, xw_ref, wr_ref, local_sem, near_send, near_recv, w_send, w_recv, x_send, x_recv
):
    blk, head = place()
    rows = x_ref.shape[0] // chunks
    core, row, far = head ^ 1, head ^ 2, head ^ 3
    greet_cross(n_blk, n_head)
    keep_w = pltpu.make_async_copy(w_ref.at[head], wr_ref.at[blk, head], local_sem.at[1])
    keep_w.start()
    wait_near = spread(1, n_head, lambda h: w_ref.at[h], wr_ref.at[blk, head], near_send, near_recv)

    def part(c):
        return pl.ds(c * rows, rows)

    def send(src, slot, owner, c, n, to):
        return pltpu.make_async_remote_copy(
            src_ref=src,
            dst_ref=xw_ref.at[slot, owner, part(c)],
            send_sem=x_send.at[n, c],
            recv_sem=x_recv.at[slot, owner, c],
            device_id=to,
            device_id_type=MESH,
        )

    def arrived(slot, owner, c):
        here = xw_ref.at[slot, owner, part(c)]
        pltpu.make_async_copy(here, here, x_recv.at[slot, owner, c]).wait()

    own = [x_ref.at[part(c)] for c in range(chunks)]
    started = []

    def go(copy):
        copy.start()
        started.append(copy)

    has_before, has_after = blk > 0, blk < n_blk - 1
    to_row = [send(own[c], 1, head, c, 0, (blk, row)) for c in range(chunks)]
    to_core = [send(own[c], 1, head, c, 1, (blk, core)) for c in range(chunks)]
    to_after = [send(own[c], 0, head, c, 2, (blk + 1, head)) for c in range(chunks)]
    to_before = [send(own[c], 2, head, c, 3, (blk - 1, head)) for c in range(chunks)]
    for c in range(chunks):
        go(to_row[c])

        @pl.when(has_after)
        def _():
            to_after[c].start()

        @pl.when(has_before)
        def _():
            to_before[c].start()

        go(to_core[c])
    keep_x = pltpu.make_async_copy(x_ref, xw_ref.at[1, head], local_sem.at[0])
    keep_x.start()
    keep_w.wait()
    wait_near()
    wait_w = spread(0, n_blk, lambda b: wr_ref.at[blk], wr_ref.at[blk], w_send, w_recv)

    for c in range(chunks):
        arrived(1, row, c)
        go(send(xw_ref.at[1, row, part(c)], 1, row, c, 4, (blk, core)))
    halo = []
    for c in range(chunks):
        for slot, there, n in ((0, has_before, 5), (2, has_after, 8)):
            on_row = send(xw_ref.at[slot, head, part(c)], slot, head, c, n, (blk, row))
            on_core = send(xw_ref.at[slot, head, part(c)], slot, head, c, n + 1, (blk, core))
            halo.append((there, on_row))
            halo.append((there, on_core))

            @pl.when(there)
            def _():
                arrived(slot, head, c)
                on_row.start()
                on_core.start()

    for c in range(chunks):
        for slot, there, n in ((0, has_before, 7), (2, has_after, 10)):
            relay = send(xw_ref.at[slot, row, part(c)], slot, row, c, n, (blk, core))
            halo.append((there, relay))

            @pl.when(there)
            def _():
                arrived(slot, row, c)
                relay.start()

    for c in range(chunks):
        arrived(1, core, c)
        arrived(1, far, c)
        for slot, there in ((0, has_before), (2, has_after)):

            @pl.when(there)
            def _():
                arrived(slot, core, c)
                arrived(slot, far, c)

    keep_x.wait()
    wait_w()
    for copy in started:
        copy.wait_send()
    for there, copies in ((has_after, to_after), (has_before, to_before)):

        @pl.when(there)
        def _():
            for copy in copies:
                copy.wait_send()

    for there, copy in halo:

        @pl.when(there)
        def _():
            copy.wait_send()


def collect(x, w, n_blk, n_head):
    chunks = 2
    return pl.pallas_call(
        functools.partial(collect_body, n_blk, n_head, chunks),
        out_shape=(
            jax.ShapeDtypeStruct((3, n_head, *x.shape), x.dtype),
            jax.ShapeDtypeStruct((n_blk, *w.shape), w.dtype),
        ),
        in_specs=[ANY, ANY],
        out_specs=(ANY, ANY),
        scratch_shapes=[
            pltpu.SemaphoreType.DMA((2,)),
            pltpu.SemaphoreType.DMA((n_head,)),
            pltpu.SemaphoreType.DMA((n_head,)),
            pltpu.SemaphoreType.DMA((n_blk,)),
            pltpu.SemaphoreType.DMA((n_blk,)),
            pltpu.SemaphoreType.DMA((11, chunks)),
            pltpu.SemaphoreType.DMA((3, n_head, chunks)),
        ],
        compiler_params=pltpu.CompilerParams(collective_id=0, has_side_effects=True),
        name="collect",
    )(x, w)


def finish_body(
    n_blk, n_head, part_ref, first_ref, w_ref, t_ref, out_ref, dw_ref, dt_ref, near, mine, far_in, w_in, t_in, w_sum, t_sum, w_end,
    t_end, x_send, x_recv, w_send, w_recv, t_send, t_recv, w_send2, w_recv2, t_send2, t_recv2
):
    blk, head = place()
    core, row, far = head ^ 1, head ^ 2, head ^ 3
    greet_cross(n_blk, n_head)

    def send(src, dst, n, to):
        return pltpu.make_async_remote_copy(
            src_ref=src, dst_ref=dst, send_sem=x_send.at[n], recv_sem=x_recv.at[n], device_id=to, device_id_type=MESH
        )

    for_far = send(part_ref.at[far], near.at[1], 1, (blk, core))
    for_core = send(part_ref.at[core], near.at[0], 0, (blk, core))
    for_far.start()
    for_core.start()
    wait_w = spread(0, n_blk, lambda b: w_ref.at[b], w_in.at[blk], w_send, w_recv)
    wait_t = spread(0, n_blk, lambda b: t_ref.at[b], t_in.at[blk], t_send, t_recv)
    for_far.wait()
    mine[...] = (part_ref[row].astype(F32) + near[1].astype(F32)).astype(BF16)
    for_row = send(mine, far_in, 2, (blk, row))
    for_row.start()
    wait_w()
    wait_t()
    w_sum[...] = w_ref[blk].astype(F32)
    t_sum[...] = t_ref[blk]

    def add(step, c):
        other = lax.rem(blk + step, n_blk)
        w_sum[...] += w_in[other].astype(F32)
        t_sum[...] += t_in[other]
        return c

    lax.fori_loop(1, n_blk, add, 0)
    wait_w2 = spread(1, n_head, lambda h: w_sum.at[h], w_end.at[head], w_send2, w_recv2)
    wait_t2 = spread(1, n_head, lambda h: t_sum.at[h], t_end.at[head], t_send2, t_recv2)
    w_end[head] = w_sum[head]
    t_end[head] = t_sum[head]
    for_core.wait()
    wait_w2()
    wait_t2()
    dt_ref[...] = jnp.sum(t_end[...], axis=0)
    parts = 3
    cut = dw_ref.shape[1] // (parts * n_head)
    for h in range(n_head):
        for p in range(parts):
            first = (p * n_head + h) * cut
            dw_ref[:, first : first + cut] = w_end[h, :, p * cut : (p + 1) * cut]
    for_row.wait()
    out_ref[...] = (
        first_ref[...] + part_ref[head].astype(F32) + near[0].astype(F32) + far_in[...].astype(F32)
    ).astype(BF16)


def finish(part, d_first, w, table, n_blk, n_head):
    rows, width = d_first.shape
    _, _, per, wide = w.shape
    return pl.pallas_call(
        functools.partial(finish_body, n_blk, n_head),
        out_shape=(
            jax.ShapeDtypeStruct((rows, width), BF16),
            jax.ShapeDtypeStruct((per, 3 * width), F32),
            jax.ShapeDtypeStruct(table.shape[2:], F32),
        ),
        in_specs=[VMEM] * 4,
        out_specs=(VMEM,) * 3,
        scratch_shapes=[
            pltpu.VMEM((2, rows, width), BF16),
            pltpu.VMEM((rows, width), BF16),
            pltpu.VMEM((rows, width), BF16),
            pltpu.VMEM(w.shape, w.dtype),
            pltpu.VMEM(table.shape, F32),
            pltpu.VMEM(w.shape[1:], F32),
            pltpu.VMEM(table.shape[1:], F32),
            pltpu.VMEM(w.shape[1:], F32),
            pltpu.VMEM(table.shape[1:], F32),
            pltpu.SemaphoreType.DMA((3,)),
            pltpu.SemaphoreType.DMA((3,)),
        ]
        + [pltpu.SemaphoreType.DMA((n_blk,))] * 4
        + [pltpu.SemaphoreType.DMA((n_head,))] * 4,
        compiler_params=pltpu.CompilerParams(collective_id=1, has_side_effects=True, vmem_limit_bytes=40 << 20),
        name="finish",
    )(part, d_first, w, table)


def greet(n_blk, n_head):
    blk, head = place()
    barrier = pltpu.get_barrier_semaphore()
    for step in range(1, n_head):
        pl.semaphore_signal(barrier, inc=1, device_id=(blk, lax.rem(head + step, n_head)), device_id_type=MESH)

    @pl.when(blk > 0)
    def _():
        pl.semaphore_signal(barrier, inc=1, device_id=(blk - 1, head), device_id_type=MESH)

    @pl.when(blk < n_blk - 1)
    def _():
        pl.semaphore_signal(barrier, inc=1, device_id=(blk + 1, head), device_id_type=MESH)

    pl.semaphore_wait(barrier, n_head - 1 + jnp.where(blk > 0, 1, 0) + jnp.where(blk < n_blk - 1, 1, 0))


def to_neighbours(n_blk, n_head, src, lo, hi, send_sem, recv_sem):
    blk, head = place()
    cases = (
        (blk > 0, blk < n_blk - 1, hi, (blk - 1, head)),
        (blk < n_blk - 1, blk > 0, lo, (blk + 1, head)),
    )

    def copy(n):
        return pltpu.make_async_remote_copy(
            src_ref=src, dst_ref=cases[n][2], send_sem=send_sem.at[n], recv_sem=recv_sem.at[n], device_id=cases[n][3],
            device_id_type=MESH,
        )

    for n in range(2):

        @pl.when(cases[n][0])
        def _():
            copy(n).start()

    def wait():
        for n in range(2):

            @pl.when(cases[n][0])
            def _():
                copy(n).wait_send()

            @pl.when(cases[n][1])
            def _():
                copy(n).wait_recv()

    return wait


def to_tokens_body(
    n_blk, n_head, out_ref, lse_ref, seq_ref, lse_lo_ref, lse_hi_ref, keep_sem, send_sem, recv_sem, lse_send, lse_recv
):
    blk, head = place()
    greet(n_blk, n_head)

    def part(h):
        return out_ref.at[h]

    def copy(step):
        to = lax.rem(head + step, n_head)
        return pltpu.make_async_remote_copy(
            src_ref=part(to), dst_ref=seq_ref.at[head], send_sem=send_sem.at[step], recv_sem=recv_sem.at[step],
            device_id=(blk, to), device_id_type=MESH,
        )

    for step in range(n_head - 1, 0, -1):
        copy(step).start()
    keep = pltpu.make_async_copy(part(head), seq_ref.at[head], keep_sem)
    keep.start()
    wait = to_neighbours(n_blk, n_head, lse_ref, lse_lo_ref, lse_hi_ref, lse_send, lse_recv)
    for step in range(1, n_head):
        copy(step).wait()
    wait()
    keep.wait()


def to_tokens(out, lse, n_blk, n_head):
    stat = jax.ShapeDtypeStruct(lse.shape, lse.dtype)
    return pl.pallas_call(
        functools.partial(to_tokens_body, n_blk, n_head),
        out_shape=(jax.ShapeDtypeStruct(out.shape, out.dtype), stat, stat),
        in_specs=[ANY, ANY],
        out_specs=(ANY,) * 3,
        scratch_shapes=[
            pltpu.SemaphoreType.DMA,
            pltpu.SemaphoreType.DMA((n_head,)),
            pltpu.SemaphoreType.DMA((n_head,)),
            pltpu.SemaphoreType.DMA((2,)),
            pltpu.SemaphoreType.DMA((2,)),
        ],
        compiler_params=pltpu.CompilerParams(collective_id=2, has_side_effects=True),
        name="to_tokens",
    )(out, lse)


def to_heads_body(
    n_blk, n_head, dseq_ref, dpart_ref, do_ref, delta_ref, delta_lo_ref, delta_hi_ref, keep_sem, send_sem, recv_sem, d_send,
    d_recv, n_send, n_recv
):
    blk, head = place()
    tok = dseq_ref.shape[2]
    greet(n_blk, n_head)
    at = pl.ds(pl.multiple_of(head * tok, tok), tok)

    def copy(step):
        to = lax.rem(head + step, n_head)
        return pltpu.make_async_remote_copy(
            src_ref=dseq_ref.at[to], dst_ref=do_ref.at[:, at], send_sem=send_sem.at[step], recv_sem=recv_sem.at[step],
            device_id=(blk, to), device_id_type=MESH,
        )

    def small_copy(step):
        to = lax.rem(head + step, n_head)
        return pltpu.make_async_remote_copy(
            src_ref=dpart_ref.at[to], dst_ref=delta_ref.at[head], send_sem=d_send.at[step], recv_sem=d_recv.at[step],
            device_id=(blk, to), device_id_type=MESH,
        )

    keep = (
        pltpu.make_async_copy(dseq_ref.at[head], do_ref.at[:, at], keep_sem.at[0]),
        pltpu.make_async_copy(dpart_ref.at[head], delta_ref.at[head], keep_sem.at[1]),
    )
    for step in range(n_head - 1, 0, -1):
        small_copy(step).start()
        copy(step).start()
    for local in keep:
        local.start()
    for step in range(1, n_head):
        small_copy(step).wait()
    keep[1].wait()
    wait = to_neighbours(n_blk, n_head, delta_ref, delta_lo_ref, delta_hi_ref, n_send, n_recv)
    for step in range(1, n_head):
        copy(step).wait()
    keep[0].wait()
    wait()


def to_heads(d_seq, d_part, n_blk, n_head):
    _, cut, tok = d_seq.shape
    stat = jax.ShapeDtypeStruct(d_part.shape, F32)
    return pl.pallas_call(
        functools.partial(to_heads_body, n_blk, n_head),
        out_shape=(jax.ShapeDtypeStruct((cut, n_head * tok), BF16), stat, stat, stat),
        in_specs=[ANY, ANY],
        out_specs=(ANY,) * 4,
        scratch_shapes=[
            pltpu.SemaphoreType.DMA((2,)),
            pltpu.SemaphoreType.DMA((n_head,)),
            pltpu.SemaphoreType.DMA((n_head,)),
            pltpu.SemaphoreType.DMA((n_head,)),
            pltpu.SemaphoreType.DMA((n_head,)),
            pltpu.SemaphoreType.DMA((2,)),
            pltpu.SemaphoreType.DMA((2,)),
        ],
        compiler_params=pltpu.CompilerParams(collective_id=3, has_side_effects=True),
        name="to_heads",
    )(d_seq, d_part)


def regroup(values, outer, inner, unit):
    if unit % 8:
        return values.reshape(-1, outer, inner, unit).transpose(0, 2, 1, 3).reshape(values.shape)
    at = lambda o, i: slice((o * inner + i) * unit, (o * inner + i + 1) * unit)
    return jnp.concatenate([values[:, at(o, i)] for i in range(inner) for o in range(outer)], axis=1)


def pack_body(*refs, count, blocks, n_head):
    (in_ref, mid_ref, down_ref, qkv_ref), vectors, (packed_ref, send_ref) = refs[:4], refs[4:-2], refs[-2:]
    unit, width = mid_ref.shape
    ff = blocks * width
    packed_ref[:, :ff] = regroup(in_ref[...].astype(F32), count, blocks, unit).astype(BF16)
    packed_ref[:, ff : ff + width] = mid_ref[...]
    for n in range(blocks):
        packed_ref[:, ff + width * (n + 1) : ff + width * (n + 2)] = down_ref[n * unit : (n + 1) * unit]

    cut = width // n_head
    vectors = [ref[...].astype(F32) for ref in vectors]
    joined = jnp.concatenate(vectors, axis=1)
    wide = 3 * cut
    pieces = jnp.concatenate([joined, jnp.zeros((1, wide - joined.shape[1]), F32)], axis=1)
    blk, head = place()
    me = blk * n_head + head
    spots = cut // unit

    def in_place(vec):
        return jnp.concatenate([jnp.where(lax.rem(me, spots) == n, vec, 0.0) for n in range(spots)], axis=1)

    placed = jnp.concatenate([in_place(vectors[0]), jnp.zeros((1, cut), F32), in_place(vectors[1])], axis=1)
    weights = qkv_ref[...].astype(F32)
    rest = jnp.zeros((BIAS_ROWS - 2, wide), F32)
    for h in range(n_head):
        columns = jnp.concatenate([weights[:, p * width + h * cut : p * width + (h + 1) * cut] for p in range(3)], axis=1)
        mine = jnp.where(me // spots == h, placed, 0.0)
        send_ref[h] = jnp.concatenate([columns, pieces, mine, rest], axis=0).astype(BF16)


def pack(w_in, w_out, w_down, w_qkv, vectors, count, n_head):
    unit, width = w_out.shape
    blocks = w_down.shape[0] // unit
    cut = width // n_head
    if unit % 8:
        down = w_down.reshape(blocks, unit, width).transpose(1, 0, 2).reshape(unit, -1)
        joined = jnp.concatenate(vectors)
        blk, head = place()
        me = blk * n_head + head
        spots = cut // unit
        zeros = jnp.zeros((cut,), BF16)
        at = lax.rem(me, spots) * unit
        placed = jnp.concatenate(
            [
                lax.dynamic_update_slice_in_dim(zeros, vectors[0], at, 0),
                zeros,
                lax.dynamic_update_slice_in_dim(zeros, vectors[1], at, 0),
            ]
        )
        owner = (jnp.arange(n_head) == me // spots)[:, None]
        rows = jnp.stack(
            [
                jnp.broadcast_to(jnp.pad(joined, (0, 3 * cut - joined.shape[0]))[None], (n_head, 3 * cut)),
                jnp.where(owner, placed[None], jnp.zeros((), BF16)),
            ]
            + [jnp.zeros((n_head, 3 * cut), BF16)] * (BIAS_ROWS - 2),
            axis=1,
        )
        columns = w_qkv.reshape(unit, 3, n_head, cut).transpose(2, 0, 1, 3).reshape(n_head, unit, 3 * cut)
        packed = jnp.concatenate([regroup(w_in, count, blocks, unit), w_out, down], axis=1)
        return packed, jnp.concatenate([columns, rows], axis=1)
    return pl.pallas_call(
        functools.partial(pack_body, count=count, blocks=blocks, n_head=n_head),
        out_shape=(
            jax.ShapeDtypeStruct((unit, 2 * w_in.shape[1] + width), BF16),
            jax.ShapeDtypeStruct((n_head, unit + BIAS_ROWS, 3 * cut), BF16),
        ),
        in_specs=[VMEM] * (4 + len(vectors)),
        out_specs=(VMEM, VMEM),
        name="pack",
    )(w_in, w_out, w_down, w_qkv, *(vec[None] for vec in vectors))


def unpack_body(packed_ref, in_ref, mid_ref, down_ref, *, count, blocks):
    unit, width = mid_ref.shape
    ff = blocks * width
    in_ref[...] = regroup(packed_ref[:, :ff].astype(F32), blocks, count, unit)
    mid_ref[...] = packed_ref[:, ff : ff + width].astype(F32)
    for n in range(blocks):
        down_ref[n * unit : (n + 1) * unit] = packed_ref[:, ff + width * (n + 1) : ff + width * (n + 2)].astype(F32)


def unpack(packed, width, count):
    unit = packed.shape[0]
    blocks = (packed.shape[1] // width - 1) // 2
    ff = blocks * width
    if unit % 8:
        packed = packed.astype(F32)
        down = packed[:, ff + width :].reshape(unit, blocks, width).transpose(1, 0, 2).reshape(-1, width)
        return regroup(packed[:, :ff], blocks, count, unit), packed[:, ff : ff + width], down
    return pl.pallas_call(
        functools.partial(unpack_body, count=count, blocks=blocks),
        out_shape=(
            jax.ShapeDtypeStruct((unit, ff), F32),
            jax.ShapeDtypeStruct((unit, width), F32),
            jax.ShapeDtypeStruct((unit * blocks, width), F32),
        ),
        in_specs=[VMEM],
        out_specs=(VMEM,) * 3,
        name="unpack",
    )(packed)


def normalize(values):
    centre = jnp.mean(values, axis=-1, keepdims=True)
    centered = values - centre
    r = lax.rsqrt(jnp.mean(centered * centered, axis=-1, keepdims=True) + 1e-05)
    return centered * r, r


def normalize_back(d_values, unit, r, gain):
    scaled = d_values * gain
    return r * (
        scaled - jnp.mean(scaled, axis=-1, keepdims=True) - unit * jnp.mean(scaled * unit, axis=-1, keepdims=True)
    )


def over_rows(values):
    return jnp.sum(values, axis=0, keepdims=True)


def dense_body(
    x_ref, seq_ref, cot_ref, vec_ref, inb_ref, w_hbm, out_ref, first_ref, dseq_ref, delta_ref, dvec_ref, dinb_ref, grad_hbm, w, grad,
    unit_ref, r_ref, normed_ref, low_ref, acc_ref, slope_ref, act_ref, e_ref, w_sem, grad_sem, *, blocks
):
    width = x_ref.shape[1]
    out_at, down_at = blocks * width, (blocks + 1) * width

    def fetch(first, size, n):
        at = pl.ds(first, size)
        copy = pltpu.make_async_copy(w_hbm.at[:, at], w.at[:, at], w_sem.at[n])
        copy.start()
        return copy

    def cols(first, c):
        return pl.ds(pl.multiple_of(first + c * width, 128), width)

    def put(first, c, n):
        at = cols(first, c)
        return pltpu.make_async_copy(grad.at[:, at], grad_hbm.at[:, at], grad_sem.at[n])

    w_out_here = fetch(out_at, width, 0)
    w_in_here = fetch(0, out_at, 1)
    w_down_here = fetch(down_at, blocks * width, 2)
    out_bias, ln1_gain, ln1_bias, down_bias, ln2_gain, ln2_bias = (vec_ref[n : n + 1] for n in range(6))
    w_out_here.wait()
    unit, r = normalize(x_ref[...].astype(F32) + mm_tn(seq_ref[...], w[:, out_at:down_at]) + out_bias)
    unit_ref[...] = unit
    r_ref[...] = r
    normed = unit * ln1_gain + ln1_bias
    normed_ref[...] = normed
    low_ref[...] = normed.astype(BF16)
    acc_ref[...] = normed + down_bias
    w_in_here.wait()
    w_down_here.wait()

    def up_down(c, carry):
        at = cols(0, c)
        hidden = mm(low_ref[...], w[:, at]) + inb_ref[:, at]
        phi = 0.5 + 0.5 * lax.erf(hidden * (2.0**-0.5))
        act = (hidden * phi).astype(BF16)
        act_ref[:, at] = act
        slope_ref[:, at] = phi + hidden * (jnp.exp(-0.5 * hidden * hidden) * ((2.0 * math.pi) ** -0.5))
        acc_ref[...] += mm(act, w[:, cols(down_at, c)])
        return carry

    lax.fori_loop(0, blocks, up_down, 0)
    unit2, r2 = normalize(acc_ref[...])
    out_ref[...] = (unit2 * ln2_gain + ln2_bias).astype(BF16)
    dy = cot_ref[...].astype(F32)
    dvec_ref[4:5] = over_rows(dy * unit2)
    dvec_ref[5:6] = over_rows(dy)
    d_second = normalize_back(dy, unit2, r2, ln2_gain)
    e_ref[...] = d_second.astype(BF16)
    dvec_ref[3:4] = over_rows(e_ref[...].astype(F32))
    acc_ref[...] = d_second

    def back(c, carry):
        at, down = cols(0, c), cols(down_at, c)
        e = e_ref[...]
        d_hidden = (mm_nt(e, w[:, down]) * slope_ref[:, at]).astype(BF16)
        dinb_ref[:, at] = over_rows(d_hidden.astype(F32))
        acc_ref[...] += mm_nt(d_hidden, w[:, at])
        grad[:, at] = mm_tn(low_ref[...], d_hidden).astype(BF16)
        put(0, c, c).start()
        grad[:, down] = mm_tn(act_ref[:, at], e).astype(BF16)
        put(down_at, c, blocks + c).start()
        return carry

    lax.fori_loop(0, blocks, back, 0)
    d_normed = acc_ref[...]
    unit = unit_ref[...]
    dvec_ref[1:2] = over_rows(d_normed * unit)
    dvec_ref[2:3] = over_rows(d_normed)
    d_first = normalize_back(d_normed, unit, r_ref[...], ln1_gain)
    first_ref[...] = d_first
    e_first = d_first.astype(BF16)
    dvec_ref[0:1] = over_rows(e_first.astype(F32))
    grad[:, out_at:down_at] = mm(seq_ref[...], e_first).astype(BF16)
    put(out_at, 0, 2 * blocks).start()
    d_seq = mm_nt(w[:, out_at:down_at], e_first).astype(BF16)
    dseq_ref[...] = d_seq
    product = d_seq.astype(F32) * seq_ref[...].astype(F32)
    n_head, groups, _ = delta_ref.shape
    for n in range(n_head):
        for g in range(groups):
            first = (n * groups + g) * HEAD_DIM
            delta_ref[n, g : g + 1] = over_rows(product[first : first + HEAD_DIM])

    def done(c, carry):
        put(0, c, c).wait()
        put(down_at, c, blocks + c).wait()
        return carry

    lax.fori_loop(0, blocks, done, 0)
    put(out_at, 0, 2 * blocks).wait()


def dense(x, seq_t, cotangent, vectors, in_bias, weights, blocks, n_head):
    tok, width = x.shape
    ff = blocks * width
    return pl.pallas_call(
        functools.partial(dense_body, blocks=blocks),
        out_shape=(
            jax.ShapeDtypeStruct((tok, width), BF16),
            jax.ShapeDtypeStruct((tok, width), F32),
            jax.ShapeDtypeStruct((width, tok), BF16),
            jax.ShapeDtypeStruct((n_head, width // n_head // HEAD_DIM, tok), F32),
            jax.ShapeDtypeStruct((8, width), F32),
            jax.ShapeDtypeStruct((1, ff), F32),
            jax.ShapeDtypeStruct(weights.shape, BF16),
        ),
        in_specs=[VMEM] * 5 + [ANY],
        out_specs=(VMEM,) * 6 + (ANY,),
        scratch_shapes=[
            pltpu.VMEM(weights.shape, BF16),
            pltpu.VMEM(weights.shape, BF16),
            pltpu.VMEM((tok, width), F32),
            pltpu.VMEM((tok, 1), F32),
            pltpu.VMEM((tok, width), F32),
            pltpu.VMEM((tok, width), BF16),
            pltpu.VMEM((tok, width), F32),
            pltpu.VMEM((tok, ff), F32),
            pltpu.VMEM((tok, ff), BF16),
            pltpu.VMEM((tok, width), BF16),
            pltpu.SemaphoreType.DMA((3,)),
            pltpu.SemaphoreType.DMA((2 * blocks + 1,)),
        ],
        compiler_params=pltpu.CompilerParams(vmem_limit_bytes=58 << 20),
        cost_estimate=pl.CostEstimate(flops=17_000_000_000, bytes_accessed=30_000_000, transcendentals=3_000_000),
        name="dense",
    )(x, seq_t, cotangent, vectors, in_bias, weights)


def window_of(segments, blk, rows, tile):
    padded = jnp.concatenate(
        [jnp.full((rows,), -1, jnp.int32), segments, jnp.full((rows,), 1 << 30, jnp.int32)]
    )
    seg = lax.dynamic_slice_in_dim(padded, blk * rows, 3 * rows, 0)
    own = seg[rows : 2 * rows]
    below = jnp.sum((seg[None, :] < own[::tile][:, None]).astype(jnp.int32), axis=1)
    upto = jnp.sum((seg[None, :] <= own[tile - 1 :: tile][:, None]).astype(jnp.int32), axis=1)
    return seg[None], below // tile, (upto - 1) // tile + 1


def shift(value, steps):
    count = lax.axis_size("blk")
    first, last = max(0, -steps), min(count, count - steps)
    return lax.ppermute(value, "blk", [(source, source + steps) for source in range(first, last)])


def body(
    inputs, segments, cotangent, w_qkv, q_bias, v_bias, w_out, out_bias, ln1_gain, ln1_bias, w_in, in_bias, w_down,
    down_bias, ln2_gain, ln2_bias
):
    n_blk, n_head = lax.axis_size("blk"), lax.axis_size("head")
    count = n_blk * n_head
    blk, head = place()
    tok, width = inputs.shape
    rows = tok * n_head
    per = w_qkv.shape[0]
    ff = w_in.shape[1]
    blocks = ff // width
    cut = width // n_head
    groups = cut // HEAD_DIM

    small = (q_bias, v_bias, out_bias, ln1_gain, ln1_bias, down_bias, ln2_gain, ln2_bias, in_bias)
    packed, to_send = pack(w_in, w_out, w_down, w_qkv, small, count, n_head)
    whole = lax.all_gather(packed, BOTH, axis=0, tiled=True)

    x_win, got = collect(inputs, to_send, n_blk, n_head)
    x_win = x_win.reshape(3 * rows, width)
    got = got.reshape(count, *got.shape[2:])
    all_small = got[:, per, : sum(vec.shape[0] for vec in small)].astype(F32)
    offsets = [0]
    for vec in small:
        offsets.append(offsets[-1] + vec.shape[0])
    (_, _, f_out_bias, f_ln1_gain, f_ln1_bias, f_down_bias, f_ln2_gain, f_ln2_bias, f_in_bias) = (
        all_small[:, a:b].reshape(-1) for a, b in zip(offsets[:-1], offsets[1:])
    )
    seg, lo, hi = window_of(segments, blk, rows, tok)
    attended, lse, turned, qkv = attend(x_win, got, seg, lo, hi, groups, rows, tok, per)
    seq_t, lse_lo, lse_hi = to_tokens(attended, lse, n_blk, n_head)
    seq_t = seq_t.reshape(width, tok)

    vectors = jnp.stack([f_out_bias, f_ln1_gain, f_ln1_bias, f_down_bias, f_ln2_gain, f_ln2_bias] + [f_out_bias] * 2)
    outputs, d_first, d_seq_t, d_part, d_vectors, d_in_bias, grads = dense(
        inputs, seq_t, cotangent, vectors, regroup(f_in_bias[None], count, blocks, per), whole, blocks, n_head
    )
    d_out_bias, d_ln1_gain, d_ln1_bias, d_down_bias, d_ln2_gain, d_ln2_bias = (d_vectors[n] for n in range(6))
    d_in_bias = regroup(d_in_bias, blocks, count, per)[0]
    d_out, delta, delta_lo, delta_hi = to_heads(d_seq_t.reshape(n_head, cut, tok), d_part, n_blk, n_head)
    delta, delta_lo, delta_hi = (a.transpose(1, 0, 2).reshape(groups, rows) for a in (delta, delta_lo, delta_hi))

    owned = lax.psum_scatter(grads, BOTH, scatter_dimension=0, tiled=True)

    do_lo, do_hi = shift(d_out, 1), shift(d_out, -1)
    dq, dk, dv = own_grads(qkv, d_out, lse, delta, seg, lo, hi, groups, rows, tok)
    d_w_qkv, d_part, d_biases = outer_grads(
        qkv, do_lo, do_hi, lse_lo, lse_hi, delta_lo, delta_hi, seg, dq, dk, dv, turned, x_win, lo, hi, groups, rows, tok
    )
    d_biases = d_biases[:, 0]
    place_own = lambda vec: lax.dynamic_update_slice_in_dim(jnp.zeros((width,), F32), vec, head * cut, 0)
    vectors = (
        place_own(d_biases[:cut]), place_own(d_biases[2 * cut :]), d_out_bias, d_ln1_gain, d_ln1_bias, d_down_bias, d_ln2_gain,
        d_ln2_bias, d_in_bias,
    )
    table = jnp.concatenate([vec.reshape(count, -1) for vec in vectors], axis=1)
    lanes = 128
    table_rows = -(-table.shape[1] // (8 * lanes)) * 8
    table = jnp.pad(table, ((0, 0), (0, table_rows * lanes - table.shape[1])))
    d_inputs, own_w_qkv, sums = finish(
        d_part.reshape(n_head, tok, width), d_first, d_w_qkv.reshape(n_blk, n_head, per, 3 * cut),
        table.reshape(n_blk, n_head, table_rows, lanes), n_blk, n_head,
    )
    sums = sums.reshape(-1)
    (o_q_bias, o_v_bias, o_out_bias, o_ln1_gain, o_ln1_bias, o_down_bias, o_ln2_gain, o_ln2_bias, o_in_bias) = (
        sums[a:b] for a, b in zip(offsets[:-1], offsets[1:])
    )
    own_w_in, own_w_out, own_w_down = unpack(owned, width, count)
    return (
        outputs, d_inputs, own_w_qkv, o_q_bias, o_v_bias, own_w_out, o_out_bias, o_ln1_gain, o_ln1_bias,
        own_w_in, o_in_bias, own_w_down, o_down_bias, o_ln2_gain, o_ln2_bias,
    )


def solution(mesh):
    rows, vec = P(BOTH, None), P(BOTH)
    placed = (rows, P(), rows, rows, vec, vec, rows, vec, vec, vec, rows, vec, rows, vec, vec, vec)
    return jax.shard_map(
        body,
        mesh=mesh,
        in_specs=placed,
        out_specs=(rows, rows, rows, vec, vec, rows, vec, vec, vec, rows, vec, rows, vec, vec, vec),
        check_vma=False,
    )
```

```python
import functools
import math

import jax
import jax.numpy as jnp
from jax import lax
from jax.experimental import pallas as pl
from jax.experimental.pallas import tpu as pltpu
from jax.sharding import PartitionSpec as P

HEAD_DIM = 64
F32, BF16 = jnp.float32, jnp.bfloat16
NEG = -1e30
MILD = 60.0
SCALE = HEAD_DIM**-0.5
MESH = pl.DeviceIdType.MESH
BOTH = ("blk", "head")
BIAS_ROWS = 8

VMEM = pl.BlockSpec(memory_space=pltpu.VMEM)
SMEM = pl.BlockSpec(memory_space=pltpu.SMEM)
ANY = pl.BlockSpec(memory_space=pl.ANY)


def in_hbm(array):
    return pltpu.with_memory_space_constraint(array, pltpu.HBM)


def mm(a, b):
    return jnp.dot(a, b, preferred_element_type=F32)


def mm_tn(a, b):
    return lax.dot_general(a, b, (((0,), (0,)), ((), ())), preferred_element_type=F32)


def mm_nt(a, b):
    return lax.dot_general(a, b, (((1,), (1,)), ((), ())), preferred_element_type=F32)


def feature_rows(n):
    return slice(n * HEAD_DIM, (n + 1) * HEAD_DIM)


def column(row):
    return jnp.broadcast_to(row, (8, row.shape[1])).T[:, :1]


def same_document(seg_ref, keys, queries):
    return column(seg_ref[:, keys]) == seg_ref[:, queries]


def attend_body(
    lo_ref, hi_ref, seg_ref, bias_ref, turned_hbm, own_hbm, x_hbm, out_hbm, lse_hbm, qkv_hbm, qkv_ref, x_buf, out_ref, lse_ref,
    turned_ref, x_sem, own_sem, out_sem, result_sem, *, groups, rows, tile
):
    count = rows // tile
    own = pl.ds(rows, rows)
    load_turned = pltpu.make_async_copy(turned_hbm, turned_ref, own_sem.at[0])
    load_own = pltpu.make_async_copy(own_hbm, qkv_ref.at[:, own], own_sem.at[1])
    keep_own = pltpu.make_async_copy(qkv_ref.at[:, own], qkv_hbm.at[:, own], own_sem.at[2])

    before = count - jnp.minimum(lo_ref[0], count)
    tiles = before + jnp.maximum(hi_ref[count - 1] - 2 * count, 0)

    def span(t):
        j = jnp.where(t < before, count - before + t, 2 * count + t - before)
        return pl.ds(pl.multiple_of(j * tile, tile), tile)

    def fetch(t):
        slot = lax.rem(t, 2)
        return pltpu.make_async_copy(x_hbm.at[span(t)], x_buf.at[slot], x_sem.at[slot])

    def keep(t):
        return pltpu.make_async_copy(qkv_ref.at[:, span(t)], qkv_hbm.at[:, span(t)], out_sem.at[t])

    load_turned.start()

    @pl.when(tiles > 0)
    def _():
        fetch(0).start()

    load_own.start()
    load_turned.wait()

    def project(t, c):
        @pl.when(t + 1 < tiles)
        def _():
            fetch(t + 1).start()

        fetch(t).wait()
        qkv_ref[:, span(t)] = (mm_nt(turned_ref[...], x_buf[lax.rem(t, 2)]) + bias_ref[...]).astype(BF16)
        keep(t).start()
        return c

    lax.fori_loop(0, tiles, project, 0)
    load_own.wait()
    keep_own.start()

    def put_out(i):
        return pltpu.make_async_copy(out_ref.at[i], out_hbm.at[i], result_sem.at[i])

    def one_query(i, mild):
        at = pl.ds(pl.multiple_of(i * tile, tile), tile)
        win = pl.ds(pl.multiple_of(rows + i * tile, tile), tile)
        queries = [qkv_ref[feature_rows(h), win] * BF16(SCALE) for h in range(groups)]

        def one_key(j, state):
            keys = pl.ds(pl.multiple_of(j * tile, tile), tile)
            same = same_document(seg_ref, keys, win)
            new = []
            ahead = mm_tn(qkv_ref[feature_rows(groups), keys], queries[0])
            for h in range(groups):
                scores = jnp.where(same, ahead, NEG)
                if h + 1 < groups:
                    ahead = mm_tn(qkv_ref[feature_rows(groups + h + 1), keys], queries[h + 1])
                value = qkv_ref[feature_rows(2 * groups + h), keys]
                top, total, acc = state[h]
                if mild:
                    weights = jnp.exp(scores)
                else:
                    peak = jnp.maximum(top, jnp.max(scores, axis=0, keepdims=True))
                    weights = jnp.exp(scores - peak)
                    fade = jnp.exp(top - peak)
                    total, acc, top = total * fade, acc * fade, peak
                total = total + jnp.sum(weights, axis=0, keepdims=True)
                new.append((top, total, acc + mm(value, weights.astype(BF16))))
            return tuple(new)

        zero = tuple(
            (jnp.full((1, tile), 0.0 if mild else NEG, F32), jnp.zeros((1, tile), F32), jnp.zeros((HEAD_DIM, tile), F32))
            for _ in range(groups)
        )
        state = lax.fori_loop(lo_ref[i], hi_ref[i], one_key, zero)
        for h in range(groups):
            top, total, acc = state[h]
            out_ref[i, h * HEAD_DIM : (h + 1) * HEAD_DIM, :] = (acc / total).astype(BF16)
            lse_ref[h : h + 1, at] = top + jnp.log(total)
        put_out(i).start()

    def longest(part, first, last):
        def grow(j, best):
            at = pl.ds(pl.multiple_of(j * tile, tile), tile)
            for h in range(groups):
                values = qkv_ref[feature_rows(part * groups + h), at].astype(F32)
                best = jnp.maximum(best, jnp.sum(values * values, axis=0, keepdims=True))
            return best

        return jnp.max(lax.fori_loop(first, last, grow, jnp.zeros((1, tile), F32)))

    reach = longest(0, count, 2 * count) * longest(1, lo_ref[0], hi_ref[count - 1])
    is_mild = reach <= (MILD / SCALE) ** 2
    for mild in (True, False):

        @pl.when(is_mild == mild)
        def _():
            @pl.loop(0, count)
            def _(i):
                one_query(i, mild)

    put_lse = pltpu.make_async_copy(lse_ref, lse_hbm, result_sem.at[count])
    put_lse.start()
    for i in range(count):
        put_out(i).wait()
    put_lse.wait()
    keep_own.wait()

    def done(t, c):
        keep(t).wait()
        return c

    lax.fori_loop(0, tiles, done, 0)


def attend(x_win, own, turned, bias, seg, lo, hi, groups, rows, tile):
    wide, width = turned.shape
    return pl.pallas_call(
        functools.partial(attend_body, groups=groups, rows=rows, tile=tile),
        out_shape=(
            pltpu.HBM((rows // tile, groups * HEAD_DIM, tile), BF16),
            pltpu.HBM((groups, rows), F32),
            pltpu.HBM((wide, 3 * rows), BF16),
        ),
        in_specs=[SMEM, SMEM, VMEM, VMEM, ANY, ANY, ANY],
        out_specs=(ANY,) * 3,
        scratch_shapes=[
            pltpu.VMEM((wide, 3 * rows), BF16),
            pltpu.VMEM((2, tile, width), BF16),
            pltpu.VMEM((rows // tile, groups * HEAD_DIM, tile), BF16),
            pltpu.VMEM((groups, rows), F32),
            pltpu.VMEM((wide, width), BF16),
            pltpu.SemaphoreType.DMA((2,)),
            pltpu.SemaphoreType.DMA((3,)),
            pltpu.SemaphoreType.DMA((2 * rows // tile,)),
            pltpu.SemaphoreType.DMA((rows // tile + 1,)),
        ],
        compiler_params=pltpu.CompilerParams(vmem_limit_bytes=32 << 20),
        cost_estimate=pl.CostEstimate(flops=36_000_000_000, bytes_accessed=24_000_000, transcendentals=15_000_000),
        name="attend",
    )(lo, hi, seg, bias, in_hbm(turned), in_hbm(own), in_hbm(x_win))


def own_grads_body(
    lo_ref, hi_ref, qkv_hbm, do_hbm, lse_ref, delta_ref, seg_ref, dq_hbm, dk_hbm, dv_hbm, qkv_ref, do_ref, dq_ref, dk_ref, dv_ref,
    acc_ref, in_sem, dq_sem, out_sem, *, groups, rows, tile
):
    count = rows // tile
    q_rows, kv_rows = pl.ds(0, groups * HEAD_DIM), pl.ds(groups * HEAD_DIM, 2 * groups * HEAD_DIM)
    before, own, after = (pl.ds(n * rows, rows) for n in range(3))

    def load(features, tokens, n):
        copy = pltpu.make_async_copy(qkv_hbm.at[features, tokens], qkv_ref.at[features, tokens], in_sem.at[n])
        copy.start()
        return copy

    first = [load(kv_rows, own, 0), load(q_rows, own, 1), pltpu.make_async_copy(do_hbm, do_ref, in_sem.at[2])]
    first[2].start()
    later = [load(kv_rows, before, 3), load(kv_rows, after, 4)]
    dk_ref[...] = jnp.zeros_like(dk_ref)
    dv_ref[...] = jnp.zeros_like(dv_ref)
    for copy in first:
        copy.wait()

    def put_dq(i):
        at = pl.ds(pl.multiple_of(i * tile, tile), tile)
        return pltpu.make_async_copy(dq_ref.at[:, :, at], dq_hbm.at[:, :, at], dq_sem.at[i])

    def one_query(i, _):
        at = pl.ds(pl.multiple_of(i * tile, tile), tile)
        win = pl.ds(pl.multiple_of(rows + i * tile, tile), tile)
        acc_ref[...] = jnp.zeros_like(acc_ref)

        def pair(j, own):
            keys = pl.ds(pl.multiple_of(j * tile, tile), tile)
            mine = pl.ds(pl.multiple_of((j - count) * tile, tile), tile)
            same = same_document(seg_ref, keys, win)

            def products(h):
                query = qkv_ref[feature_rows(h), win] * BF16(SCALE)
                return query, mm_tn(qkv_ref[feature_rows(groups + h), keys], query), mm_tn(qkv_ref[feature_rows(2 * groups + h), keys], do_ref[feature_rows(h), at])

            ahead = products(0)
            for h in range(groups):
                query, scores, d_weights = ahead
                if h + 1 < groups:
                    ahead = products(h + 1)
                weights = jnp.exp(jnp.where(same, scores - lse_ref[h : h + 1, at], NEG))
                d_scores = (weights * (d_weights - delta_ref[h : h + 1, at])).astype(BF16)
                acc_ref[h] += mm(qkv_ref[feature_rows(groups + h), keys], d_scores)
                if own:
                    dv_ref[h, mine, :] += mm_nt(weights.astype(BF16), do_ref[feature_rows(h), at])
                    dk_ref[h, mine, :] += mm_nt(d_scores, query)

        def inside(j, c):
            pair(j, True)
            return c

        def outside(j, c):
            pair(j, False)
            return c

        lo, hi = lo_ref[i], hi_ref[i]
        lax.fori_loop(jnp.maximum(lo, count), jnp.minimum(hi, 2 * count), inside, 0)

        @pl.when(i == 0)
        def _():
            for copy in later:
                copy.wait()

        lax.fori_loop(lo, jnp.minimum(hi, count), outside, 0)
        lax.fori_loop(jnp.maximum(lo, 2 * count), hi, outside, 0)
        dq_ref[:, :, at] = (acc_ref[...] * SCALE).astype(BF16)
        put_dq(i).start()
        return 0

    lax.fori_loop(0, count, one_query, 0)
    results = [pltpu.make_async_copy(dk_ref, dk_hbm, out_sem.at[0]), pltpu.make_async_copy(dv_ref, dv_hbm, out_sem.at[1])]
    for copy in results:
        copy.start()
    for copy in results + [put_dq(i) for i in range(count)]:
        copy.wait()


def own_grads(qkv, d_out, lse, delta, seg, lo, hi, groups, rows, tile):
    return pl.pallas_call(
        functools.partial(own_grads_body, groups=groups, rows=rows, tile=tile),
        out_shape=(
            pltpu.HBM((groups, HEAD_DIM, rows), BF16),
            pltpu.HBM((groups, rows, HEAD_DIM), F32),
            pltpu.HBM((groups, rows, HEAD_DIM), F32),
        ),
        in_specs=[SMEM, SMEM, ANY, ANY, VMEM, VMEM, VMEM],
        out_specs=(ANY,) * 3,
        scratch_shapes=[
            pltpu.VMEM(qkv.shape, BF16),
            pltpu.VMEM(d_out.shape, BF16),
            pltpu.VMEM((groups, HEAD_DIM, rows), BF16),
            pltpu.VMEM((groups, rows, HEAD_DIM), F32),
            pltpu.VMEM((groups, rows, HEAD_DIM), F32),
            pltpu.VMEM((groups, HEAD_DIM, tile), F32),
            pltpu.SemaphoreType.DMA((5,)),
            pltpu.SemaphoreType.DMA((rows // tile,)),
            pltpu.SemaphoreType.DMA((2,)),
        ],
        compiler_params=pltpu.CompilerParams(vmem_limit_bytes=36 << 20),
        cost_estimate=pl.CostEstimate(flops=60_000_000_000, bytes_accessed=20_000_000, transcendentals=15_000_000),
        name="own_grads",
    )(lo, hi, in_hbm(qkv), in_hbm(d_out), lse, delta, seg)


def outer_grads_body(
    lo_ref, hi_ref, qkv_hbm, do_lo_ref, do_hi_ref, lse_lo_ref, lse_hi_ref, delta_lo_ref, delta_hi_ref, seg_ref, dq_hbm, dk_hbm,
    dv_hbm, turned_hbm, x_hbm, dw_hbm, part_hbm, sum_ref, qkv_ref, out_ref, dk_acc, dv_acc, dw_acc, x_buf,
    turned_ref, dw_ref, part_ref, in_sem, tile_sem, out_sem, *, groups, rows, tile
):
    count = rows // tile
    features = groups * HEAD_DIM
    q_rows, kv_rows = pl.ds(0, features), pl.ds(features, 2 * features)
    before, own, after = (pl.ds(n * rows, rows) for n in range(3))

    def load(src, dst, sem):
        copy = pltpu.make_async_copy(src, dst, sem)
        copy.start()
        return copy

    def sums(j):
        at = pl.ds(pl.multiple_of(j * tile, tile), tile)
        return (
            pltpu.make_async_copy(dk_hbm.at[:, at], dk_acc.at[:, at], tile_sem.at[0, j]),
            pltpu.make_async_copy(dv_hbm.at[:, at], dv_acc.at[:, at], tile_sem.at[1, j]),
        )

    first = [
        load(qkv_hbm.at[kv_rows, own], qkv_ref.at[kv_rows, own], in_sem.at[0]),
        load(qkv_hbm.at[q_rows, before], qkv_ref.at[q_rows, before], in_sem.at[1]),
        load(qkv_hbm.at[q_rows, after], qkv_ref.at[q_rows, after], in_sem.at[2]),
    ]
    for j in range(count):
        for copy in sums(j):
            copy.start()
    later = [load(turned_hbm, turned_ref, in_sem.at[3]), load(x_hbm.at[own], x_buf, in_sem.at[4])]
    later += [load(dq_hbm.at[h], out_ref.at[feature_rows(h)], in_sem.at[5 + h]) for h in range(groups)]
    for copy in first:
        copy.wait()

    def one_key(j, _):
        mine = pl.ds(pl.multiple_of(j * tile, tile), tile)
        keys = pl.ds(pl.multiple_of(rows + j * tile, tile), tile)
        for copy in sums(j):
            copy.wait()

        def pair(i, base, do_ref, lse_ref, delta_ref):
            at = pl.ds(pl.multiple_of((i - base) * tile, tile), tile)
            win = pl.ds(pl.multiple_of(i * tile, tile), tile)
            same = same_document(seg_ref, keys, win)

            def products(h):
                query = qkv_ref[feature_rows(h), win] * BF16(SCALE)
                return query, mm_tn(qkv_ref[feature_rows(groups + h), keys], query), mm_tn(qkv_ref[feature_rows(2 * groups + h), keys], do_ref[feature_rows(h), at])

            ahead = products(0)
            for h in range(groups):
                query, scores, d_weights = ahead
                if h + 1 < groups:
                    ahead = products(h + 1)
                weights = jnp.exp(jnp.where(same, scores - lse_ref[h : h + 1, at], NEG))
                d_scores = (weights * (d_weights - delta_ref[h : h + 1, at])).astype(BF16)
                dv_acc[h, mine, :] += mm_nt(weights.astype(BF16), do_ref[feature_rows(h), at])
                dk_acc[h, mine, :] += mm_nt(d_scores, query)

        def before(i, c):
            pair(i, 0, do_lo_ref, lse_lo_ref, delta_lo_ref)
            return c

        def after(i, c):
            pair(i, 2 * count, do_hi_ref, lse_hi_ref, delta_hi_ref)
            return c

        lo, hi = lo_ref[j], hi_ref[j]
        lax.fori_loop(lo, jnp.minimum(hi, count), before, 0)
        lax.fori_loop(jnp.maximum(lo, 2 * count), hi, after, 0)
        for h in range(groups):
            out_ref[feature_rows(groups + h), mine] = dk_acc[h, mine, :].T.astype(BF16)
            out_ref[feature_rows(2 * groups + h), mine] = dv_acc[h, mine, :].T.astype(BF16)
        return 0

    lax.fori_loop(0, count, one_key, 0)
    for copy in later:
        copy.wait()
    dw_acc[...] = jnp.zeros_like(dw_acc)
    sum_ref[...] = jnp.zeros_like(sum_ref)

    def put_part(j):
        at = pl.ds(pl.multiple_of(j * tile, tile), tile)
        return pltpu.make_async_copy(part_ref.at[at], part_hbm.at[at], out_sem.at[j])

    def back(j, _):
        mine = pl.ds(pl.multiple_of(j * tile, tile), tile)
        d = out_ref[:, mine]
        part_ref[mine, :] = mm_tn(d, turned_ref[...]).astype(BF16)
        put_part(j).start()
        dw_acc[...] += mm(d, x_buf[mine, :])
        sum_ref[...] += jnp.sum(d.astype(F32), axis=1, keepdims=True)
        return 0

    lax.fori_loop(0, count, back, 0)
    dw_ref[...] = dw_acc[...].T.astype(BF16)
    load(dw_ref, dw_hbm, out_sem.at[count]).wait()
    for j in range(count):
        put_part(j).wait()


def outer_grads(
    qkv, do_lo, do_hi, lse_lo, lse_hi, delta_lo, delta_hi, seg, dq, dk, dv, turned, x_win, lo, hi, groups, rows, tile
):
    wide, width = turned.shape
    return pl.pallas_call(
        functools.partial(outer_grads_body, groups=groups, rows=rows, tile=tile),
        out_shape=(
            pltpu.HBM((width, wide), BF16),
            pltpu.HBM((rows, width), BF16),
            jax.ShapeDtypeStruct((wide, 1), F32),
        ),
        in_specs=[SMEM, SMEM, ANY] + [VMEM] * 7 + [ANY] * 5,
        out_specs=(ANY, ANY, VMEM),
        scratch_shapes=[
            pltpu.VMEM(qkv.shape, BF16),
            pltpu.VMEM((wide, rows), BF16),
            pltpu.VMEM((groups, rows, HEAD_DIM), F32),
            pltpu.VMEM((groups, rows, HEAD_DIM), F32),
            pltpu.VMEM((wide, width), F32),
            pltpu.VMEM((rows, width), BF16),
            pltpu.VMEM((wide, width), BF16),
            pltpu.VMEM((width, wide), BF16),
            pltpu.VMEM((rows, width), BF16),
            pltpu.SemaphoreType.DMA((5 + groups,)),
            pltpu.SemaphoreType.DMA((2, rows // tile)),
            pltpu.SemaphoreType.DMA((rows // tile + 1,)),
        ],
        compiler_params=pltpu.CompilerParams(vmem_limit_bytes=44 << 20),
        cost_estimate=pl.CostEstimate(flops=24_000_000_000, bytes_accessed=24_000_000, transcendentals=5_000_000),
        name="outer_grads",
    )(lo, hi, in_hbm(qkv), do_lo, do_hi, lse_lo, lse_hi, delta_lo, delta_hi, seg, in_hbm(dq), in_hbm(dk), in_hbm(dv), in_hbm(turned), in_hbm(x_win))


def place():
    return lax.axis_index("blk"), lax.axis_index("head")


def greet_cross(n_blk, n_head):
    blk, head = place()
    barrier = pltpu.get_barrier_semaphore()

    def say_head(step, c):
        to = lax.rem(head + step, n_head)
        pl.semaphore_signal(barrier, inc=1, device_id=(blk, to), device_id_type=MESH)
        return c

    def say_blk(step, c):
        to = lax.rem(blk + step, n_blk)
        pl.semaphore_signal(barrier, inc=1, device_id=(to, head), device_id_type=MESH)
        return c

    lax.fori_loop(1, n_head, say_head, 0)
    lax.fori_loop(1, n_blk, say_blk, 0)
    pl.semaphore_wait(barrier, n_blk + n_head - 2)


def spread(axis, count, src_of, dst, send_sems, recv_sems):
    blk, head = place()
    me = blk if axis == 0 else head

    def copy(step):
        to = lax.rem(me + step, count)
        return pltpu.make_async_remote_copy(
            src_ref=src_of(to),
            dst_ref=dst,
            send_sem=send_sems.at[step],
            recv_sem=recv_sems.at[step],
            device_id=(to, head) if axis == 0 else (blk, to),
            device_id_type=MESH,
        )

    def begin(step, c):
        copy(step).start()
        return c

    def end(step, c):
        copy(step).wait()
        return c

    lax.fori_loop(1, count, begin, 0)
    return lambda: lax.fori_loop(1, count, end, 0)


def collect_body(
    n_blk, n_head, chunks, x_ref, w_ref, xw_ref, wr_ref, qkv_hbm, turned_hbm, bias_ref, vec_ref, inb_ref, x_own, got_ref, w_full, turned_ref, qkv_ref,
    local_sem, near_send, near_recv, w_send, w_recv, x_send, x_recv
):
    blk, head = place()
    rows = x_ref.shape[0] // chunks
    core, row, far = head ^ 1, head ^ 2, head ^ 3
    greet_cross(n_blk, n_head)
    keep_w = pltpu.make_async_copy(w_ref.at[head], wr_ref.at[blk, head], local_sem.at[1])
    keep_w.start()
    wait_near = spread(1, n_head, lambda h: w_ref.at[h], wr_ref.at[blk, head], near_send, near_recv)

    def part(c):
        return pl.ds(c * rows, rows)

    def send(src, slot, owner, c, n, to):
        return pltpu.make_async_remote_copy(
            src_ref=src,
            dst_ref=xw_ref.at[slot, owner, part(c)],
            send_sem=x_send.at[n, c],
            recv_sem=x_recv.at[slot, owner, c],
            device_id=to,
            device_id_type=MESH,
        )

    def arrived(slot, owner, c):
        here = xw_ref.at[slot, owner, part(c)]
        pltpu.make_async_copy(here, here, x_recv.at[slot, owner, c]).wait()

    own = [x_ref.at[part(c)] for c in range(chunks)]
    started = []

    def go(copy):
        copy.start()
        started.append(copy)

    has_before, has_after = blk > 0, blk < n_blk - 1
    to_row = [send(own[c], 1, head, c, 0, (blk, row)) for c in range(chunks)]
    to_core = [send(own[c], 1, head, c, 1, (blk, core)) for c in range(chunks)]
    to_after = [send(own[c], 0, head, c, 2, (blk + 1, head)) for c in range(chunks)]
    to_before = [send(own[c], 2, head, c, 3, (blk - 1, head)) for c in range(chunks)]
    for c in range(chunks):
        go(to_row[c])

        @pl.when(has_after)
        def _():
            to_after[c].start()

        @pl.when(has_before)
        def _():
            to_before[c].start()

        go(to_core[c])
    keep_x = pltpu.make_async_copy(x_ref, xw_ref.at[1, head], local_sem.at[0])
    keep_x.start()
    keep_w.wait()
    wait_near()
    wait_w = spread(0, n_blk, lambda b: wr_ref.at[blk], wr_ref.at[blk], w_send, w_recv)

    for c in range(chunks):
        arrived(1, row, c)
        go(send(xw_ref.at[1, row, part(c)], 1, row, c, 4, (blk, core)))
    halo = []
    for c in range(chunks):
        for slot, there, n in ((0, has_before, 5), (2, has_after, 8)):
            on_row = send(xw_ref.at[slot, head, part(c)], slot, head, c, n, (blk, row))
            on_core = send(xw_ref.at[slot, head, part(c)], slot, head, c, n + 1, (blk, core))
            halo.append((there, on_row))
            halo.append((there, on_core))

            @pl.when(there)
            def _():
                arrived(slot, head, c)
                on_row.start()
                on_core.start()

    for c in range(chunks):
        arrived(1, core, c)
        arrived(1, far, c)
    keep_x.wait()
    load_x = pltpu.make_async_copy(xw_ref.at[1], x_own, local_sem.at[0])
    load_x.start()
    wait_w()
    load_w = pltpu.make_async_copy(wr_ref, got_ref, local_sem.at[1])
    load_w.start()
    load_w.wait()
    per = w_full.shape[0] // (n_blk * n_head)
    bias = jnp.zeros((1, w_full.shape[1]), F32)
    for b in range(n_blk):
        for h in range(n_head):
            first = (b * n_head + h) * per
            w_full[first : first + per] = got_ref[b, h, :per].astype(F32)
            bias = bias + got_ref[b, h, per + 1 : per + 2].astype(F32)
    turned_ref[...] = w_full[...].T.astype(BF16)
    bias_ref[...] = column(bias)
    keep_turned = pltpu.make_async_copy(turned_ref, turned_hbm, local_sem.at[1])
    keep_turned.start()
    load_x.wait()
    tok = x_ref.shape[0]

    def project(n, c):
        at = pl.ds(pl.multiple_of(n * tok, tok), tok)
        qkv_ref[:, at] = (mm_nt(turned_ref[...], x_own[n]) + bias_ref[...]).astype(BF16)
        return c

    lax.fori_loop(0, n_head, project, 0)
    keep_qkv = pltpu.make_async_copy(qkv_ref, qkv_hbm, local_sem.at[0])
    keep_qkv.start()

    vec_ref[...] = jnp.zeros_like(vec_ref)
    if per % 8 == 0:
        pieces = [got_ref[b, h, per : per + 1].astype(F32) for b in range(n_blk) for h in range(n_head)]
        for n in range(2, 8):
            vec_ref[n - 2 : n - 1] = jnp.concatenate([row[:, n * per : (n + 1) * per] for row in pieces], axis=1)
        hidden = inb_ref.shape[1] // len(pieces)
        inb_ref[...] = jnp.concatenate([row[:, 8 * per : 8 * per + hidden] for row in pieces], axis=1)
    else:
        inb_ref[...] = jnp.zeros_like(inb_ref)

    for c in range(chunks):
        for slot, there, n in ((0, has_before, 7), (2, has_after, 10)):
            relay = send(xw_ref.at[slot, row, part(c)], slot, row, c, n, (blk, core))
            halo.append((there, relay))

            @pl.when(there)
            def _():
                arrived(slot, row, c)
                relay.start()

    for c in range(chunks):
        for slot, there in ((0, has_before), (2, has_after)):

            @pl.when(there)
            def _():
                arrived(slot, core, c)
                arrived(slot, far, c)

    keep_turned.wait()
    keep_qkv.wait()
    for copy in started:
        copy.wait_send()
    for there, copies in ((has_after, to_after), (has_before, to_before)):

        @pl.when(there)
        def _():
            for copy in copies:
                copy.wait_send()

    for there, copy in halo:

        @pl.when(there)
        def _():
            copy.wait_send()


def collect(x, w, ff, n_blk, n_head):
    chunks = 2
    tok, width = x.shape
    wide = w.shape[2]
    rows = n_head * tok
    return pl.pallas_call(
        functools.partial(collect_body, n_blk, n_head, chunks),
        out_shape=(
            pltpu.HBM((3, n_head, *x.shape), x.dtype),
            pltpu.HBM((n_blk, *w.shape), w.dtype),
            pltpu.HBM((wide, rows), BF16),
            pltpu.HBM((wide, width), BF16),
            jax.ShapeDtypeStruct((wide, 1), F32),
            jax.ShapeDtypeStruct((8, width), F32),
            jax.ShapeDtypeStruct((1, ff), F32),
        ),
        in_specs=[ANY, ANY],
        out_specs=(ANY,) * 4 + (VMEM,) * 3,
        scratch_shapes=[
            pltpu.VMEM((n_head, tok, width), x.dtype),
            pltpu.VMEM((n_blk, *w.shape), w.dtype),
            pltpu.VMEM((width, wide), F32),
            pltpu.VMEM((wide, width), BF16),
            pltpu.VMEM((wide, rows), BF16),
            pltpu.SemaphoreType.DMA((2,)),
            pltpu.SemaphoreType.DMA((n_head,)),
            pltpu.SemaphoreType.DMA((n_head,)),
            pltpu.SemaphoreType.DMA((n_blk,)),
            pltpu.SemaphoreType.DMA((n_blk,)),
            pltpu.SemaphoreType.DMA((11, chunks)),
            pltpu.SemaphoreType.DMA((3, n_head, chunks)),
        ],
        compiler_params=pltpu.CompilerParams(collective_id=0, has_side_effects=True, vmem_limit_bytes=32 << 20),
        name="collect",
    )(in_hbm(x), in_hbm(w))


def finish_body(
    n_blk, n_head, part_ref, first_hbm, w_ref, t_ref, out_ref, dw_ref, dt_ref, part_row, part_own, first_ref, w_own, near, mine,
    far_in, w_in, t_in, w_sum, t_sum, w_end, t_end, load_sem, x_send, x_recv, w_send, w_recv, t_send, t_recv, w_send2, w_recv2,
    t_send2, t_recv2
):
    blk, head = place()
    core, row, far = head ^ 1, head ^ 2, head ^ 3

    def load(src, dst, n):
        copy = pltpu.make_async_copy(src, dst, load_sem.at[n])
        copy.start()
        return copy

    loads = [
        load(part_ref.at[row], part_row, 0), load(w_ref.at[blk], w_own, 1), load(part_ref.at[head], part_own, 2),
        load(first_hbm, first_ref, 3),
    ]
    greet_cross(n_blk, n_head)

    def send(src, dst, n, to):
        return pltpu.make_async_remote_copy(
            src_ref=src, dst_ref=dst, send_sem=x_send.at[n], recv_sem=x_recv.at[n], device_id=to, device_id_type=MESH
        )

    for_far = send(part_ref.at[far], near.at[1], 1, (blk, core))
    for_core = send(part_ref.at[core], near.at[0], 0, (blk, core))
    for_far.start()
    for_core.start()
    wait_w = spread(0, n_blk, lambda b: w_ref.at[b], w_in.at[blk], w_send, w_recv)
    wait_t = spread(0, n_blk, lambda b: t_ref.at[b], t_in.at[blk], t_send, t_recv)
    loads[0].wait()
    for_far.wait()
    mine[...] = (part_row[...].astype(F32) + near[1].astype(F32)).astype(BF16)
    for_row = send(mine, far_in, 2, (blk, row))
    for_row.start()
    wait_w()
    wait_t()
    loads[1].wait()
    w_sum[...] = w_own[...].astype(F32)
    t_sum[...] = t_ref[blk]

    def add(step, c):
        other = lax.rem(blk + step, n_blk)
        w_sum[...] += w_in[other].astype(F32)
        t_sum[...] += t_in[other]
        return c

    lax.fori_loop(1, n_blk, add, 0)
    wait_w2 = spread(1, n_head, lambda h: w_sum.at[h], w_end.at[head], w_send2, w_recv2)
    wait_t2 = spread(1, n_head, lambda h: t_sum.at[h], t_end.at[head], t_send2, t_recv2)
    w_end[head] = w_sum[head]
    t_end[head] = t_sum[head]
    for_core.wait()
    wait_w2()
    wait_t2()
    dt_ref[...] = jnp.sum(t_end[...], axis=0)
    parts = 3
    cut = dw_ref.shape[1] // (parts * n_head)
    for h in range(n_head):
        for p in range(parts):
            first = (p * n_head + h) * cut
            dw_ref[:, first : first + cut] = w_end[h, :, p * cut : (p + 1) * cut]
    loads[2].wait()
    loads[3].wait()
    for_row.wait()
    out_ref[...] = (
        first_ref[...] + part_own[...].astype(F32) + near[0].astype(F32) + far_in[...].astype(F32)
    ).astype(BF16)


def finish(part, d_first, w, table, n_blk, n_head):
    rows, width = d_first.shape
    _, _, per, wide = w.shape
    return pl.pallas_call(
        functools.partial(finish_body, n_blk, n_head),
        out_shape=(
            jax.ShapeDtypeStruct((rows, width), BF16),
            jax.ShapeDtypeStruct((per, 3 * width), F32),
            jax.ShapeDtypeStruct(table.shape[2:], F32),
        ),
        in_specs=[ANY, ANY, ANY, VMEM],
        out_specs=(VMEM,) * 3,
        scratch_shapes=[
            pltpu.VMEM((rows, width), BF16),
            pltpu.VMEM((rows, width), BF16),
            pltpu.VMEM((rows, width), F32),
            pltpu.VMEM(w.shape[1:], w.dtype),
            pltpu.VMEM((2, rows, width), BF16),
            pltpu.VMEM((rows, width), BF16),
            pltpu.VMEM((rows, width), BF16),
            pltpu.VMEM(w.shape, w.dtype),
            pltpu.VMEM(table.shape, F32),
            pltpu.VMEM(w.shape[1:], F32),
            pltpu.VMEM(table.shape[1:], F32),
            pltpu.VMEM(w.shape[1:], F32),
            pltpu.VMEM(table.shape[1:], F32),
            pltpu.SemaphoreType.DMA((4,)),
            pltpu.SemaphoreType.DMA((3,)),
            pltpu.SemaphoreType.DMA((3,)),
        ]
        + [pltpu.SemaphoreType.DMA((n_blk,))] * 4
        + [pltpu.SemaphoreType.DMA((n_head,))] * 4,
        compiler_params=pltpu.CompilerParams(collective_id=1, has_side_effects=True, vmem_limit_bytes=40 << 20),
        name="finish",
    )(in_hbm(part), in_hbm(d_first), in_hbm(w), table)


def greet(n_blk, n_head):
    blk, head = place()
    barrier = pltpu.get_barrier_semaphore()
    for step in range(1, n_head):
        pl.semaphore_signal(barrier, inc=1, device_id=(blk, lax.rem(head + step, n_head)), device_id_type=MESH)

    @pl.when(blk > 0)
    def _():
        pl.semaphore_signal(barrier, inc=1, device_id=(blk - 1, head), device_id_type=MESH)

    @pl.when(blk < n_blk - 1)
    def _():
        pl.semaphore_signal(barrier, inc=1, device_id=(blk + 1, head), device_id_type=MESH)

    pl.semaphore_wait(barrier, n_head - 1 + jnp.where(blk > 0, 1, 0) + jnp.where(blk < n_blk - 1, 1, 0))


def to_neighbours(n_blk, n_head, src, lo, hi, send_sem, recv_sem):
    blk, head = place()
    cases = (
        (blk > 0, blk < n_blk - 1, hi, (blk - 1, head)),
        (blk < n_blk - 1, blk > 0, lo, (blk + 1, head)),
    )

    def copy(n):
        return pltpu.make_async_remote_copy(
            src_ref=src, dst_ref=cases[n][2], send_sem=send_sem.at[n], recv_sem=recv_sem.at[n], device_id=cases[n][3],
            device_id_type=MESH,
        )

    for n in range(2):

        @pl.when(cases[n][0])
        def _():
            copy(n).start()

    def wait():
        for n in range(2):

            @pl.when(cases[n][0])
            def _():
                copy(n).wait_send()

            @pl.when(cases[n][1])
            def _():
                copy(n).wait_recv()

    return wait


def to_tokens_body(
    n_blk, n_head, out_ref, lse_ref, seq_ref, lse_lo_ref, lse_hi_ref, keep_sem, send_sem, recv_sem, lse_send, lse_recv
):
    blk, head = place()
    greet(n_blk, n_head)

    def part(h):
        return out_ref.at[h]

    def copy(step):
        to = lax.rem(head + step, n_head)
        return pltpu.make_async_remote_copy(
            src_ref=part(to), dst_ref=seq_ref.at[head], send_sem=send_sem.at[step], recv_sem=recv_sem.at[step],
            device_id=(blk, to), device_id_type=MESH,
        )

    for step in range(n_head - 1, 0, -1):
        copy(step).start()
    keep = pltpu.make_async_copy(part(head), seq_ref.at[head], keep_sem)
    keep.start()
    wait = to_neighbours(n_blk, n_head, lse_ref, lse_lo_ref, lse_hi_ref, lse_send, lse_recv)
    for step in range(1, n_head):
        copy(step).wait()
    wait()
    keep.wait()


def to_tokens(out, lse, n_blk, n_head):
    stat = jax.ShapeDtypeStruct(lse.shape, lse.dtype)
    return pl.pallas_call(
        functools.partial(to_tokens_body, n_blk, n_head),
        out_shape=(jax.ShapeDtypeStruct(out.shape, out.dtype), stat, stat),
        in_specs=[ANY, ANY],
        out_specs=(ANY,) * 3,
        scratch_shapes=[
            pltpu.SemaphoreType.DMA,
            pltpu.SemaphoreType.DMA((n_head,)),
            pltpu.SemaphoreType.DMA((n_head,)),
            pltpu.SemaphoreType.DMA((2,)),
            pltpu.SemaphoreType.DMA((2,)),
        ],
        compiler_params=pltpu.CompilerParams(collective_id=2, has_side_effects=True),
        name="to_tokens",
    )(in_hbm(out), in_hbm(lse))


def to_heads_body(
    n_blk, n_head, dseq_ref, dpart_ref, do_ref, delta_ref, delta_lo_ref, delta_hi_ref, keep_sem, send_sem, recv_sem, d_send,
    d_recv, n_send, n_recv
):
    blk, head = place()
    tok = dseq_ref.shape[2]
    greet(n_blk, n_head)
    at = pl.ds(pl.multiple_of(head * tok, tok), tok)

    def copy(step):
        to = lax.rem(head + step, n_head)
        return pltpu.make_async_remote_copy(
            src_ref=dseq_ref.at[to], dst_ref=do_ref.at[:, at], send_sem=send_sem.at[step], recv_sem=recv_sem.at[step],
            device_id=(blk, to), device_id_type=MESH,
        )

    def small_copy(step):
        to = lax.rem(head + step, n_head)
        return pltpu.make_async_remote_copy(
            src_ref=dpart_ref.at[to], dst_ref=delta_ref.at[head], send_sem=d_send.at[step], recv_sem=d_recv.at[step],
            device_id=(blk, to), device_id_type=MESH,
        )

    keep = (
        pltpu.make_async_copy(dseq_ref.at[head], do_ref.at[:, at], keep_sem.at[0]),
        pltpu.make_async_copy(dpart_ref.at[head], delta_ref.at[head], keep_sem.at[1]),
    )
    for step in range(n_head - 1, 0, -1):
        small_copy(step).start()
        copy(step).start()
    for local in keep:
        local.start()
    for step in range(1, n_head):
        small_copy(step).wait()
    keep[1].wait()
    wait = to_neighbours(n_blk, n_head, delta_ref, delta_lo_ref, delta_hi_ref, n_send, n_recv)
    for step in range(1, n_head):
        copy(step).wait()
    keep[0].wait()
    wait()


def to_heads(d_seq, d_part, n_blk, n_head):
    _, cut, tok = d_seq.shape
    stat = jax.ShapeDtypeStruct(d_part.shape, F32)
    return pl.pallas_call(
        functools.partial(to_heads_body, n_blk, n_head),
        out_shape=(jax.ShapeDtypeStruct((cut, n_head * tok), BF16), stat, stat, stat),
        in_specs=[ANY, ANY],
        out_specs=(ANY,) * 4,
        scratch_shapes=[
            pltpu.SemaphoreType.DMA((2,)),
            pltpu.SemaphoreType.DMA((n_head,)),
            pltpu.SemaphoreType.DMA((n_head,)),
            pltpu.SemaphoreType.DMA((n_head,)),
            pltpu.SemaphoreType.DMA((n_head,)),
            pltpu.SemaphoreType.DMA((2,)),
            pltpu.SemaphoreType.DMA((2,)),
        ],
        compiler_params=pltpu.CompilerParams(collective_id=3, has_side_effects=True),
        name="to_heads",
    )(in_hbm(d_seq), in_hbm(d_part))


def regroup(values, outer, inner, unit):
    if unit % 8:
        return values.reshape(-1, outer, inner, unit).transpose(0, 2, 1, 3).reshape(values.shape)
    at = lambda o, i: slice((o * inner + i) * unit, (o * inner + i + 1) * unit)
    return jnp.concatenate([values[:, at(o, i)] for i in range(inner) for o in range(outer)], axis=1)


def pack_body(*refs, count, blocks, n_head):
    (in_ref, mid_ref, down_ref, qkv_ref), vectors, (packed_ref, send_ref) = refs[:4], refs[4:-2], refs[-2:]
    unit, width = mid_ref.shape
    ff = blocks * width
    packed_ref[:, :ff] = regroup(in_ref[...].astype(F32), count, blocks, unit).astype(BF16)
    packed_ref[:, ff : ff + width] = mid_ref[...]
    for n in range(blocks):
        packed_ref[:, ff + width * (n + 1) : ff + width * (n + 2)] = down_ref[n * unit : (n + 1) * unit]

    cut = width // n_head
    vectors = [ref[...].astype(F32) for ref in vectors]
    joined = jnp.concatenate(vectors, axis=1)
    wide = 3 * cut
    pieces = jnp.concatenate([joined, jnp.zeros((1, wide - joined.shape[1]), F32)], axis=1)
    blk, head = place()
    me = blk * n_head + head
    spots = cut // unit

    def in_place(vec):
        return jnp.concatenate([jnp.where(lax.rem(me, spots) == n, vec, 0.0) for n in range(spots)], axis=1)

    placed = jnp.concatenate([in_place(vectors[0]), jnp.zeros((1, cut), F32), in_place(vectors[1])], axis=1)
    weights = qkv_ref[...].astype(F32)
    rest = jnp.zeros((BIAS_ROWS - 2, wide), F32)
    for h in range(n_head):
        columns = jnp.concatenate([weights[:, p * width + h * cut : p * width + (h + 1) * cut] for p in range(3)], axis=1)
        mine = jnp.where(me // spots == h, placed, 0.0)
        send_ref[h] = jnp.concatenate([columns, pieces, mine, rest], axis=0).astype(BF16)


def pack(w_in, w_out, w_down, w_qkv, vectors, count, n_head):
    unit, width = w_out.shape
    blocks = w_down.shape[0] // unit
    cut = width // n_head
    if unit % 8:
        down = w_down.reshape(blocks, unit, width).transpose(1, 0, 2).reshape(unit, -1)
        joined = jnp.concatenate(vectors)
        blk, head = place()
        me = blk * n_head + head
        spots = cut // unit
        zeros = jnp.zeros((cut,), BF16)
        at = lax.rem(me, spots) * unit
        placed = jnp.concatenate(
            [
                lax.dynamic_update_slice_in_dim(zeros, vectors[0], at, 0),
                zeros,
                lax.dynamic_update_slice_in_dim(zeros, vectors[1], at, 0),
            ]
        )
        owner = (jnp.arange(n_head) == me // spots)[:, None]
        rows = jnp.stack(
            [
                jnp.broadcast_to(jnp.pad(joined, (0, 3 * cut - joined.shape[0]))[None], (n_head, 3 * cut)),
                jnp.where(owner, placed[None], jnp.zeros((), BF16)),
            ]
            + [jnp.zeros((n_head, 3 * cut), BF16)] * (BIAS_ROWS - 2),
            axis=1,
        )
        columns = w_qkv.reshape(unit, 3, n_head, cut).transpose(2, 0, 1, 3).reshape(n_head, unit, 3 * cut)
        packed = jnp.concatenate([regroup(w_in, count, blocks, unit), w_out, down], axis=1)
        return packed, jnp.concatenate([columns, rows], axis=1)
    return pl.pallas_call(
        functools.partial(pack_body, count=count, blocks=blocks, n_head=n_head),
        out_shape=(
            jax.ShapeDtypeStruct((unit, 2 * w_in.shape[1] + width), BF16),
            jax.ShapeDtypeStruct((n_head, unit + BIAS_ROWS, 3 * cut), BF16),
        ),
        in_specs=[VMEM] * (4 + len(vectors)),
        out_specs=(VMEM, VMEM),
        name="pack",
    )(w_in, w_out, w_down, w_qkv, *(vec[None] for vec in vectors))


def unpack_body(packed_ref, in_ref, mid_ref, down_ref, *, count, blocks):
    unit, width = mid_ref.shape
    ff = blocks * width
    in_ref[...] = regroup(packed_ref[:, :ff].astype(F32), blocks, count, unit)
    mid_ref[...] = packed_ref[:, ff : ff + width].astype(F32)
    for n in range(blocks):
        down_ref[n * unit : (n + 1) * unit] = packed_ref[:, ff + width * (n + 1) : ff + width * (n + 2)].astype(F32)


def unpack(packed, width, count):
    unit = packed.shape[0]
    blocks = (packed.shape[1] // width - 1) // 2
    ff = blocks * width
    if unit % 8:
        packed = packed.astype(F32)
        down = packed[:, ff + width :].reshape(unit, blocks, width).transpose(1, 0, 2).reshape(-1, width)
        return regroup(packed[:, :ff], blocks, count, unit), packed[:, ff : ff + width], down
    return pl.pallas_call(
        functools.partial(unpack_body, count=count, blocks=blocks),
        out_shape=(
            jax.ShapeDtypeStruct((unit, ff), F32),
            jax.ShapeDtypeStruct((unit, width), F32),
            jax.ShapeDtypeStruct((unit * blocks, width), F32),
        ),
        in_specs=[VMEM],
        out_specs=(VMEM,) * 3,
        name="unpack",
    )(packed)


def normalize(values):
    centre = jnp.mean(values, axis=-1, keepdims=True)
    centered = values - centre
    r = lax.rsqrt(jnp.mean(centered * centered, axis=-1, keepdims=True) + 1e-05)
    return centered * r, r


def normalize_back(d_values, unit, r, gain):
    scaled = d_values * gain
    return r * (
        scaled - jnp.mean(scaled, axis=-1, keepdims=True) - unit * jnp.mean(scaled * unit, axis=-1, keepdims=True)
    )


def over_rows(values):
    return jnp.sum(values, axis=0, keepdims=True)


def dense_body(
    x_ref, seq_ref, cot_ref, vec_ref, inb_ref, w_hbm, out_ref, first_ref, dseq_ref, delta_ref, dvec_ref, dinb_ref, grad_hbm, bias_ref, dbias_ref, w, grad,
    unit_ref, r_ref, normed_ref, low_ref, acc_ref, slope_ref, act_ref, e_ref, w_sem, grad_sem, *, blocks, count
):
    width = x_ref.shape[1]
    out_at, down_at = blocks * width, (blocks + 1) * width

    def fetch(first, size, n):
        at = pl.ds(first, size)
        copy = pltpu.make_async_copy(w_hbm.at[:, at], w.at[:, at], w_sem.at[n])
        copy.start()
        return copy

    def cols(first, c):
        return pl.ds(pl.multiple_of(first + c * width, 128), width)

    def put(first, c, n):
        at = cols(first, c)
        return pltpu.make_async_copy(grad.at[:, at], grad_hbm.at[:, at], grad_sem.at[n])

    piece = width // count
    bias_ref[...] = inb_ref[...] if piece % 8 else regroup(inb_ref[...], count, blocks, piece)
    w_out_here = fetch(out_at, width, 0)
    w_in_here = fetch(0, out_at, 1)
    w_down_here = fetch(down_at, blocks * width, 2)
    out_bias, ln1_gain, ln1_bias, down_bias, ln2_gain, ln2_bias = (vec_ref[n : n + 1] for n in range(6))
    w_out_here.wait()
    unit, r = normalize(x_ref[...].astype(F32) + mm_tn(seq_ref[...], w[:, out_at:down_at]) + out_bias)
    unit_ref[...] = unit
    r_ref[...] = r
    normed = unit * ln1_gain + ln1_bias
    normed_ref[...] = normed
    low_ref[...] = normed.astype(BF16)
    acc_ref[...] = normed + down_bias
    w_in_here.wait()
    w_down_here.wait()

    def up_down(c, carry):
        at = cols(0, c)
        hidden = mm(low_ref[...], w[:, at]) + bias_ref[:, at]
        phi = 0.5 + 0.5 * lax.erf(hidden * (2.0**-0.5))
        act = (hidden * phi).astype(BF16)
        act_ref[:, at] = act
        slope_ref[:, at] = phi + hidden * (jnp.exp(-0.5 * hidden * hidden) * ((2.0 * math.pi) ** -0.5))
        acc_ref[...] += mm(act, w[:, cols(down_at, c)])
        return carry

    lax.fori_loop(0, blocks, up_down, 0, unroll=2)
    unit2, r2 = normalize(acc_ref[...])
    out_ref[...] = (unit2 * ln2_gain + ln2_bias).astype(BF16)
    dy = cot_ref[...].astype(F32)
    dvec_ref[4:5] = over_rows(dy * unit2)
    dvec_ref[5:6] = over_rows(dy)
    d_second = normalize_back(dy, unit2, r2, ln2_gain)
    e_ref[...] = d_second.astype(BF16)
    dvec_ref[3:4] = over_rows(e_ref[...].astype(F32))
    acc_ref[...] = d_second

    def back(c, carry):
        at, down = cols(0, c), cols(down_at, c)
        e = e_ref[...]
        d_hidden = (mm_nt(e, w[:, down]) * slope_ref[:, at]).astype(BF16)
        dbias_ref[:, at] = over_rows(d_hidden.astype(F32))
        acc_ref[...] += mm_nt(d_hidden, w[:, at])
        grad[:, at] = mm_tn(low_ref[...], d_hidden).astype(BF16)
        put(0, c, c).start()
        grad[:, down] = mm_tn(act_ref[:, at], e).astype(BF16)
        put(down_at, c, blocks + c).start()
        return carry

    lax.fori_loop(0, blocks, back, 0, unroll=2)
    d_normed = acc_ref[...]
    unit = unit_ref[...]
    dvec_ref[1:2] = over_rows(d_normed * unit)
    dvec_ref[2:3] = over_rows(d_normed)
    d_first = normalize_back(d_normed, unit, r_ref[...], ln1_gain)
    first_ref[...] = d_first
    e_first = d_first.astype(BF16)
    dvec_ref[0:1] = over_rows(e_first.astype(F32))
    grad[:, out_at:down_at] = mm(seq_ref[...], e_first).astype(BF16)
    put(out_at, 0, 2 * blocks).start()
    d_seq = mm_nt(w[:, out_at:down_at], e_first).astype(BF16)
    dseq_ref[...] = d_seq
    product = d_seq.astype(F32) * seq_ref[...].astype(F32)
    n_head, groups, _ = delta_ref.shape
    for n in range(n_head):
        for g in range(groups):
            first = (n * groups + g) * HEAD_DIM
            delta_ref[n, g : g + 1] = over_rows(product[first : first + HEAD_DIM])

    dinb_ref[...] = dbias_ref[...] if piece % 8 else regroup(dbias_ref[...], blocks, count, piece)

    def done(c, carry):
        put(0, c, c).wait()
        put(down_at, c, blocks + c).wait()
        return carry

    lax.fori_loop(0, blocks, done, 0)
    put(out_at, 0, 2 * blocks).wait()


def dense(x, seq_t, cotangent, vectors, in_bias, weights, blocks, n_head, count):
    tok, width = x.shape
    ff = blocks * width
    return pl.pallas_call(
        functools.partial(dense_body, blocks=blocks, count=count),
        out_shape=(
            jax.ShapeDtypeStruct((tok, width), BF16),
            jax.ShapeDtypeStruct((tok, width), F32),
            jax.ShapeDtypeStruct((width, tok), BF16),
            jax.ShapeDtypeStruct((n_head, width // n_head // HEAD_DIM, tok), F32),
            jax.ShapeDtypeStruct((8, width), F32),
            jax.ShapeDtypeStruct((1, ff), F32),
            jax.ShapeDtypeStruct(weights.shape, BF16),
        ),
        in_specs=[VMEM] * 5 + [ANY],
        out_specs=(VMEM,) * 6 + (ANY,),
        scratch_shapes=[
            pltpu.VMEM((1, ff), F32),
            pltpu.VMEM((1, ff), F32),
            pltpu.VMEM(weights.shape, BF16),
            pltpu.VMEM(weights.shape, BF16),
            pltpu.VMEM((tok, width), F32),
            pltpu.VMEM((tok, 1), F32),
            pltpu.VMEM((tok, width), F32),
            pltpu.VMEM((tok, width), BF16),
            pltpu.VMEM((tok, width), F32),
            pltpu.VMEM((tok, ff), F32),
            pltpu.VMEM((tok, ff), BF16),
            pltpu.VMEM((tok, width), BF16),
            pltpu.SemaphoreType.DMA((3,)),
            pltpu.SemaphoreType.DMA((2 * blocks + 1,)),
        ],
        compiler_params=pltpu.CompilerParams(vmem_limit_bytes=58 << 20),
        cost_estimate=pl.CostEstimate(flops=17_000_000_000, bytes_accessed=30_000_000, transcendentals=3_000_000),
        name="dense",
    )(x, seq_t, cotangent, vectors, in_bias, weights)


def window_of(segments, blk, rows, tile):
    padded = jnp.concatenate(
        [jnp.full((rows,), -1, jnp.int32), segments, jnp.full((rows,), 1 << 30, jnp.int32)]
    )
    seg = lax.dynamic_slice_in_dim(padded, blk * rows, 3 * rows, 0)
    own = seg[rows : 2 * rows]
    below = jnp.sum((seg[None, :] < own[::tile][:, None]).astype(jnp.int32), axis=1)
    upto = jnp.sum((seg[None, :] <= own[tile - 1 :: tile][:, None]).astype(jnp.int32), axis=1)
    return seg[None], below // tile, (upto - 1) // tile + 1


def shift(value, steps):
    count = lax.axis_size("blk")
    first, last = max(0, -steps), min(count, count - steps)
    return lax.ppermute(value, "blk", [(source, source + steps) for source in range(first, last)])


def body(
    inputs, segments, cotangent, w_qkv, q_bias, v_bias, w_out, out_bias, ln1_gain, ln1_bias, w_in, in_bias, w_down,
    down_bias, ln2_gain, ln2_bias
):
    n_blk, n_head = lax.axis_size("blk"), lax.axis_size("head")
    count = n_blk * n_head
    blk, head = place()
    tok, width = inputs.shape
    rows = tok * n_head
    per = w_qkv.shape[0]
    ff = w_in.shape[1]
    blocks = ff // width
    cut = width // n_head
    groups = cut // HEAD_DIM

    small = (q_bias, v_bias, out_bias, ln1_gain, ln1_bias, down_bias, ln2_gain, ln2_bias, in_bias)
    packed, to_send = pack(w_in, w_out, w_down, w_qkv, small, count, n_head)
    whole = lax.all_gather(packed, BOTH, axis=0, tiled=True)

    x_win, got, own_qkv, turned, qkv_bias, vectors, hidden_bias = collect(inputs, to_send, ff, n_blk, n_head)
    x_win = x_win.reshape(3 * rows, width)
    offsets = [0]
    for vec in small:
        offsets.append(offsets[-1] + vec.shape[0])
    if per % 8:
        got = got.reshape(count, *got.shape[2:])
        all_small = got[:, per, : offsets[-1]].astype(F32)
        full = [all_small[:, a:b].reshape(-1) for a, b in zip(offsets[:-1], offsets[1:])]
        vectors = jnp.stack(full[2:8] + full[2:4])
        hidden_bias = regroup(full[8][None], count, blocks, per)
    seg, lo, hi = window_of(segments, blk, rows, tok)
    attended, lse, qkv = attend(x_win, own_qkv, turned, qkv_bias, seg, lo, hi, groups, rows, tok)
    seq_t, lse_lo, lse_hi = to_tokens(attended, lse, n_blk, n_head)
    seq_t = seq_t.reshape(width, tok)

    outputs, d_first, d_seq_t, d_part, d_vectors, d_in_bias, grads = dense(
        inputs, seq_t, cotangent, vectors, hidden_bias, whole, blocks, n_head, count
    )
    d_out_bias, d_ln1_gain, d_ln1_bias, d_down_bias, d_ln2_gain, d_ln2_bias = (d_vectors[n] for n in range(6))
    if per % 8:
        d_in_bias = regroup(d_in_bias, blocks, count, per)
    d_in_bias = d_in_bias[0]
    d_out, delta, delta_lo, delta_hi = to_heads(d_seq_t.reshape(n_head, cut, tok), d_part, n_blk, n_head)
    delta, delta_lo, delta_hi = (a.transpose(1, 0, 2).reshape(groups, rows) for a in (delta, delta_lo, delta_hi))

    owned = lax.psum_scatter(grads, BOTH, scatter_dimension=0, tiled=True)

    do_lo, do_hi = shift(d_out, 1), shift(d_out, -1)
    dq, dk, dv = own_grads(qkv, d_out, lse, delta, seg, lo, hi, groups, rows, tok)
    d_w_qkv, d_part, d_biases = outer_grads(
        qkv, do_lo, do_hi, lse_lo, lse_hi, delta_lo, delta_hi, seg, dq, dk, dv, turned, x_win, lo, hi, groups, rows, tok
    )
    d_biases = d_biases[:, 0]
    place_own = lambda vec: lax.dynamic_update_slice_in_dim(jnp.zeros((width,), F32), vec, head * cut, 0)
    vectors = (
        place_own(d_biases[:cut]), place_own(d_biases[2 * cut :]), d_out_bias, d_ln1_gain, d_ln1_bias, d_down_bias, d_ln2_gain,
        d_ln2_bias, d_in_bias,
    )
    table = jnp.concatenate([vec.reshape(count, -1) for vec in vectors], axis=1)
    lanes = 128
    table_rows = -(-table.shape[1] // (8 * lanes)) * 8
    table = jnp.pad(table, ((0, 0), (0, table_rows * lanes - table.shape[1])))
    d_inputs, own_w_qkv, sums = finish(
        d_part.reshape(n_head, tok, width), d_first, d_w_qkv.reshape(n_blk, n_head, per, 3 * cut),
        table.reshape(n_blk, n_head, table_rows, lanes), n_blk, n_head,
    )
    sums = sums.reshape(-1)
    (o_q_bias, o_v_bias, o_out_bias, o_ln1_gain, o_ln1_bias, o_down_bias, o_ln2_gain, o_ln2_bias, o_in_bias) = (
        sums[a:b] for a, b in zip(offsets[:-1], offsets[1:])
    )
    own_w_in, own_w_out, own_w_down = unpack(owned, width, count)
    return (
        outputs, d_inputs, own_w_qkv, o_q_bias, o_v_bias, own_w_out, o_out_bias, o_ln1_gain, o_ln1_bias,
        own_w_in, o_in_bias, own_w_down, o_down_bias, o_ln2_gain, o_ln2_bias,
    )


def solution(mesh):
    rows, vec = P(BOTH, None), P(BOTH)
    placed = (rows, P(), rows, rows, vec, vec, rows, vec, vec, vec, rows, vec, rows, vec, vec, vec)
    return jax.shard_map(
        body,
        mesh=mesh,
        in_specs=placed,
        out_specs=(rows, rows, rows, vec, vec, rows, vec, vec, vec, rows, vec, rows, vec, vec, vec),
        check_vma=False,
    )
```

```python
import functools
import math

import jax
import jax.numpy as jnp
from jax import lax
from jax.experimental import pallas as pl
from jax.experimental.pallas import tpu as pltpu
from jax.sharding import PartitionSpec as P

HEAD_DIM = 64
F32, BF16 = jnp.float32, jnp.bfloat16
NEG = -1e30
MILD = 60.0
SCALE = HEAD_DIM**-0.5
MESH = pl.DeviceIdType.MESH
BOTH = ("blk", "head")
BIAS_ROWS = 8

VMEM = pl.BlockSpec(memory_space=pltpu.VMEM)
SMEM = pl.BlockSpec(memory_space=pltpu.SMEM)
ANY = pl.BlockSpec(memory_space=pl.ANY)


def in_hbm(array):
    return pltpu.with_memory_space_constraint(array, pltpu.HBM)


def mm(a, b):
    return jnp.dot(a, b, preferred_element_type=F32)


def mm_tn(a, b):
    return lax.dot_general(a, b, (((0,), (0,)), ((), ())), preferred_element_type=F32)


def mm_nt(a, b):
    return lax.dot_general(a, b, (((1,), (1,)), ((), ())), preferred_element_type=F32)


def feature_rows(n):
    return slice(n * HEAD_DIM, (n + 1) * HEAD_DIM)


def column(row):
    return jnp.broadcast_to(row, (8, row.shape[1])).T[:, :1]


def same_document(seg_ref, keys, queries):
    return column(seg_ref[:, keys]) == seg_ref[:, queries]


def attend_body(
    lo_ref, hi_ref, seg_ref, bias_ref, turned_hbm, own_hbm, x_hbm, out_hbm, lse_hbm, qkv_hbm, qkv_ref, x_buf, out_ref, lse_ref,
    turned_ref, x_sem, own_sem, out_sem, result_sem, *, groups, rows, tile
):
    count = rows // tile
    own = pl.ds(rows, rows)
    load_turned = pltpu.make_async_copy(turned_hbm, turned_ref, own_sem.at[0])
    load_own = pltpu.make_async_copy(own_hbm, qkv_ref.at[:, own], own_sem.at[1])
    keep_own = pltpu.make_async_copy(qkv_ref.at[:, own], qkv_hbm.at[:, own], own_sem.at[2])

    before = count - jnp.minimum(lo_ref[0], count)
    tiles = before + jnp.maximum(hi_ref[count - 1] - 2 * count, 0)

    def span(t):
        j = jnp.where(t < before, count - before + t, 2 * count + t - before)
        return pl.ds(pl.multiple_of(j * tile, tile), tile)

    def fetch(t):
        slot = lax.rem(t, 2)
        return pltpu.make_async_copy(x_hbm.at[span(t)], x_buf.at[slot], x_sem.at[slot])

    def keep(t):
        return pltpu.make_async_copy(qkv_ref.at[:, span(t)], qkv_hbm.at[:, span(t)], out_sem.at[t])

    load_turned.start()

    @pl.when(tiles > 0)
    def _():
        fetch(0).start()

    load_own.start()
    load_turned.wait()

    def project(t, c):
        @pl.when(t + 1 < tiles)
        def _():
            fetch(t + 1).start()

        fetch(t).wait()
        qkv_ref[:, span(t)] = (mm_nt(turned_ref[...], x_buf[lax.rem(t, 2)]) + bias_ref[...]).astype(BF16)
        keep(t).start()
        return c

    lax.fori_loop(0, tiles, project, 0)
    load_own.wait()
    keep_own.start()

    def put_out(i):
        return pltpu.make_async_copy(out_ref.at[i], out_hbm.at[i], result_sem.at[i])

    def one_query(i, mild):
        at = pl.ds(pl.multiple_of(i * tile, tile), tile)
        win = pl.ds(pl.multiple_of(rows + i * tile, tile), tile)
        queries = [qkv_ref[feature_rows(h), win] * BF16(SCALE) for h in range(groups)]

        def meet(tiles, state):
            keys = [pl.ds(pl.multiple_of(j * tile, tile), tile) for j in tiles]
            same = [same_document(seg_ref, at, win) for at in keys]
            steps = [(n, h) for n in range(len(tiles)) for h in range(groups)]

            def product(n, h):
                return mm_tn(qkv_ref[feature_rows(groups + h), keys[n]], queries[h])

            state = list(state)
            ahead = product(*steps[0])
            for at, (n, h) in enumerate(steps):
                scores = jnp.where(same[n], ahead, NEG)
                if at + 1 < len(steps):
                    ahead = product(*steps[at + 1])
                value = qkv_ref[feature_rows(2 * groups + h), keys[n]]
                top, total, acc = state[h]
                if mild:
                    weights = jnp.exp(scores)
                else:
                    peak = jnp.maximum(top, jnp.max(scores, axis=0, keepdims=True))
                    weights = jnp.exp(scores - peak)
                    fade = jnp.exp(top - peak)
                    total, acc, top = total * fade, acc * fade, peak
                total = total + jnp.sum(weights, axis=0, keepdims=True)
                state[h] = (top, total, acc + mm(value, weights.astype(BF16)))
            return tuple(state)

        zero = tuple(
            (jnp.full((1, tile), 0.0 if mild else NEG, F32), jnp.zeros((1, tile), F32), jnp.zeros((HEAD_DIM, tile), F32))
            for _ in range(groups)
        )
        lo, hi = lo_ref[i], hi_ref[i]
        start = lo
        state = zero
        if mild:
            pairs = (hi - lo) // 2
            state = lax.fori_loop(0, pairs, lambda t, c: meet([lo + 2 * t, lo + 2 * t + 1], c), state)
            start = lo + 2 * pairs
        state = lax.fori_loop(start, hi, lambda j, c: meet([j], c), state)
        for h in range(groups):
            top, total, acc = state[h]
            out_ref[i, h * HEAD_DIM : (h + 1) * HEAD_DIM, :] = (acc / total).astype(BF16)
            lse_ref[h : h + 1, at] = top + jnp.log(total)
        put_out(i).start()

    def longest(part, first, last):
        def grow(j, best):
            at = pl.ds(pl.multiple_of(j * tile, tile), tile)
            for h in range(groups):
                values = qkv_ref[feature_rows(part * groups + h), at].astype(F32)
                best = jnp.maximum(best, jnp.sum(values * values, axis=0, keepdims=True))
            return best

        return jnp.max(lax.fori_loop(first, last, grow, jnp.zeros((1, tile), F32)))

    reach = longest(0, count, 2 * count) * longest(1, lo_ref[0], hi_ref[count - 1])
    is_mild = reach <= (MILD / SCALE) ** 2
    for mild in (True, False):

        @pl.when(is_mild == mild)
        def _():
            @pl.loop(0, count)
            def _(i):
                one_query(i, mild)

    put_lse = pltpu.make_async_copy(lse_ref, lse_hbm, result_sem.at[count])
    put_lse.start()
    for i in range(count):
        put_out(i).wait()
    put_lse.wait()
    keep_own.wait()

    def done(t, c):
        keep(t).wait()
        return c

    lax.fori_loop(0, tiles, done, 0)


def attend(x_win, own, turned, bias, seg, lo, hi, groups, rows, tile):
    wide, width = turned.shape
    return pl.pallas_call(
        functools.partial(attend_body, groups=groups, rows=rows, tile=tile),
        out_shape=(
            pltpu.HBM((rows // tile, groups * HEAD_DIM, tile), BF16),
            pltpu.HBM((groups, rows), F32),
            pltpu.HBM((wide, 3 * rows), BF16),
        ),
        in_specs=[SMEM, SMEM, VMEM, VMEM, ANY, ANY, ANY],
        out_specs=(ANY,) * 3,
        scratch_shapes=[
            pltpu.VMEM((wide, 3 * rows), BF16),
            pltpu.VMEM((2, tile, width), BF16),
            pltpu.VMEM((rows // tile, groups * HEAD_DIM, tile), BF16),
            pltpu.VMEM((groups, rows), F32),
            pltpu.VMEM((wide, width), BF16),
            pltpu.SemaphoreType.DMA((2,)),
            pltpu.SemaphoreType.DMA((3,)),
            pltpu.SemaphoreType.DMA((2 * rows // tile,)),
            pltpu.SemaphoreType.DMA((rows // tile + 1,)),
        ],
        compiler_params=pltpu.CompilerParams(vmem_limit_bytes=32 << 20),
        cost_estimate=pl.CostEstimate(flops=36_000_000_000, bytes_accessed=24_000_000, transcendentals=15_000_000),
        name="attend",
    )(lo, hi, seg, bias, in_hbm(turned), in_hbm(own), in_hbm(x_win))


def own_grads_body(
    lo_ref, hi_ref, qkv_hbm, do_hbm, lse_ref, delta_ref, seg_ref, dq_hbm, dk_hbm, dv_hbm, qkv_ref, do_ref, dq_ref, dk_ref, dv_ref,
    acc_ref, in_sem, dq_sem, out_sem, *, groups, rows, tile
):
    count = rows // tile
    q_rows, kv_rows = pl.ds(0, groups * HEAD_DIM), pl.ds(groups * HEAD_DIM, 2 * groups * HEAD_DIM)
    before, own, after = (pl.ds(n * rows, rows) for n in range(3))

    def load(features, tokens, n):
        copy = pltpu.make_async_copy(qkv_hbm.at[features, tokens], qkv_ref.at[features, tokens], in_sem.at[n])
        copy.start()
        return copy

    first = [load(kv_rows, own, 0), load(q_rows, own, 1), pltpu.make_async_copy(do_hbm, do_ref, in_sem.at[2])]
    first[2].start()
    later = [load(kv_rows, before, 3), load(kv_rows, after, 4)]
    acc_ref[...] = jnp.zeros_like(acc_ref)
    for copy in first:
        copy.wait()

    def tokens(n):
        return pl.ds(pl.multiple_of(n * tile, tile), tile)

    def put_dq(i):
        return pltpu.make_async_copy(dq_ref.at[:, :, tokens(i)], dq_hbm.at[:, :, tokens(i)], dq_sem.at[i])

    def put_sums(j):
        return (
            pltpu.make_async_copy(dk_ref.at[:, tokens(j)], dk_hbm.at[:, tokens(j)], out_sem.at[0, j]),
            pltpu.make_async_copy(dv_ref.at[:, tokens(j)], dv_hbm.at[:, tokens(j)], out_sem.at[1, j]),
        )

    def pair(i, j, mine):
        at, win, keys = tokens(i), tokens(count + i), tokens(j)
        same = same_document(seg_ref, keys, win)

        def products(h):
            query = qkv_ref[feature_rows(h), win] * BF16(SCALE)
            return (
                query,
                mm_tn(qkv_ref[feature_rows(groups + h), keys], query),
                mm_tn(qkv_ref[feature_rows(2 * groups + h), keys], do_ref[feature_rows(h), at]),
            )

        ahead = products(0)
        for h in range(groups):
            query, scores, d_weights = ahead
            if h + 1 < groups:
                ahead = products(h + 1)
            weights = jnp.exp(jnp.where(same, scores - lse_ref[h : h + 1, at], NEG))
            d_scores = (weights * (d_weights - delta_ref[h : h + 1, at])).astype(BF16)
            acc_ref[h, :, at] += mm(qkv_ref[feature_rows(groups + h), keys], d_scores)
            if mine is not None:
                dv_ref[h, tokens(mine), :] += mm_nt(weights.astype(BF16), do_ref[feature_rows(h), at])
                dk_ref[h, tokens(mine), :] += mm_nt(d_scores, query)

    def one_key(j, _):
        dk_ref[:, tokens(j), :] = jnp.zeros((groups, tile, HEAD_DIM), F32)
        dv_ref[:, tokens(j), :] = jnp.zeros((groups, tile, HEAD_DIM), F32)

        def inside(i, c):
            pair(i - count, count + j, j)
            return c

        lax.fori_loop(jnp.maximum(lo_ref[j], count), jnp.minimum(hi_ref[j], 2 * count), inside, 0)
        for copy in put_sums(j):
            copy.start()
        return 0

    lax.fori_loop(0, count, one_key, 0)
    for copy in later:
        copy.wait()

    def one_query(i, _):
        low = count - jnp.minimum(lo_ref[i], count)
        high = jnp.maximum(hi_ref[i] - 2 * count, 0)

        def outside(t, c):
            pair(i, jnp.where(t < low, count - low + t, 2 * count + t - low), None)
            return c

        lax.fori_loop(0, low + high, outside, 0)
        dq_ref[:, :, tokens(i)] = (acc_ref[:, :, tokens(i)] * SCALE).astype(BF16)
        put_dq(i).start()
        return 0

    lax.fori_loop(0, count, one_query, 0)
    for n in range(count):
        put_dq(n).wait()
        for copy in put_sums(n):
            copy.wait()


def own_grads(qkv, d_out, lse, delta, seg, lo, hi, groups, rows, tile):
    return pl.pallas_call(
        functools.partial(own_grads_body, groups=groups, rows=rows, tile=tile),
        out_shape=(
            pltpu.HBM((groups, HEAD_DIM, rows), BF16),
            pltpu.HBM((groups, rows, HEAD_DIM), F32),
            pltpu.HBM((groups, rows, HEAD_DIM), F32),
        ),
        in_specs=[SMEM, SMEM, ANY, ANY, VMEM, VMEM, VMEM],
        out_specs=(ANY,) * 3,
        scratch_shapes=[
            pltpu.VMEM(qkv.shape, BF16),
            pltpu.VMEM(d_out.shape, BF16),
            pltpu.VMEM((groups, HEAD_DIM, rows), BF16),
            pltpu.VMEM((groups, rows, HEAD_DIM), F32),
            pltpu.VMEM((groups, rows, HEAD_DIM), F32),
            pltpu.VMEM((groups, HEAD_DIM, rows), F32),
            pltpu.SemaphoreType.DMA((5,)),
            pltpu.SemaphoreType.DMA((rows // tile,)),
            pltpu.SemaphoreType.DMA((2, rows // tile)),
        ],
        compiler_params=pltpu.CompilerParams(vmem_limit_bytes=36 << 20),
        cost_estimate=pl.CostEstimate(flops=60_000_000_000, bytes_accessed=20_000_000, transcendentals=15_000_000),
        name="own_grads",
    )(lo, hi, in_hbm(qkv), in_hbm(d_out), lse, delta, seg)


def outer_grads_body(
    lo_ref, hi_ref, qkv_hbm, do_lo_ref, do_hi_ref, lse_lo_ref, lse_hi_ref, delta_lo_ref, delta_hi_ref, seg_ref, dq_hbm, dk_hbm,
    dv_hbm, turned_hbm, x_hbm, dw_hbm, part_hbm, sum_ref, qkv_ref, out_ref, dk_acc, dv_acc, dw_acc, x_buf,
    turned_ref, dw_ref, part_ref, in_sem, tile_sem, out_sem, *, groups, rows, tile
):
    count = rows // tile
    features = groups * HEAD_DIM
    q_rows, kv_rows = pl.ds(0, features), pl.ds(features, 2 * features)
    before, own, after = (pl.ds(n * rows, rows) for n in range(3))

    def load(src, dst, sem):
        copy = pltpu.make_async_copy(src, dst, sem)
        copy.start()
        return copy

    def sums(j):
        at = pl.ds(pl.multiple_of(j * tile, tile), tile)
        return (
            pltpu.make_async_copy(dk_hbm.at[:, at], dk_acc.at[:, at], tile_sem.at[0, j]),
            pltpu.make_async_copy(dv_hbm.at[:, at], dv_acc.at[:, at], tile_sem.at[1, j]),
        )

    first = [
        load(qkv_hbm.at[kv_rows, own], qkv_ref.at[kv_rows, own], in_sem.at[0]),
        load(qkv_hbm.at[q_rows, before], qkv_ref.at[q_rows, before], in_sem.at[1]),
        load(qkv_hbm.at[q_rows, after], qkv_ref.at[q_rows, after], in_sem.at[2]),
    ]
    for j in range(count):
        for copy in sums(j):
            copy.start()
    later = [load(turned_hbm, turned_ref, in_sem.at[3]), load(x_hbm.at[own], x_buf, in_sem.at[4])]
    later += [load(dq_hbm.at[h], out_ref.at[feature_rows(h)], in_sem.at[5 + h]) for h in range(groups)]
    for copy in first:
        copy.wait()

    def one_key(j, _):
        mine = pl.ds(pl.multiple_of(j * tile, tile), tile)
        keys = pl.ds(pl.multiple_of(rows + j * tile, tile), tile)
        for copy in sums(j):
            copy.wait()

        def pair(i, base, do_ref, lse_ref, delta_ref):
            at = pl.ds(pl.multiple_of((i - base) * tile, tile), tile)
            win = pl.ds(pl.multiple_of(i * tile, tile), tile)
            same = same_document(seg_ref, keys, win)

            def products(h):
                query = qkv_ref[feature_rows(h), win] * BF16(SCALE)
                return query, mm_tn(qkv_ref[feature_rows(groups + h), keys], query), mm_tn(qkv_ref[feature_rows(2 * groups + h), keys], do_ref[feature_rows(h), at])

            ahead = products(0)
            for h in range(groups):
                query, scores, d_weights = ahead
                if h + 1 < groups:
                    ahead = products(h + 1)
                weights = jnp.exp(jnp.where(same, scores - lse_ref[h : h + 1, at], NEG))
                d_scores = (weights * (d_weights - delta_ref[h : h + 1, at])).astype(BF16)
                dv_acc[h, mine, :] += mm_nt(weights.astype(BF16), do_ref[feature_rows(h), at])
                dk_acc[h, mine, :] += mm_nt(d_scores, query)

        def before(i, c):
            pair(i, 0, do_lo_ref, lse_lo_ref, delta_lo_ref)
            return c

        def after(i, c):
            pair(i, 2 * count, do_hi_ref, lse_hi_ref, delta_hi_ref)
            return c

        lo, hi = lo_ref[j], hi_ref[j]
        lax.fori_loop(lo, jnp.minimum(hi, count), before, 0)
        lax.fori_loop(jnp.maximum(lo, 2 * count), hi, after, 0)
        for h in range(groups):
            out_ref[feature_rows(groups + h), mine] = dk_acc[h, mine, :].T.astype(BF16)
            out_ref[feature_rows(2 * groups + h), mine] = dv_acc[h, mine, :].T.astype(BF16)
        return 0

    lax.fori_loop(0, count, one_key, 0)
    for copy in later:
        copy.wait()
    dw_acc[...] = jnp.zeros_like(dw_acc)
    sum_ref[...] = jnp.zeros_like(sum_ref)

    def put_part(j):
        at = pl.ds(pl.multiple_of(j * tile, tile), tile)
        return pltpu.make_async_copy(part_ref.at[at], part_hbm.at[at], out_sem.at[j])

    def back(j, _):
        mine = pl.ds(pl.multiple_of(j * tile, tile), tile)
        d = out_ref[:, mine]
        part_ref[mine, :] = mm_tn(d, turned_ref[...]).astype(BF16)
        put_part(j).start()
        dw_acc[...] += mm(d, x_buf[mine, :])
        sum_ref[...] += jnp.sum(d.astype(F32), axis=1, keepdims=True)
        return 0

    lax.fori_loop(0, count, back, 0)
    dw_ref[...] = dw_acc[...].T.astype(BF16)
    load(dw_ref, dw_hbm, out_sem.at[count]).wait()
    for j in range(count):
        put_part(j).wait()


def outer_grads(
    qkv, do_lo, do_hi, lse_lo, lse_hi, delta_lo, delta_hi, seg, dq, dk, dv, turned, x_win, lo, hi, groups, rows, tile
):
    wide, width = turned.shape
    return pl.pallas_call(
        functools.partial(outer_grads_body, groups=groups, rows=rows, tile=tile),
        out_shape=(
            pltpu.HBM((width, wide), BF16),
            pltpu.HBM((rows, width), BF16),
            jax.ShapeDtypeStruct((wide, 1), F32),
        ),
        in_specs=[SMEM, SMEM, ANY] + [VMEM] * 7 + [ANY] * 5,
        out_specs=(ANY, ANY, VMEM),
        scratch_shapes=[
            pltpu.VMEM(qkv.shape, BF16),
            pltpu.VMEM((wide, rows), BF16),
            pltpu.VMEM((groups, rows, HEAD_DIM), F32),
            pltpu.VMEM((groups, rows, HEAD_DIM), F32),
            pltpu.VMEM((wide, width), F32),
            pltpu.VMEM((rows, width), BF16),
            pltpu.VMEM((wide, width), BF16),
            pltpu.VMEM((width, wide), BF16),
            pltpu.VMEM((rows, width), BF16),
            pltpu.SemaphoreType.DMA((5 + groups,)),
            pltpu.SemaphoreType.DMA((2, rows // tile)),
            pltpu.SemaphoreType.DMA((rows // tile + 1,)),
        ],
        compiler_params=pltpu.CompilerParams(vmem_limit_bytes=44 << 20),
        cost_estimate=pl.CostEstimate(flops=24_000_000_000, bytes_accessed=24_000_000, transcendentals=5_000_000),
        name="outer_grads",
    )(lo, hi, in_hbm(qkv), do_lo, do_hi, lse_lo, lse_hi, delta_lo, delta_hi, seg, in_hbm(dq), in_hbm(dk), in_hbm(dv), in_hbm(turned), in_hbm(x_win))


def place():
    return lax.axis_index("blk"), lax.axis_index("head")


def greet_cross(n_blk, n_head):
    blk, head = place()
    barrier = pltpu.get_barrier_semaphore()

    def say_head(step, c):
        to = lax.rem(head + step, n_head)
        pl.semaphore_signal(barrier, inc=1, device_id=(blk, to), device_id_type=MESH)
        return c

    def say_blk(step, c):
        to = lax.rem(blk + step, n_blk)
        pl.semaphore_signal(barrier, inc=1, device_id=(to, head), device_id_type=MESH)
        return c

    lax.fori_loop(1, n_head, say_head, 0)
    lax.fori_loop(1, n_blk, say_blk, 0)
    pl.semaphore_wait(barrier, n_blk + n_head - 2)


def spread(axis, count, src_of, dst, send_sems, recv_sems):
    blk, head = place()
    me = blk if axis == 0 else head

    def copy(step):
        to = lax.rem(me + step, count)
        return pltpu.make_async_remote_copy(
            src_ref=src_of(to),
            dst_ref=dst,
            send_sem=send_sems.at[step],
            recv_sem=recv_sems.at[step],
            device_id=(to, head) if axis == 0 else (blk, to),
            device_id_type=MESH,
        )

    def begin(step, c):
        copy(step).start()
        return c

    def end(step, c):
        copy(step).wait()
        return c

    lax.fori_loop(1, count, begin, 0)
    return lambda: lax.fori_loop(1, count, end, 0)


def collect_body(
    n_blk, n_head, chunks, x_ref, w_ref, xw_ref, wr_ref, qkv_hbm, turned_hbm, bias_ref, vec_ref, inb_ref, x_own, got_ref, w_full, turned_ref, qkv_ref,
    local_sem, near_send, near_recv, w_send, w_recv, x_send, x_recv
):
    blk, head = place()
    rows = x_ref.shape[0] // chunks
    core, row, far = head ^ 1, head ^ 2, head ^ 3
    greet_cross(n_blk, n_head)
    keep_w = pltpu.make_async_copy(w_ref.at[head], wr_ref.at[blk, head], local_sem.at[1])
    keep_w.start()
    wait_near = spread(1, n_head, lambda h: w_ref.at[h], wr_ref.at[blk, head], near_send, near_recv)

    def part(c):
        return pl.ds(c * rows, rows)

    def send(src, slot, owner, c, n, to):
        return pltpu.make_async_remote_copy(
            src_ref=src,
            dst_ref=xw_ref.at[slot, owner, part(c)],
            send_sem=x_send.at[n, c],
            recv_sem=x_recv.at[slot, owner, c],
            device_id=to,
            device_id_type=MESH,
        )

    def arrived(slot, owner, c):
        here = xw_ref.at[slot, owner, part(c)]
        pltpu.make_async_copy(here, here, x_recv.at[slot, owner, c]).wait()

    own = [x_ref.at[part(c)] for c in range(chunks)]
    started = []

    def go(copy):
        copy.start()
        started.append(copy)

    has_before, has_after = blk > 0, blk < n_blk - 1
    to_row = [send(own[c], 1, head, c, 0, (blk, row)) for c in range(chunks)]
    to_core = [send(own[c], 1, head, c, 1, (blk, core)) for c in range(chunks)]
    to_after = [send(own[c], 0, head, c, 2, (blk + 1, head)) for c in range(chunks)]
    to_before = [send(own[c], 2, head, c, 3, (blk - 1, head)) for c in range(chunks)]
    for c in range(chunks):
        go(to_row[c])

        @pl.when(has_after)
        def _():
            to_after[c].start()

        @pl.when(has_before)
        def _():
            to_before[c].start()

        go(to_core[c])
    keep_x = pltpu.make_async_copy(x_ref, xw_ref.at[1, head], local_sem.at[0])
    keep_x.start()
    keep_w.wait()
    wait_near()
    wait_w = spread(0, n_blk, lambda b: wr_ref.at[blk], wr_ref.at[blk], w_send, w_recv)

    for c in range(chunks):
        arrived(1, row, c)
        go(send(xw_ref.at[1, row, part(c)], 1, row, c, 4, (blk, core)))
    halo = []
    for c in range(chunks):
        for slot, there, n in ((0, has_before, 5), (2, has_after, 8)):
            on_row = send(xw_ref.at[slot, head, part(c)], slot, head, c, n, (blk, row))
            on_core = send(xw_ref.at[slot, head, part(c)], slot, head, c, n + 1, (blk, core))
            halo.append((there, on_row))
            halo.append((there, on_core))

            @pl.when(there)
            def _():
                arrived(slot, head, c)
                on_row.start()
                on_core.start()

    for c in range(chunks):
        arrived(1, core, c)
        arrived(1, far, c)
    keep_x.wait()
    load_x = pltpu.make_async_copy(xw_ref.at[1], x_own, local_sem.at[0])
    load_x.start()
    wait_w()
    load_w = pltpu.make_async_copy(wr_ref, got_ref, local_sem.at[1])
    load_w.start()
    load_w.wait()
    per = w_full.shape[0] // (n_blk * n_head)
    bias = jnp.zeros((1, w_full.shape[1]), F32)
    for b in range(n_blk):
        for h in range(n_head):
            first = (b * n_head + h) * per
            w_full[first : first + per] = got_ref[b, h, :per].astype(F32)
            bias = bias + got_ref[b, h, per + 1 : per + 2].astype(F32)
    turned_ref[...] = w_full[...].T.astype(BF16)
    bias_ref[...] = column(bias)
    keep_turned = pltpu.make_async_copy(turned_ref, turned_hbm, local_sem.at[1])
    keep_turned.start()
    load_x.wait()
    tok = x_ref.shape[0]

    def project(n, c):
        at = pl.ds(pl.multiple_of(n * tok, tok), tok)
        qkv_ref[:, at] = (mm_nt(turned_ref[...], x_own[n]) + bias_ref[...]).astype(BF16)
        return c

    lax.fori_loop(0, n_head, project, 0)
    keep_qkv = pltpu.make_async_copy(qkv_ref, qkv_hbm, local_sem.at[0])
    keep_qkv.start()

    vec_ref[...] = jnp.zeros_like(vec_ref)
    if per % 8 == 0:
        pieces = [got_ref[b, h, per : per + 1].astype(F32) for b in range(n_blk) for h in range(n_head)]
        for n in range(2, 8):
            vec_ref[n - 2 : n - 1] = jnp.concatenate([row[:, n * per : (n + 1) * per] for row in pieces], axis=1)
        hidden = inb_ref.shape[1] // len(pieces)
        inb_ref[...] = jnp.concatenate([row[:, 8 * per : 8 * per + hidden] for row in pieces], axis=1)
    else:
        inb_ref[...] = jnp.zeros_like(inb_ref)

    for c in range(chunks):
        for slot, there, n in ((0, has_before, 7), (2, has_after, 10)):
            relay = send(xw_ref.at[slot, row, part(c)], slot, row, c, n, (blk, core))
            halo.append((there, relay))

            @pl.when(there)
            def _():
                arrived(slot, row, c)
                relay.start()

    for c in range(chunks):
        for slot, there in ((0, has_before), (2, has_after)):

            @pl.when(there)
            def _():
                arrived(slot, core, c)
                arrived(slot, far, c)

    keep_turned.wait()
    keep_qkv.wait()
    for copy in started:
        copy.wait_send()
    for there, copies in ((has_after, to_after), (has_before, to_before)):

        @pl.when(there)
        def _():
            for copy in copies:
                copy.wait_send()

    for there, copy in halo:

        @pl.when(there)
        def _():
            copy.wait_send()


def collect(x, w, ff, n_blk, n_head):
    chunks = 2
    tok, width = x.shape
    wide = w.shape[2]
    rows = n_head * tok
    return pl.pallas_call(
        functools.partial(collect_body, n_blk, n_head, chunks),
        out_shape=(
            pltpu.HBM((3, n_head, *x.shape), x.dtype),
            pltpu.HBM((n_blk, *w.shape), w.dtype),
            pltpu.HBM((wide, rows), BF16),
            pltpu.HBM((wide, width), BF16),
            jax.ShapeDtypeStruct((wide, 1), F32),
            jax.ShapeDtypeStruct((8, width), F32),
            jax.ShapeDtypeStruct((1, ff), F32),
        ),
        in_specs=[ANY, ANY],
        out_specs=(ANY,) * 4 + (VMEM,) * 3,
        scratch_shapes=[
            pltpu.VMEM((n_head, tok, width), x.dtype),
            pltpu.VMEM((n_blk, *w.shape), w.dtype),
            pltpu.VMEM((width, wide), F32),
            pltpu.VMEM((wide, width), BF16),
            pltpu.VMEM((wide, rows), BF16),
            pltpu.SemaphoreType.DMA((2,)),
            pltpu.SemaphoreType.DMA((n_head,)),
            pltpu.SemaphoreType.DMA((n_head,)),
            pltpu.SemaphoreType.DMA((n_blk,)),
            pltpu.SemaphoreType.DMA((n_blk,)),
            pltpu.SemaphoreType.DMA((11, chunks)),
            pltpu.SemaphoreType.DMA((3, n_head, chunks)),
        ],
        compiler_params=pltpu.CompilerParams(collective_id=0, has_side_effects=True, vmem_limit_bytes=32 << 20),
        name="collect",
    )(in_hbm(x), in_hbm(w))


def finish_body(
    n_blk, n_head, part_ref, first_hbm, w_ref, t_ref, out_ref, dw_ref, dt_ref, part_row, part_own, first_ref, w_own, near, mine,
    far_in, w_in, t_in, w_sum, t_sum, w_end, t_end, load_sem, x_send, x_recv, w_send, w_recv, t_send, t_recv, w_send2, w_recv2,
    t_send2, t_recv2
):
    blk, head = place()
    core, row, far = head ^ 1, head ^ 2, head ^ 3

    def load(src, dst, n):
        copy = pltpu.make_async_copy(src, dst, load_sem.at[n])
        copy.start()
        return copy

    loads = [
        load(part_ref.at[row], part_row, 0), load(w_ref.at[blk], w_own, 1), load(part_ref.at[head], part_own, 2),
        load(first_hbm, first_ref, 3),
    ]
    greet_cross(n_blk, n_head)

    def send(src, dst, n, to):
        return pltpu.make_async_remote_copy(
            src_ref=src, dst_ref=dst, send_sem=x_send.at[n], recv_sem=x_recv.at[n], device_id=to, device_id_type=MESH
        )

    for_far = send(part_ref.at[far], near.at[1], 1, (blk, core))
    for_core = send(part_ref.at[core], near.at[0], 0, (blk, core))
    for_far.start()
    for_core.start()
    wait_w = spread(0, n_blk, lambda b: w_ref.at[b], w_in.at[blk], w_send, w_recv)
    wait_t = spread(0, n_blk, lambda b: t_ref.at[b], t_in.at[blk], t_send, t_recv)
    loads[0].wait()
    for_far.wait()
    mine[...] = (part_row[...].astype(F32) + near[1].astype(F32)).astype(BF16)
    for_row = send(mine, far_in, 2, (blk, row))
    for_row.start()
    wait_w()
    wait_t()
    loads[1].wait()
    w_sum[...] = w_own[...].astype(F32)
    t_sum[...] = t_ref[blk]

    def add(step, c):
        other = lax.rem(blk + step, n_blk)
        w_sum[...] += w_in[other].astype(F32)
        t_sum[...] += t_in[other]
        return c

    lax.fori_loop(1, n_blk, add, 0)
    wait_w2 = spread(1, n_head, lambda h: w_sum.at[h], w_end.at[head], w_send2, w_recv2)
    wait_t2 = spread(1, n_head, lambda h: t_sum.at[h], t_end.at[head], t_send2, t_recv2)
    w_end[head] = w_sum[head]
    t_end[head] = t_sum[head]
    for_core.wait()
    wait_w2()
    wait_t2()
    dt_ref[...] = jnp.sum(t_end[...], axis=0)
    parts = 3
    cut = dw_ref.shape[1] // (parts * n_head)
    for h in range(n_head):
        for p in range(parts):
            first = (p * n_head + h) * cut
            dw_ref[:, first : first + cut] = w_end[h, :, p * cut : (p + 1) * cut]
    loads[2].wait()
    loads[3].wait()
    for_row.wait()
    out_ref[...] = (
        first_ref[...] + part_own[...].astype(F32) + near[0].astype(F32) + far_in[...].astype(F32)
    ).astype(BF16)


def finish(part, d_first, w, table, n_blk, n_head):
    rows, width = d_first.shape
    _, _, per, wide = w.shape
    return pl.pallas_call(
        functools.partial(finish_body, n_blk, n_head),
        out_shape=(
            jax.ShapeDtypeStruct((rows, width), BF16),
            jax.ShapeDtypeStruct((per, 3 * width), F32),
            jax.ShapeDtypeStruct(table.shape[2:], F32),
        ),
        in_specs=[ANY, ANY, ANY, VMEM],
        out_specs=(VMEM,) * 3,
        scratch_shapes=[
            pltpu.VMEM((rows, width), BF16),
            pltpu.VMEM((rows, width), BF16),
            pltpu.VMEM((rows, width), F32),
            pltpu.VMEM(w.shape[1:], w.dtype),
            pltpu.VMEM((2, rows, width), BF16),
            pltpu.VMEM((rows, width), BF16),
            pltpu.VMEM((rows, width), BF16),
            pltpu.VMEM(w.shape, w.dtype),
            pltpu.VMEM(table.shape, F32),
            pltpu.VMEM(w.shape[1:], F32),
            pltpu.VMEM(table.shape[1:], F32),
            pltpu.VMEM(w.shape[1:], F32),
            pltpu.VMEM(table.shape[1:], F32),
            pltpu.SemaphoreType.DMA((4,)),
            pltpu.SemaphoreType.DMA((3,)),
            pltpu.SemaphoreType.DMA((3,)),
        ]
        + [pltpu.SemaphoreType.DMA((n_blk,))] * 4
        + [pltpu.SemaphoreType.DMA((n_head,))] * 4,
        compiler_params=pltpu.CompilerParams(collective_id=1, has_side_effects=True, vmem_limit_bytes=40 << 20),
        name="finish",
    )(in_hbm(part), in_hbm(d_first), in_hbm(w), table)


def greet(n_blk, n_head):
    blk, head = place()
    barrier = pltpu.get_barrier_semaphore()
    for step in range(1, n_head):
        pl.semaphore_signal(barrier, inc=1, device_id=(blk, lax.rem(head + step, n_head)), device_id_type=MESH)

    @pl.when(blk > 0)
    def _():
        pl.semaphore_signal(barrier, inc=1, device_id=(blk - 1, head), device_id_type=MESH)

    @pl.when(blk < n_blk - 1)
    def _():
        pl.semaphore_signal(barrier, inc=1, device_id=(blk + 1, head), device_id_type=MESH)

    pl.semaphore_wait(barrier, n_head - 1 + jnp.where(blk > 0, 1, 0) + jnp.where(blk < n_blk - 1, 1, 0))


def to_neighbours(n_blk, n_head, src, lo, hi, send_sem, recv_sem):
    blk, head = place()
    cases = (
        (blk > 0, blk < n_blk - 1, hi, (blk - 1, head)),
        (blk < n_blk - 1, blk > 0, lo, (blk + 1, head)),
    )

    def copy(n):
        return pltpu.make_async_remote_copy(
            src_ref=src, dst_ref=cases[n][2], send_sem=send_sem.at[n], recv_sem=recv_sem.at[n], device_id=cases[n][3],
            device_id_type=MESH,
        )

    for n in range(2):

        @pl.when(cases[n][0])
        def _():
            copy(n).start()

    def wait():
        for n in range(2):

            @pl.when(cases[n][0])
            def _():
                copy(n).wait_send()

            @pl.when(cases[n][1])
            def _():
                copy(n).wait_recv()

    return wait


def to_tokens_body(
    n_blk, n_head, out_ref, lse_ref, seq_ref, lse_lo_ref, lse_hi_ref, keep_sem, send_sem, recv_sem, lse_send, lse_recv
):
    blk, head = place()
    greet(n_blk, n_head)

    def part(h):
        return out_ref.at[h]

    def copy(step):
        to = lax.rem(head + step, n_head)
        return pltpu.make_async_remote_copy(
            src_ref=part(to), dst_ref=seq_ref.at[head], send_sem=send_sem.at[step], recv_sem=recv_sem.at[step],
            device_id=(blk, to), device_id_type=MESH,
        )

    for step in range(n_head - 1, 0, -1):
        copy(step).start()
    keep = pltpu.make_async_copy(part(head), seq_ref.at[head], keep_sem)
    keep.start()
    wait = to_neighbours(n_blk, n_head, lse_ref, lse_lo_ref, lse_hi_ref, lse_send, lse_recv)
    for step in range(1, n_head):
        copy(step).wait()
    wait()
    keep.wait()


def to_tokens(out, lse, n_blk, n_head):
    stat = jax.ShapeDtypeStruct(lse.shape, lse.dtype)
    return pl.pallas_call(
        functools.partial(to_tokens_body, n_blk, n_head),
        out_shape=(jax.ShapeDtypeStruct(out.shape, out.dtype), stat, stat),
        in_specs=[ANY, ANY],
        out_specs=(ANY,) * 3,
        scratch_shapes=[
            pltpu.SemaphoreType.DMA,
            pltpu.SemaphoreType.DMA((n_head,)),
            pltpu.SemaphoreType.DMA((n_head,)),
            pltpu.SemaphoreType.DMA((2,)),
            pltpu.SemaphoreType.DMA((2,)),
        ],
        compiler_params=pltpu.CompilerParams(collective_id=2, has_side_effects=True),
        name="to_tokens",
    )(in_hbm(out), in_hbm(lse))


def to_heads_body(
    n_blk, n_head, dseq_ref, dpart_ref, do_ref, delta_ref, delta_lo_ref, delta_hi_ref, keep_sem, send_sem, recv_sem, d_send,
    d_recv, n_send, n_recv
):
    blk, head = place()
    tok = dseq_ref.shape[2]
    greet(n_blk, n_head)
    at = pl.ds(pl.multiple_of(head * tok, tok), tok)

    def copy(step):
        to = lax.rem(head + step, n_head)
        return pltpu.make_async_remote_copy(
            src_ref=dseq_ref.at[to], dst_ref=do_ref.at[:, at], send_sem=send_sem.at[step], recv_sem=recv_sem.at[step],
            device_id=(blk, to), device_id_type=MESH,
        )

    def small_copy(step):
        to = lax.rem(head + step, n_head)
        return pltpu.make_async_remote_copy(
            src_ref=dpart_ref.at[to], dst_ref=delta_ref.at[head], send_sem=d_send.at[step], recv_sem=d_recv.at[step],
            device_id=(blk, to), device_id_type=MESH,
        )

    keep = (
        pltpu.make_async_copy(dseq_ref.at[head], do_ref.at[:, at], keep_sem.at[0]),
        pltpu.make_async_copy(dpart_ref.at[head], delta_ref.at[head], keep_sem.at[1]),
    )
    for step in range(n_head - 1, 0, -1):
        small_copy(step).start()
        copy(step).start()
    for local in keep:
        local.start()
    for step in range(1, n_head):
        small_copy(step).wait()
    keep[1].wait()
    wait = to_neighbours(n_blk, n_head, delta_ref, delta_lo_ref, delta_hi_ref, n_send, n_recv)
    for step in range(1, n_head):
        copy(step).wait()
    keep[0].wait()
    wait()


def to_heads(d_seq, d_part, n_blk, n_head):
    _, cut, tok = d_seq.shape
    stat = jax.ShapeDtypeStruct(d_part.shape, F32)
    return pl.pallas_call(
        functools.partial(to_heads_body, n_blk, n_head),
        out_shape=(jax.ShapeDtypeStruct((cut, n_head * tok), BF16), stat, stat, stat),
        in_specs=[ANY, ANY],
        out_specs=(ANY,) * 4,
        scratch_shapes=[
            pltpu.SemaphoreType.DMA((2,)),
            pltpu.SemaphoreType.DMA((n_head,)),
            pltpu.SemaphoreType.DMA((n_head,)),
            pltpu.SemaphoreType.DMA((n_head,)),
            pltpu.SemaphoreType.DMA((n_head,)),
            pltpu.SemaphoreType.DMA((2,)),
            pltpu.SemaphoreType.DMA((2,)),
        ],
        compiler_params=pltpu.CompilerParams(collective_id=3, has_side_effects=True),
        name="to_heads",
    )(in_hbm(d_seq), in_hbm(d_part))


def regroup(values, outer, inner, unit):
    if unit % 8:
        return values.reshape(-1, outer, inner, unit).transpose(0, 2, 1, 3).reshape(values.shape)
    at = lambda o, i: slice((o * inner + i) * unit, (o * inner + i + 1) * unit)
    return jnp.concatenate([values[:, at(o, i)] for i in range(inner) for o in range(outer)], axis=1)


def pack_body(*refs, count, blocks, n_head):
    (in_ref, mid_ref, down_ref, qkv_ref), vectors, (packed_ref, send_ref) = refs[:4], refs[4:-2], refs[-2:]
    unit, width = mid_ref.shape
    ff = blocks * width
    packed_ref[:, :ff] = regroup(in_ref[...].astype(F32), count, blocks, unit).astype(BF16)
    packed_ref[:, ff : ff + width] = mid_ref[...]
    for n in range(blocks):
        packed_ref[:, ff + width * (n + 1) : ff + width * (n + 2)] = down_ref[n * unit : (n + 1) * unit]

    cut = width // n_head
    vectors = [ref[...].astype(F32) for ref in vectors]
    joined = jnp.concatenate(vectors, axis=1)
    wide = 3 * cut
    pieces = jnp.concatenate([joined, jnp.zeros((1, wide - joined.shape[1]), F32)], axis=1)
    blk, head = place()
    me = blk * n_head + head
    spots = cut // unit

    def in_place(vec):
        return jnp.concatenate([jnp.where(lax.rem(me, spots) == n, vec, 0.0) for n in range(spots)], axis=1)

    placed = jnp.concatenate([in_place(vectors[0]), jnp.zeros((1, cut), F32), in_place(vectors[1])], axis=1)
    weights = qkv_ref[...].astype(F32)
    rest = jnp.zeros((BIAS_ROWS - 2, wide), F32)
    for h in range(n_head):
        columns = jnp.concatenate([weights[:, p * width + h * cut : p * width + (h + 1) * cut] for p in range(3)], axis=1)
        mine = jnp.where(me // spots == h, placed, 0.0)
        send_ref[h] = jnp.concatenate([columns, pieces, mine, rest], axis=0).astype(BF16)


def pack(w_in, w_out, w_down, w_qkv, vectors, count, n_head):
    unit, width = w_out.shape
    blocks = w_down.shape[0] // unit
    cut = width // n_head
    if unit % 8:
        down = w_down.reshape(blocks, unit, width).transpose(1, 0, 2).reshape(unit, -1)
        joined = jnp.concatenate(vectors)
        blk, head = place()
        me = blk * n_head + head
        spots = cut // unit
        zeros = jnp.zeros((cut,), BF16)
        at = lax.rem(me, spots) * unit
        placed = jnp.concatenate(
            [
                lax.dynamic_update_slice_in_dim(zeros, vectors[0], at, 0),
                zeros,
                lax.dynamic_update_slice_in_dim(zeros, vectors[1], at, 0),
            ]
        )
        owner = (jnp.arange(n_head) == me // spots)[:, None]
        rows = jnp.stack(
            [
                jnp.broadcast_to(jnp.pad(joined, (0, 3 * cut - joined.shape[0]))[None], (n_head, 3 * cut)),
                jnp.where(owner, placed[None], jnp.zeros((), BF16)),
            ]
            + [jnp.zeros((n_head, 3 * cut), BF16)] * (BIAS_ROWS - 2),
            axis=1,
        )
        columns = w_qkv.reshape(unit, 3, n_head, cut).transpose(2, 0, 1, 3).reshape(n_head, unit, 3 * cut)
        packed = jnp.concatenate([regroup(w_in, count, blocks, unit), w_out, down], axis=1)
        return packed, jnp.concatenate([columns, rows], axis=1)
    return pl.pallas_call(
        functools.partial(pack_body, count=count, blocks=blocks, n_head=n_head),
        out_shape=(
            jax.ShapeDtypeStruct((unit, 2 * w_in.shape[1] + width), BF16),
            jax.ShapeDtypeStruct((n_head, unit + BIAS_ROWS, 3 * cut), BF16),
        ),
        in_specs=[VMEM] * (4 + len(vectors)),
        out_specs=(VMEM, VMEM),
        name="pack",
    )(w_in, w_out, w_down, w_qkv, *(vec[None] for vec in vectors))


def unpack_body(packed_ref, in_ref, mid_ref, down_ref, *, count, blocks):
    unit, width = mid_ref.shape
    ff = blocks * width
    in_ref[...] = regroup(packed_ref[:, :ff].astype(F32), blocks, count, unit)
    mid_ref[...] = packed_ref[:, ff : ff + width].astype(F32)
    for n in range(blocks):
        down_ref[n * unit : (n + 1) * unit] = packed_ref[:, ff + width * (n + 1) : ff + width * (n + 2)].astype(F32)


def unpack(packed, width, count):
    unit = packed.shape[0]
    blocks = (packed.shape[1] // width - 1) // 2
    ff = blocks * width
    if unit % 8:
        packed = packed.astype(F32)
        down = packed[:, ff + width :].reshape(unit, blocks, width).transpose(1, 0, 2).reshape(-1, width)
        return regroup(packed[:, :ff], blocks, count, unit), packed[:, ff : ff + width], down
    return pl.pallas_call(
        functools.partial(unpack_body, count=count, blocks=blocks),
        out_shape=(
            jax.ShapeDtypeStruct((unit, ff), F32),
            jax.ShapeDtypeStruct((unit, width), F32),
            jax.ShapeDtypeStruct((unit * blocks, width), F32),
        ),
        in_specs=[VMEM],
        out_specs=(VMEM,) * 3,
        name="unpack",
    )(packed)


def normalize(values):
    centre = jnp.mean(values, axis=-1, keepdims=True)
    centered = values - centre
    r = lax.rsqrt(jnp.mean(centered * centered, axis=-1, keepdims=True) + 1e-05)
    return centered * r, r


def normalize_back(d_values, unit, r, gain):
    scaled = d_values * gain
    return r * (
        scaled - jnp.mean(scaled, axis=-1, keepdims=True) - unit * jnp.mean(scaled * unit, axis=-1, keepdims=True)
    )


def over_rows(values):
    return jnp.sum(values, axis=0, keepdims=True)


def dense_body(
    x_ref, seq_ref, cot_ref, vec_ref, inb_ref, w_hbm, out_ref, first_ref, dseq_ref, delta_ref, dvec_ref, dinb_ref, grad_hbm, bias_ref, dbias_ref, w, grad,
    unit_ref, r_ref, normed_ref, low_ref, acc_ref, slope_ref, act_ref, e_ref, w_sem, grad_sem, *, blocks, count
):
    width = x_ref.shape[1]
    out_at, down_at = blocks * width, (blocks + 1) * width

    def fetch(first, size, n):
        at = pl.ds(first, size)
        copy = pltpu.make_async_copy(w_hbm.at[:, at], w.at[:, at], w_sem.at[n])
        copy.start()
        return copy

    def cols(first, c):
        return pl.ds(pl.multiple_of(first + c * width, 128), width)

    def put(first, c, n):
        at = cols(first, c)
        return pltpu.make_async_copy(grad.at[:, at], grad_hbm.at[:, at], grad_sem.at[n])

    piece = width // count
    bias_ref[...] = inb_ref[...] if piece % 8 else regroup(inb_ref[...], count, blocks, piece)
    w_out_here = fetch(out_at, width, 0)
    w_in_here = fetch(0, out_at, 1)
    w_down_here = fetch(down_at, blocks * width, 2)
    out_bias, ln1_gain, ln1_bias, down_bias, ln2_gain, ln2_bias = (vec_ref[n : n + 1] for n in range(6))
    w_out_here.wait()
    unit, r = normalize(x_ref[...].astype(F32) + mm_tn(seq_ref[...], w[:, out_at:down_at]) + out_bias)
    unit_ref[...] = unit
    r_ref[...] = r
    normed = unit * ln1_gain + ln1_bias
    normed_ref[...] = normed
    low_ref[...] = normed.astype(BF16)
    acc_ref[...] = normed + down_bias
    w_in_here.wait()
    w_down_here.wait()

    def up_down(c, carry):
        at = cols(0, c)
        hidden = mm(low_ref[...], w[:, at]) + bias_ref[:, at]
        phi = 0.5 + 0.5 * lax.erf(hidden * (2.0**-0.5))
        act = (hidden * phi).astype(BF16)
        act_ref[:, at] = act
        slope_ref[:, at] = phi + hidden * (jnp.exp(-0.5 * hidden * hidden) * ((2.0 * math.pi) ** -0.5))
        acc_ref[...] += mm(act, w[:, cols(down_at, c)])
        return carry

    lax.fori_loop(0, blocks, up_down, 0, unroll=2)
    unit2, r2 = normalize(acc_ref[...])
    out_ref[...] = (unit2 * ln2_gain + ln2_bias).astype(BF16)
    dy = cot_ref[...].astype(F32)
    dvec_ref[4:5] = over_rows(dy * unit2)
    dvec_ref[5:6] = over_rows(dy)
    d_second = normalize_back(dy, unit2, r2, ln2_gain)
    e_ref[...] = d_second.astype(BF16)
    dvec_ref[3:4] = over_rows(e_ref[...].astype(F32))
    acc_ref[...] = d_second

    def back(c, carry):
        at, down = cols(0, c), cols(down_at, c)
        e = e_ref[...]
        d_hidden = (mm_nt(e, w[:, down]) * slope_ref[:, at]).astype(BF16)
        dbias_ref[:, at] = over_rows(d_hidden.astype(F32))
        acc_ref[...] += mm_nt(d_hidden, w[:, at])
        grad[:, at] = mm_tn(low_ref[...], d_hidden).astype(BF16)
        put(0, c, c).start()
        grad[:, down] = mm_tn(act_ref[:, at], e).astype(BF16)
        put(down_at, c, blocks + c).start()
        return carry

    lax.fori_loop(0, blocks, back, 0, unroll=2)
    d_normed = acc_ref[...]
    unit = unit_ref[...]
    dvec_ref[1:2] = over_rows(d_normed * unit)
    dvec_ref[2:3] = over_rows(d_normed)
    d_first = normalize_back(d_normed, unit, r_ref[...], ln1_gain)
    first_ref[...] = d_first
    e_first = d_first.astype(BF16)
    dvec_ref[0:1] = over_rows(e_first.astype(F32))
    grad[:, out_at:down_at] = mm(seq_ref[...], e_first).astype(BF16)
    put(out_at, 0, 2 * blocks).start()
    d_seq = mm_nt(w[:, out_at:down_at], e_first).astype(BF16)
    dseq_ref[...] = d_seq
    product = d_seq.astype(F32) * seq_ref[...].astype(F32)
    n_head, groups, _ = delta_ref.shape
    for n in range(n_head):
        for g in range(groups):
            first = (n * groups + g) * HEAD_DIM
            delta_ref[n, g : g + 1] = over_rows(product[first : first + HEAD_DIM])

    dinb_ref[...] = dbias_ref[...] if piece % 8 else regroup(dbias_ref[...], blocks, count, piece)

    def done(c, carry):
        put(0, c, c).wait()
        put(down_at, c, blocks + c).wait()
        return carry

    lax.fori_loop(0, blocks, done, 0)
    put(out_at, 0, 2 * blocks).wait()


def dense(x, seq_t, cotangent, vectors, in_bias, weights, blocks, n_head, count):
    tok, width = x.shape
    ff = blocks * width
    return pl.pallas_call(
        functools.partial(dense_body, blocks=blocks, count=count),
        out_shape=(
            jax.ShapeDtypeStruct((tok, width), BF16),
            jax.ShapeDtypeStruct((tok, width), F32),
            jax.ShapeDtypeStruct((width, tok), BF16),
            jax.ShapeDtypeStruct((n_head, width // n_head // HEAD_DIM, tok), F32),
            jax.ShapeDtypeStruct((8, width), F32),
            jax.ShapeDtypeStruct((1, ff), F32),
            jax.ShapeDtypeStruct(weights.shape, BF16),
        ),
        in_specs=[VMEM] * 5 + [ANY],
        out_specs=(VMEM,) * 6 + (ANY,),
        scratch_shapes=[
            pltpu.VMEM((1, ff), F32),
            pltpu.VMEM((1, ff), F32),
            pltpu.VMEM(weights.shape, BF16),
            pltpu.VMEM(weights.shape, BF16),
            pltpu.VMEM((tok, width), F32),
            pltpu.VMEM((tok, 1), F32),
            pltpu.VMEM((tok, width), F32),
            pltpu.VMEM((tok, width), BF16),
            pltpu.VMEM((tok, width), F32),
            pltpu.VMEM((tok, ff), F32),
            pltpu.VMEM((tok, ff), BF16),
            pltpu.VMEM((tok, width), BF16),
            pltpu.SemaphoreType.DMA((3,)),
            pltpu.SemaphoreType.DMA((2 * blocks + 1,)),
        ],
        compiler_params=pltpu.CompilerParams(vmem_limit_bytes=58 << 20),
        cost_estimate=pl.CostEstimate(flops=17_000_000_000, bytes_accessed=30_000_000, transcendentals=3_000_000),
        name="dense",
    )(x, seq_t, cotangent, vectors, in_bias, weights)


def window_of(segments, blk, rows, tile):
    padded = jnp.concatenate(
        [jnp.full((rows,), -1, jnp.int32), segments, jnp.full((rows,), 1 << 30, jnp.int32)]
    )
    seg = lax.dynamic_slice_in_dim(padded, blk * rows, 3 * rows, 0)
    own = seg[rows : 2 * rows]
    below = jnp.sum((seg[None, :] < own[::tile][:, None]).astype(jnp.int32), axis=1)
    upto = jnp.sum((seg[None, :] <= own[tile - 1 :: tile][:, None]).astype(jnp.int32), axis=1)
    return seg[None], below // tile, (upto - 1) // tile + 1


def shift(value, steps):
    count = lax.axis_size("blk")
    first, last = max(0, -steps), min(count, count - steps)
    return lax.ppermute(value, "blk", [(source, source + steps) for source in range(first, last)])


def body(
    inputs, segments, cotangent, w_qkv, q_bias, v_bias, w_out, out_bias, ln1_gain, ln1_bias, w_in, in_bias, w_down,
    down_bias, ln2_gain, ln2_bias
):
    n_blk, n_head = lax.axis_size("blk"), lax.axis_size("head")
    count = n_blk * n_head
    blk, head = place()
    tok, width = inputs.shape
    rows = tok * n_head
    per = w_qkv.shape[0]
    ff = w_in.shape[1]
    blocks = ff // width
    cut = width // n_head
    groups = cut // HEAD_DIM

    small = (q_bias, v_bias, out_bias, ln1_gain, ln1_bias, down_bias, ln2_gain, ln2_bias, in_bias)
    packed, to_send = pack(w_in, w_out, w_down, w_qkv, small, count, n_head)
    whole = lax.all_gather(packed, BOTH, axis=0, tiled=True)

    x_win, got, own_qkv, turned, qkv_bias, vectors, hidden_bias = collect(inputs, to_send, ff, n_blk, n_head)
    x_win = x_win.reshape(3 * rows, width)
    offsets = [0]
    for vec in small:
        offsets.append(offsets[-1] + vec.shape[0])
    if per % 8:
        got = got.reshape(count, *got.shape[2:])
        all_small = got[:, per, : offsets[-1]].astype(F32)
        full = [all_small[:, a:b].reshape(-1) for a, b in zip(offsets[:-1], offsets[1:])]
        vectors = jnp.stack(full[2:8] + full[2:4])
        hidden_bias = regroup(full[8][None], count, blocks, per)
    seg, lo, hi = window_of(segments, blk, rows, tok)
    attended, lse, qkv = attend(x_win, own_qkv, turned, qkv_bias, seg, lo, hi, groups, rows, tok)
    seq_t, lse_lo, lse_hi = to_tokens(attended, lse, n_blk, n_head)
    seq_t = seq_t.reshape(width, tok)

    outputs, d_first, d_seq_t, d_part, d_vectors, d_in_bias, grads = dense(
        inputs, seq_t, cotangent, vectors, hidden_bias, whole, blocks, n_head, count
    )
    d_out_bias, d_ln1_gain, d_ln1_bias, d_down_bias, d_ln2_gain, d_ln2_bias = (d_vectors[n] for n in range(6))
    if per % 8:
        d_in_bias = regroup(d_in_bias, blocks, count, per)
    d_in_bias = d_in_bias[0]
    d_out, delta, delta_lo, delta_hi = to_heads(d_seq_t.reshape(n_head, cut, tok), d_part, n_blk, n_head)
    delta, delta_lo, delta_hi = (a.transpose(1, 0, 2).reshape(groups, rows) for a in (delta, delta_lo, delta_hi))

    owned = lax.psum_scatter(grads, BOTH, scatter_dimension=0, tiled=True)

    do_lo, do_hi = shift(d_out, 1), shift(d_out, -1)
    dq, dk, dv = own_grads(qkv, d_out, lse, delta, seg, lo, hi, groups, rows, tok)
    d_w_qkv, d_part, d_biases = outer_grads(
        qkv, do_lo, do_hi, lse_lo, lse_hi, delta_lo, delta_hi, seg, dq, dk, dv, turned, x_win, lo, hi, groups, rows, tok
    )
    d_biases = d_biases[:, 0]
    place_own = lambda vec: lax.dynamic_update_slice_in_dim(jnp.zeros((width,), F32), vec, head * cut, 0)
    vectors = (
        place_own(d_biases[:cut]), place_own(d_biases[2 * cut :]), d_out_bias, d_ln1_gain, d_ln1_bias, d_down_bias, d_ln2_gain,
        d_ln2_bias, d_in_bias,
    )
    table = jnp.concatenate([vec.reshape(count, -1) for vec in vectors], axis=1)
    lanes = 128
    table_rows = -(-table.shape[1] // (8 * lanes)) * 8
    table = jnp.pad(table, ((0, 0), (0, table_rows * lanes - table.shape[1])))
    d_inputs, own_w_qkv, sums = finish(
        d_part.reshape(n_head, tok, width), d_first, d_w_qkv.reshape(n_blk, n_head, per, 3 * cut),
        table.reshape(n_blk, n_head, table_rows, lanes), n_blk, n_head,
    )
    sums = sums.reshape(-1)
    (o_q_bias, o_v_bias, o_out_bias, o_ln1_gain, o_ln1_bias, o_down_bias, o_ln2_gain, o_ln2_bias, o_in_bias) = (
        sums[a:b] for a, b in zip(offsets[:-1], offsets[1:])
    )
    own_w_in, own_w_out, own_w_down = unpack(owned, width, count)
    return (
        outputs, d_inputs, own_w_qkv, o_q_bias, o_v_bias, own_w_out, o_out_bias, o_ln1_gain, o_ln1_bias,
        own_w_in, o_in_bias, own_w_down, o_down_bias, o_ln2_gain, o_ln2_bias,
    )


def solution(mesh):
    rows, vec = P(BOTH, None), P(BOTH)
    placed = (rows, P(), rows, rows, vec, vec, rows, vec, vec, vec, rows, vec, rows, vec, vec, vec)
    return jax.shard_map(
        body,
        mesh=mesh,
        in_specs=placed,
        out_specs=(rows, rows, rows, vec, vec, rows, vec, vec, vec, rows, vec, rows, vec, vec, vec),
        check_vma=False,
    )
```

```python
import functools
import math

import jax
import jax.numpy as jnp
from jax import lax
from jax.experimental import pallas as pl
from jax.experimental.pallas import tpu as pltpu
from jax.sharding import PartitionSpec as P

HEAD_DIM = 64
F32, BF16 = jnp.float32, jnp.bfloat16
NEG = -1e30
MILD = 60.0
SCALE = HEAD_DIM**-0.5
MESH = pl.DeviceIdType.MESH
BOTH = ("blk", "head")
BIAS_ROWS = 8

VMEM = pl.BlockSpec(memory_space=pltpu.VMEM)
SMEM = pl.BlockSpec(memory_space=pltpu.SMEM)
ANY = pl.BlockSpec(memory_space=pl.ANY)


def in_hbm(array):
    return pltpu.with_memory_space_constraint(array, pltpu.HBM)


def mm(a, b):
    return jnp.dot(a, b, preferred_element_type=F32)


def mm_tn(a, b):
    return lax.dot_general(a, b, (((0,), (0,)), ((), ())), preferred_element_type=F32)


def mm_nt(a, b):
    return lax.dot_general(a, b, (((1,), (1,)), ((), ())), preferred_element_type=F32)


def feature_rows(n):
    return slice(n * HEAD_DIM, (n + 1) * HEAD_DIM)


def column(row):
    return jnp.broadcast_to(row, (8, row.shape[1])).T[:, :1]


def same_document(seg_ref, keys, queries):
    return column(seg_ref[:, keys]) == seg_ref[:, queries]


def attend_body(
    lo_ref, hi_ref, seg_ref, bias_ref, turned_hbm, own_hbm, x_hbm, out_hbm, lse_hbm, qkv_hbm, qkv_ref, x_buf, out_ref, lse_ref,
    turned_ref, x_sem, own_sem, out_sem, result_sem, *, groups, rows, tile
):
    count = rows // tile
    own = pl.ds(rows, rows)
    load_turned = pltpu.make_async_copy(turned_hbm, turned_ref, own_sem.at[0])
    load_own = pltpu.make_async_copy(own_hbm, qkv_ref.at[:, own], own_sem.at[1])
    keep_own = pltpu.make_async_copy(qkv_ref.at[:, own], qkv_hbm.at[:, own], own_sem.at[2])

    before = count - jnp.minimum(lo_ref[0], count)
    tiles = before + jnp.maximum(hi_ref[count - 1] - 2 * count, 0)

    def span(t):
        j = jnp.where(t < before, count - before + t, 2 * count + t - before)
        return pl.ds(pl.multiple_of(j * tile, tile), tile)

    def fetch(t):
        slot = lax.rem(t, 2)
        return pltpu.make_async_copy(x_hbm.at[span(t)], x_buf.at[slot], x_sem.at[slot])

    def keep(t):
        return pltpu.make_async_copy(qkv_ref.at[:, span(t)], qkv_hbm.at[:, span(t)], out_sem.at[t])

    load_turned.start()

    @pl.when(tiles > 0)
    def _():
        fetch(0).start()

    load_own.start()
    load_turned.wait()

    def project(t, c):
        @pl.when(t + 1 < tiles)
        def _():
            fetch(t + 1).start()

        fetch(t).wait()
        qkv_ref[:, span(t)] = (mm_nt(turned_ref[...], x_buf[lax.rem(t, 2)]) + bias_ref[...]).astype(BF16)
        keep(t).start()
        return c

    lax.fori_loop(0, tiles, project, 0)
    load_own.wait()
    keep_own.start()

    def put_out(i):
        return pltpu.make_async_copy(out_ref.at[i], out_hbm.at[i], result_sem.at[i])

    def one_query(i, mild):
        at = pl.ds(pl.multiple_of(i * tile, tile), tile)
        win = pl.ds(pl.multiple_of(rows + i * tile, tile), tile)
        queries = [qkv_ref[feature_rows(h), win] * BF16(SCALE) for h in range(groups)]

        def meet(tiles, state):
            keys = [pl.ds(pl.multiple_of(j * tile, tile), tile) for j in tiles]
            same = [same_document(seg_ref, at, win) for at in keys]
            steps = [(n, h) for n in range(len(tiles)) for h in range(groups)]

            def product(n, h):
                return mm_tn(qkv_ref[feature_rows(groups + h), keys[n]], queries[h])

            state = list(state)
            ahead = product(*steps[0])
            for at, (n, h) in enumerate(steps):
                scores = jnp.where(same[n], ahead, NEG)
                if at + 1 < len(steps):
                    ahead = product(*steps[at + 1])
                value = qkv_ref[feature_rows(2 * groups + h), keys[n]]
                top, total, acc = state[h]
                if mild:
                    weights = jnp.exp(scores)
                else:
                    peak = jnp.maximum(top, jnp.max(scores, axis=0, keepdims=True))
                    weights = jnp.exp(scores - peak)
                    fade = jnp.exp(top - peak)
                    total, acc, top = total * fade, acc * fade, peak
                total = total + jnp.sum(weights, axis=0, keepdims=True)
                state[h] = (top, total, acc + mm(value, weights.astype(BF16)))
            return tuple(state)

        zero = tuple(
            (jnp.full((1, tile), 0.0 if mild else NEG, F32), jnp.zeros((1, tile), F32), jnp.zeros((HEAD_DIM, tile), F32))
            for _ in range(groups)
        )
        lo, hi = lo_ref[i], hi_ref[i]
        start = lo
        state = zero
        if mild:
            pairs = (hi - lo) // 2
            state = lax.fori_loop(0, pairs, lambda t, c: meet([lo + 2 * t, lo + 2 * t + 1], c), state)
            start = lo + 2 * pairs
        state = lax.fori_loop(start, hi, lambda j, c: meet([j], c), state)
        for h in range(groups):
            top, total, acc = state[h]
            out_ref[i, h * HEAD_DIM : (h + 1) * HEAD_DIM, :] = (acc / total).astype(BF16)
            lse_ref[h : h + 1, at] = top + jnp.log(total)
        put_out(i).start()

    def longest(part, first, last):
        def grow(j, best):
            at = pl.ds(pl.multiple_of(j * tile, tile), tile)
            for h in range(groups):
                values = qkv_ref[feature_rows(part * groups + h), at].astype(F32)
                best = jnp.maximum(best, jnp.sum(values * values, axis=0, keepdims=True))
            return best

        return jnp.max(lax.fori_loop(first, last, grow, jnp.zeros((1, tile), F32)))

    reach = longest(0, count, 2 * count) * longest(1, lo_ref[0], hi_ref[count - 1])
    is_mild = reach <= (MILD / SCALE) ** 2
    for mild in (True, False):

        @pl.when(is_mild == mild)
        def _():
            @pl.loop(0, count)
            def _(i):
                one_query(i, mild)

    put_lse = pltpu.make_async_copy(lse_ref, lse_hbm, result_sem.at[count])
    put_lse.start()
    for i in range(count):
        put_out(i).wait()
    put_lse.wait()
    keep_own.wait()

    def done(t, c):
        keep(t).wait()
        return c

    lax.fori_loop(0, tiles, done, 0)


def attend(x_win, own, turned, bias, seg, lo, hi, groups, rows, tile):
    wide, width = turned.shape
    return pl.pallas_call(
        functools.partial(attend_body, groups=groups, rows=rows, tile=tile),
        out_shape=(
            pltpu.HBM((rows // tile, groups * HEAD_DIM, tile), BF16),
            pltpu.HBM((groups, rows), F32),
            pltpu.HBM((wide, 3 * rows), BF16),
        ),
        in_specs=[SMEM, SMEM, VMEM, VMEM, ANY, ANY, ANY],
        out_specs=(ANY,) * 3,
        scratch_shapes=[
            pltpu.VMEM((wide, 3 * rows), BF16),
            pltpu.VMEM((2, tile, width), BF16),
            pltpu.VMEM((rows // tile, groups * HEAD_DIM, tile), BF16),
            pltpu.VMEM((groups, rows), F32),
            pltpu.VMEM((wide, width), BF16),
            pltpu.SemaphoreType.DMA((2,)),
            pltpu.SemaphoreType.DMA((3,)),
            pltpu.SemaphoreType.DMA((2 * rows // tile,)),
            pltpu.SemaphoreType.DMA((rows // tile + 1,)),
        ],
        compiler_params=pltpu.CompilerParams(vmem_limit_bytes=32 << 20),
        cost_estimate=pl.CostEstimate(flops=36_000_000_000, bytes_accessed=24_000_000, transcendentals=15_000_000),
        name="attend",
    )(lo, hi, seg, bias, in_hbm(turned), in_hbm(own), in_hbm(x_win))


def own_grads_body(
    lo_ref, hi_ref, qkv_hbm, do_hbm, lse_ref, delta_ref, seg_ref, dq_hbm, dk_hbm, dv_hbm, qkv_ref, do_ref, dq_ref, dk_ref, dv_ref,
    acc_ref, in_sem, dq_sem, out_sem, *, groups, rows, tile
):
    count = rows // tile
    q_rows, kv_rows = pl.ds(0, groups * HEAD_DIM), pl.ds(groups * HEAD_DIM, 2 * groups * HEAD_DIM)
    before, own, after = (pl.ds(n * rows, rows) for n in range(3))

    def load(features, tokens, n):
        copy = pltpu.make_async_copy(qkv_hbm.at[features, tokens], qkv_ref.at[features, tokens], in_sem.at[n])
        copy.start()
        return copy

    first = [load(kv_rows, own, 0), load(q_rows, own, 1), pltpu.make_async_copy(do_hbm, do_ref, in_sem.at[2])]
    first[2].start()
    later = [load(kv_rows, before, 3), load(kv_rows, after, 4)]
    acc_ref[...] = jnp.zeros_like(acc_ref)
    for copy in first:
        copy.wait()

    def tokens(n):
        return pl.ds(pl.multiple_of(n * tile, tile), tile)

    def put_dq(i):
        return pltpu.make_async_copy(dq_ref.at[:, :, tokens(i)], dq_hbm.at[:, :, tokens(i)], dq_sem.at[i])

    def put_sums(j):
        return (
            pltpu.make_async_copy(dk_ref.at[:, tokens(j)], dk_hbm.at[:, tokens(j)], out_sem.at[0, j]),
            pltpu.make_async_copy(dv_ref.at[:, tokens(j)], dv_hbm.at[:, tokens(j)], out_sem.at[1, j]),
        )

    def pair(i, j, mine):
        at, win, keys = tokens(i), tokens(count + i), tokens(j)
        same = same_document(seg_ref, keys, win)

        def products(h):
            query = qkv_ref[feature_rows(h), win] * BF16(SCALE)
            return (
                query,
                mm_tn(qkv_ref[feature_rows(groups + h), keys], query),
                mm_tn(qkv_ref[feature_rows(2 * groups + h), keys], do_ref[feature_rows(h), at]),
            )

        ahead = products(0)
        for h in range(groups):
            query, scores, d_weights = ahead
            if h + 1 < groups:
                ahead = products(h + 1)
            weights = jnp.exp(jnp.where(same, scores - lse_ref[h : h + 1, at], NEG))
            d_scores = (weights * (d_weights - delta_ref[h : h + 1, at])).astype(BF16)
            acc_ref[h, :, at] += mm(qkv_ref[feature_rows(groups + h), keys], d_scores)
            if mine is not None:
                dv_ref[h, tokens(mine), :] += mm_nt(weights.astype(BF16), do_ref[feature_rows(h), at])
                dk_ref[h, tokens(mine), :] += mm_nt(d_scores, query)

    def one_key(j, _):
        dk_ref[:, tokens(j), :] = jnp.zeros((groups, tile, HEAD_DIM), F32)
        dv_ref[:, tokens(j), :] = jnp.zeros((groups, tile, HEAD_DIM), F32)

        def inside(i, c):
            pair(i - count, count + j, j)
            return c

        lax.fori_loop(jnp.maximum(lo_ref[j], count), jnp.minimum(hi_ref[j], 2 * count), inside, 0)
        for copy in put_sums(j):
            copy.start()
        return 0

    lax.fori_loop(0, count, one_key, 0)
    for copy in later:
        copy.wait()

    def one_query(i, _):
        low = count - jnp.minimum(lo_ref[i], count)
        high = jnp.maximum(hi_ref[i] - 2 * count, 0)

        def outside(t, c):
            pair(i, jnp.where(t < low, count - low + t, 2 * count + t - low), None)
            return c

        lax.fori_loop(0, low + high, outside, 0)
        dq_ref[:, :, tokens(i)] = (acc_ref[:, :, tokens(i)] * SCALE).astype(BF16)
        put_dq(i).start()
        return 0

    lax.fori_loop(0, count, one_query, 0)
    for n in range(count):
        put_dq(n).wait()
        for copy in put_sums(n):
            copy.wait()


def own_grads(qkv, d_out, lse, delta, seg, lo, hi, groups, rows, tile):
    return pl.pallas_call(
        functools.partial(own_grads_body, groups=groups, rows=rows, tile=tile),
        out_shape=(
            pltpu.HBM((groups, HEAD_DIM, rows), BF16),
            pltpu.HBM((groups, rows, HEAD_DIM), F32),
            pltpu.HBM((groups, rows, HEAD_DIM), F32),
        ),
        in_specs=[SMEM, SMEM, ANY, ANY, VMEM, VMEM, VMEM],
        out_specs=(ANY,) * 3,
        scratch_shapes=[
            pltpu.VMEM(qkv.shape, BF16),
            pltpu.VMEM(d_out.shape, BF16),
            pltpu.VMEM((groups, HEAD_DIM, rows), BF16),
            pltpu.VMEM((groups, rows, HEAD_DIM), F32),
            pltpu.VMEM((groups, rows, HEAD_DIM), F32),
            pltpu.VMEM((groups, HEAD_DIM, rows), F32),
            pltpu.SemaphoreType.DMA((5,)),
            pltpu.SemaphoreType.DMA((rows // tile,)),
            pltpu.SemaphoreType.DMA((2, rows // tile)),
        ],
        compiler_params=pltpu.CompilerParams(vmem_limit_bytes=36 << 20),
        cost_estimate=pl.CostEstimate(flops=60_000_000_000, bytes_accessed=20_000_000, transcendentals=15_000_000),
        name="own_grads",
    )(lo, hi, in_hbm(qkv), in_hbm(d_out), lse, delta, seg)


def outer_grads_body(
    lo_ref, hi_ref, qkv_hbm, do_lo_ref, do_hi_ref, lse_lo_ref, lse_hi_ref, delta_lo_ref, delta_hi_ref, seg_ref, dq_hbm, dk_hbm,
    dv_hbm, turned_hbm, x_hbm, dw_hbm, part_hbm, sum_ref, qkv_ref, out_ref, dk_acc, dv_acc, dw_acc, x_buf,
    turned_ref, dw_ref, part_ref, in_sem, tile_sem, out_sem, *, groups, rows, tile
):
    count = rows // tile
    features = groups * HEAD_DIM
    q_rows, kv_rows = pl.ds(0, features), pl.ds(features, 2 * features)
    before, own, after = (pl.ds(n * rows, rows) for n in range(3))

    def load(src, dst, sem):
        copy = pltpu.make_async_copy(src, dst, sem)
        copy.start()
        return copy

    def sums(j):
        at = pl.ds(pl.multiple_of(j * tile, tile), tile)
        return (
            pltpu.make_async_copy(dk_hbm.at[:, at], dk_acc.at[:, at], tile_sem.at[0, j]),
            pltpu.make_async_copy(dv_hbm.at[:, at], dv_acc.at[:, at], tile_sem.at[1, j]),
        )

    first = [
        load(qkv_hbm.at[kv_rows, own], qkv_ref.at[kv_rows, own], in_sem.at[0]),
        load(qkv_hbm.at[q_rows, before], qkv_ref.at[q_rows, before], in_sem.at[1]),
        load(qkv_hbm.at[q_rows, after], qkv_ref.at[q_rows, after], in_sem.at[2]),
    ]
    for j in range(count):
        for copy in sums(j):
            copy.start()
    later = [load(turned_hbm, turned_ref, in_sem.at[3]), load(x_hbm.at[own], x_buf, in_sem.at[4])]
    later += [load(dq_hbm.at[h], out_ref.at[feature_rows(h)], in_sem.at[5 + h]) for h in range(groups)]
    for copy in first:
        copy.wait()

    def one_key(j, _):
        mine = pl.ds(pl.multiple_of(j * tile, tile), tile)
        keys = pl.ds(pl.multiple_of(rows + j * tile, tile), tile)
        for copy in sums(j):
            copy.wait()

        def pair(i, base, do_ref, lse_ref, delta_ref):
            at = pl.ds(pl.multiple_of((i - base) * tile, tile), tile)
            win = pl.ds(pl.multiple_of(i * tile, tile), tile)
            same = same_document(seg_ref, keys, win)

            def products(h):
                query = qkv_ref[feature_rows(h), win] * BF16(SCALE)
                return query, mm_tn(qkv_ref[feature_rows(groups + h), keys], query), mm_tn(qkv_ref[feature_rows(2 * groups + h), keys], do_ref[feature_rows(h), at])

            ahead = products(0)
            for h in range(groups):
                query, scores, d_weights = ahead
                if h + 1 < groups:
                    ahead = products(h + 1)
                weights = jnp.exp(jnp.where(same, scores - lse_ref[h : h + 1, at], NEG))
                d_scores = (weights * (d_weights - delta_ref[h : h + 1, at])).astype(BF16)
                dv_acc[h, mine, :] += mm_nt(weights.astype(BF16), do_ref[feature_rows(h), at])
                dk_acc[h, mine, :] += mm_nt(d_scores, query)

        def before(i, c):
            pair(i, 0, do_lo_ref, lse_lo_ref, delta_lo_ref)
            return c

        def after(i, c):
            pair(i, 2 * count, do_hi_ref, lse_hi_ref, delta_hi_ref)
            return c

        lo, hi = lo_ref[j], hi_ref[j]
        lax.fori_loop(lo, jnp.minimum(hi, count), before, 0)
        lax.fori_loop(jnp.maximum(lo, 2 * count), hi, after, 0)
        for h in range(groups):
            out_ref[feature_rows(groups + h), mine] = dk_acc[h, mine, :].T.astype(BF16)
            out_ref[feature_rows(2 * groups + h), mine] = dv_acc[h, mine, :].T.astype(BF16)
        return 0

    lax.fori_loop(0, count, one_key, 0)
    for copy in later:
        copy.wait()
    dw_acc[...] = jnp.zeros_like(dw_acc)
    sum_ref[...] = jnp.zeros_like(sum_ref)

    def put_part(j):
        at = pl.ds(pl.multiple_of(j * tile, tile), tile)
        return pltpu.make_async_copy(part_ref.at[at], part_hbm.at[at], out_sem.at[j])

    def back(j, _):
        mine = pl.ds(pl.multiple_of(j * tile, tile), tile)
        d = out_ref[:, mine]
        part_ref[mine, :] = mm_tn(d, turned_ref[...]).astype(BF16)
        put_part(j).start()
        dw_acc[...] += mm(d, x_buf[mine, :])
        sum_ref[...] += jnp.sum(d.astype(F32), axis=1, keepdims=True)
        return 0

    lax.fori_loop(0, count, back, 0)
    dw_ref[...] = dw_acc[...].T.astype(BF16)
    load(dw_ref, dw_hbm, out_sem.at[count]).wait()
    for j in range(count):
        put_part(j).wait()


def outer_grads(
    qkv, do_lo, do_hi, lse_lo, lse_hi, delta_lo, delta_hi, seg, dq, dk, dv, turned, x_win, lo, hi, groups, rows, tile
):
    wide, width = turned.shape
    return pl.pallas_call(
        functools.partial(outer_grads_body, groups=groups, rows=rows, tile=tile),
        out_shape=(
            pltpu.HBM((width, wide), BF16),
            pltpu.HBM((rows, width), BF16),
            jax.ShapeDtypeStruct((wide, 1), F32),
        ),
        in_specs=[SMEM, SMEM, ANY] + [VMEM] * 7 + [ANY] * 5,
        out_specs=(ANY, ANY, VMEM),
        scratch_shapes=[
            pltpu.VMEM(qkv.shape, BF16),
            pltpu.VMEM((wide, rows), BF16),
            pltpu.VMEM((groups, rows, HEAD_DIM), F32),
            pltpu.VMEM((groups, rows, HEAD_DIM), F32),
            pltpu.VMEM((wide, width), F32),
            pltpu.VMEM((rows, width), BF16),
            pltpu.VMEM((wide, width), BF16),
            pltpu.VMEM((width, wide), BF16),
            pltpu.VMEM((rows, width), BF16),
            pltpu.SemaphoreType.DMA((5 + groups,)),
            pltpu.SemaphoreType.DMA((2, rows // tile)),
            pltpu.SemaphoreType.DMA((rows // tile + 1,)),
        ],
        compiler_params=pltpu.CompilerParams(vmem_limit_bytes=44 << 20),
        cost_estimate=pl.CostEstimate(flops=24_000_000_000, bytes_accessed=24_000_000, transcendentals=5_000_000),
        name="outer_grads",
    )(lo, hi, in_hbm(qkv), do_lo, do_hi, lse_lo, lse_hi, delta_lo, delta_hi, seg, in_hbm(dq), in_hbm(dk), in_hbm(dv), in_hbm(turned), in_hbm(x_win))


def place():
    return lax.axis_index("blk"), lax.axis_index("head")


def greet_cross(n_blk, n_head):
    blk, head = place()
    barrier = pltpu.get_barrier_semaphore()

    def say_head(step, c):
        to = lax.rem(head + step, n_head)
        pl.semaphore_signal(barrier, inc=1, device_id=(blk, to), device_id_type=MESH)
        return c

    def say_blk(step, c):
        to = lax.rem(blk + step, n_blk)
        pl.semaphore_signal(barrier, inc=1, device_id=(to, head), device_id_type=MESH)
        return c

    lax.fori_loop(1, n_head, say_head, 0)
    lax.fori_loop(1, n_blk, say_blk, 0)
    pl.semaphore_wait(barrier, n_blk + n_head - 2)


def spread(axis, count, src_of, dst, send_sems, recv_sems):
    blk, head = place()
    me = blk if axis == 0 else head

    def copy(step):
        to = lax.rem(me + step, count)
        return pltpu.make_async_remote_copy(
            src_ref=src_of(to),
            dst_ref=dst,
            send_sem=send_sems.at[step],
            recv_sem=recv_sems.at[step],
            device_id=(to, head) if axis == 0 else (blk, to),
            device_id_type=MESH,
        )

    def begin(step, c):
        copy(step).start()
        return c

    def end(step, c):
        copy(step).wait()
        return c

    lax.fori_loop(1, count, begin, 0)
    return lambda: lax.fori_loop(1, count, end, 0)


def collect_body(
    n_blk, n_head, chunks, x_ref, w_ref, xw_ref, wr_ref, qkv_hbm, turned_hbm, bias_ref, vec_ref, inb_ref, x_own, got_ref, w_full, turned_ref, qkv_ref,
    local_sem, near_send, near_recv, w_send, w_recv, x_send, x_recv
):
    blk, head = place()
    rows = x_ref.shape[0] // chunks
    core, row, far = head ^ 1, head ^ 2, head ^ 3
    greet_cross(n_blk, n_head)
    keep_w = pltpu.make_async_copy(w_ref.at[head], wr_ref.at[blk, head], local_sem.at[1])
    keep_w.start()
    wait_near = spread(1, n_head, lambda h: w_ref.at[h], wr_ref.at[blk, head], near_send, near_recv)

    def part(c):
        return pl.ds(c * rows, rows)

    def send(src, slot, owner, c, n, to):
        return pltpu.make_async_remote_copy(
            src_ref=src,
            dst_ref=xw_ref.at[slot, owner, part(c)],
            send_sem=x_send.at[n, c],
            recv_sem=x_recv.at[slot, owner, c],
            device_id=to,
            device_id_type=MESH,
        )

    def arrived(slot, owner, c):
        here = xw_ref.at[slot, owner, part(c)]
        pltpu.make_async_copy(here, here, x_recv.at[slot, owner, c]).wait()

    own = [x_ref.at[part(c)] for c in range(chunks)]
    started = []

    def go(copy):
        copy.start()
        started.append(copy)

    has_before, has_after = blk > 0, blk < n_blk - 1
    to_row = [send(own[c], 1, head, c, 0, (blk, row)) for c in range(chunks)]
    to_core = [send(own[c], 1, head, c, 1, (blk, core)) for c in range(chunks)]
    to_after = [send(own[c], 0, head, c, 2, (blk + 1, head)) for c in range(chunks)]
    to_before = [send(own[c], 2, head, c, 3, (blk - 1, head)) for c in range(chunks)]
    for c in range(chunks):
        go(to_row[c])

        @pl.when(has_after)
        def _():
            to_after[c].start()

        @pl.when(has_before)
        def _():
            to_before[c].start()

        go(to_core[c])
    keep_x = pltpu.make_async_copy(x_ref, xw_ref.at[1, head], local_sem.at[0])
    keep_x.start()
    keep_w.wait()
    wait_near()
    wait_w = spread(0, n_blk, lambda b: wr_ref.at[blk], wr_ref.at[blk], w_send, w_recv)

    for c in range(chunks):
        arrived(1, row, c)
        go(send(xw_ref.at[1, row, part(c)], 1, row, c, 4, (blk, core)))
    halo = []
    for c in range(chunks):
        for slot, there, n in ((0, has_before, 5), (2, has_after, 8)):
            on_row = send(xw_ref.at[slot, head, part(c)], slot, head, c, n, (blk, row))
            on_core = send(xw_ref.at[slot, head, part(c)], slot, head, c, n + 1, (blk, core))
            halo.append((there, on_row))
            halo.append((there, on_core))

            @pl.when(there)
            def _():
                arrived(slot, head, c)
                on_row.start()
                on_core.start()

    for c in range(chunks):
        arrived(1, core, c)
        arrived(1, far, c)
    keep_x.wait()
    load_x = pltpu.make_async_copy(xw_ref.at[1], x_own, local_sem.at[0])
    load_x.start()
    wait_w()
    load_w = pltpu.make_async_copy(wr_ref, got_ref, local_sem.at[1])
    load_w.start()
    load_w.wait()
    per = w_full.shape[0] // (n_blk * n_head)
    bias = jnp.zeros((1, w_full.shape[1]), F32)
    for b in range(n_blk):
        for h in range(n_head):
            first = (b * n_head + h) * per
            w_full[first : first + per] = got_ref[b, h, :per].astype(F32)
            bias = bias + got_ref[b, h, per + 1 : per + 2].astype(F32)
    turned_ref[...] = w_full[...].T.astype(BF16)
    bias_ref[...] = column(bias)
    keep_turned = pltpu.make_async_copy(turned_ref, turned_hbm, local_sem.at[1])
    keep_turned.start()
    load_x.wait()
    tok = x_ref.shape[0]

    def project(n, c):
        at = pl.ds(pl.multiple_of(n * tok, tok), tok)
        qkv_ref[:, at] = (mm_nt(turned_ref[...], x_own[n]) + bias_ref[...]).astype(BF16)
        return c

    lax.fori_loop(0, n_head, project, 0)
    keep_qkv = pltpu.make_async_copy(qkv_ref, qkv_hbm, local_sem.at[0])
    keep_qkv.start()

    vec_ref[...] = jnp.zeros_like(vec_ref)
    if per % 8 == 0:
        pieces = [got_ref[b, h, per : per + 1].astype(F32) for b in range(n_blk) for h in range(n_head)]
        for n in range(2, 8):
            vec_ref[n - 2 : n - 1] = jnp.concatenate([row[:, n * per : (n + 1) * per] for row in pieces], axis=1)
        hidden = inb_ref.shape[1] // len(pieces)
        inb_ref[...] = jnp.concatenate([row[:, 8 * per : 8 * per + hidden] for row in pieces], axis=1)
    else:
        inb_ref[...] = jnp.zeros_like(inb_ref)

    for c in range(chunks):
        for slot, there, n in ((0, has_before, 7), (2, has_after, 10)):
            relay = send(xw_ref.at[slot, row, part(c)], slot, row, c, n, (blk, core))
            halo.append((there, relay))

            @pl.when(there)
            def _():
                arrived(slot, row, c)
                relay.start()

    for c in range(chunks):
        for slot, there in ((0, has_before), (2, has_after)):

            @pl.when(there)
            def _():
                arrived(slot, core, c)
                arrived(slot, far, c)

    keep_turned.wait()
    keep_qkv.wait()
    for copy in started:
        copy.wait_send()
    for there, copies in ((has_after, to_after), (has_before, to_before)):

        @pl.when(there)
        def _():
            for copy in copies:
                copy.wait_send()

    for there, copy in halo:

        @pl.when(there)
        def _():
            copy.wait_send()


def collect(x, w, ff, n_blk, n_head):
    chunks = 2
    tok, width = x.shape
    wide = w.shape[2]
    rows = n_head * tok
    return pl.pallas_call(
        functools.partial(collect_body, n_blk, n_head, chunks),
        out_shape=(
            pltpu.HBM((3, n_head, *x.shape), x.dtype),
            pltpu.HBM((n_blk, *w.shape), w.dtype),
            pltpu.HBM((wide, rows), BF16),
            pltpu.HBM((wide, width), BF16),
            jax.ShapeDtypeStruct((wide, 1), F32),
            jax.ShapeDtypeStruct((8, width), F32),
            jax.ShapeDtypeStruct((1, ff), F32),
        ),
        in_specs=[ANY, ANY],
        out_specs=(ANY,) * 4 + (VMEM,) * 3,
        scratch_shapes=[
            pltpu.VMEM((n_head, tok, width), x.dtype),
            pltpu.VMEM((n_blk, *w.shape), w.dtype),
            pltpu.VMEM((width, wide), F32),
            pltpu.VMEM((wide, width), BF16),
            pltpu.VMEM((wide, rows), BF16),
            pltpu.SemaphoreType.DMA((2,)),
            pltpu.SemaphoreType.DMA((n_head,)),
            pltpu.SemaphoreType.DMA((n_head,)),
            pltpu.SemaphoreType.DMA((n_blk,)),
            pltpu.SemaphoreType.DMA((n_blk,)),
            pltpu.SemaphoreType.DMA((11, chunks)),
            pltpu.SemaphoreType.DMA((3, n_head, chunks)),
        ],
        compiler_params=pltpu.CompilerParams(collective_id=0, has_side_effects=True, vmem_limit_bytes=32 << 20),
        name="collect",
    )(in_hbm(x), in_hbm(w))


def finish_body(
    n_blk, n_head, part_ref, first_hbm, w_ref, t_ref, out_ref, dw_ref, dt_ref, part_row, part_own, first_ref, w_own, near, mine,
    far_in, w_in, t_in, w_sum, t_sum, w_end, t_end, load_sem, x_send, x_recv, w_send, w_recv, t_send, t_recv, w_send2, w_recv2,
    t_send2, t_recv2
):
    blk, head = place()
    core, row, far = head ^ 1, head ^ 2, head ^ 3

    def load(src, dst, n):
        copy = pltpu.make_async_copy(src, dst, load_sem.at[n])
        copy.start()
        return copy

    loads = [
        load(part_ref.at[row], part_row, 0), load(w_ref.at[blk], w_own, 1), load(part_ref.at[head], part_own, 2),
        load(first_hbm, first_ref, 3),
    ]
    greet_cross(n_blk, n_head)

    def send(src, dst, n, to):
        return pltpu.make_async_remote_copy(
            src_ref=src, dst_ref=dst, send_sem=x_send.at[n], recv_sem=x_recv.at[n], device_id=to, device_id_type=MESH
        )

    for_far = send(part_ref.at[far], near.at[1], 1, (blk, core))
    for_core = send(part_ref.at[core], near.at[0], 0, (blk, core))
    for_far.start()
    for_core.start()
    wait_w = spread(0, n_blk, lambda b: w_ref.at[b], w_in.at[blk], w_send, w_recv)
    wait_t = spread(0, n_blk, lambda b: t_ref.at[b], t_in.at[blk], t_send, t_recv)
    loads[0].wait()
    for_far.wait()
    mine[...] = (part_row[...].astype(F32) + near[1].astype(F32)).astype(BF16)
    for_row = send(mine, far_in, 2, (blk, row))
    for_row.start()
    wait_w()
    wait_t()
    loads[1].wait()
    w_sum[...] = w_own[...].astype(F32)
    t_sum[...] = t_ref[blk]

    def add(step, c):
        other = lax.rem(blk + step, n_blk)
        w_sum[...] += w_in[other].astype(F32)
        t_sum[...] += t_in[other]
        return c

    lax.fori_loop(1, n_blk, add, 0)
    wait_w2 = spread(1, n_head, lambda h: w_sum.at[h], w_end.at[head], w_send2, w_recv2)
    wait_t2 = spread(1, n_head, lambda h: t_sum.at[h], t_end.at[head], t_send2, t_recv2)
    w_end[head] = w_sum[head]
    t_end[head] = t_sum[head]
    for_core.wait()
    wait_w2()
    wait_t2()
    dt_ref[...] = jnp.sum(t_end[...], axis=0)
    parts = 3
    cut = dw_ref.shape[1] // (parts * n_head)
    for h in range(n_head):
        for p in range(parts):
            first = (p * n_head + h) * cut
            dw_ref[:, first : first + cut] = w_end[h, :, p * cut : (p + 1) * cut]
    loads[2].wait()
    loads[3].wait()
    for_row.wait()
    out_ref[...] = (
        first_ref[...] + part_own[...].astype(F32) + near[0].astype(F32) + far_in[...].astype(F32)
    ).astype(BF16)


def finish(part, d_first, w, table, n_blk, n_head):
    rows, width = d_first.shape
    _, _, per, wide = w.shape
    return pl.pallas_call(
        functools.partial(finish_body, n_blk, n_head),
        out_shape=(
            jax.ShapeDtypeStruct((rows, width), BF16),
            jax.ShapeDtypeStruct((per, 3 * width), F32),
            jax.ShapeDtypeStruct(table.shape[2:], F32),
        ),
        in_specs=[ANY, ANY, ANY, VMEM],
        out_specs=(VMEM,) * 3,
        scratch_shapes=[
            pltpu.VMEM((rows, width), BF16),
            pltpu.VMEM((rows, width), BF16),
            pltpu.VMEM((rows, width), F32),
            pltpu.VMEM(w.shape[1:], w.dtype),
            pltpu.VMEM((2, rows, width), BF16),
            pltpu.VMEM((rows, width), BF16),
            pltpu.VMEM((rows, width), BF16),
            pltpu.VMEM(w.shape, w.dtype),
            pltpu.VMEM(table.shape, F32),
            pltpu.VMEM(w.shape[1:], F32),
            pltpu.VMEM(table.shape[1:], F32),
            pltpu.VMEM(w.shape[1:], F32),
            pltpu.VMEM(table.shape[1:], F32),
            pltpu.SemaphoreType.DMA((4,)),
            pltpu.SemaphoreType.DMA((3,)),
            pltpu.SemaphoreType.DMA((3,)),
        ]
        + [pltpu.SemaphoreType.DMA((n_blk,))] * 4
        + [pltpu.SemaphoreType.DMA((n_head,))] * 4,
        compiler_params=pltpu.CompilerParams(collective_id=1, has_side_effects=True, vmem_limit_bytes=40 << 20),
        name="finish",
    )(in_hbm(part), in_hbm(d_first), in_hbm(w), table)


def greet(n_blk, n_head):
    blk, head = place()
    barrier = pltpu.get_barrier_semaphore()
    for step in range(1, n_head):
        pl.semaphore_signal(barrier, inc=1, device_id=(blk, lax.rem(head + step, n_head)), device_id_type=MESH)

    @pl.when(blk > 0)
    def _():
        pl.semaphore_signal(barrier, inc=1, device_id=(blk - 1, head), device_id_type=MESH)

    @pl.when(blk < n_blk - 1)
    def _():
        pl.semaphore_signal(barrier, inc=1, device_id=(blk + 1, head), device_id_type=MESH)

    pl.semaphore_wait(barrier, n_head - 1 + jnp.where(blk > 0, 1, 0) + jnp.where(blk < n_blk - 1, 1, 0))


def to_neighbours(n_blk, n_head, src, lo, hi, send_sem, recv_sem):
    blk, head = place()
    cases = (
        (blk > 0, blk < n_blk - 1, hi, (blk - 1, head)),
        (blk < n_blk - 1, blk > 0, lo, (blk + 1, head)),
    )

    def copy(n):
        return pltpu.make_async_remote_copy(
            src_ref=src, dst_ref=cases[n][2], send_sem=send_sem.at[n], recv_sem=recv_sem.at[n], device_id=cases[n][3],
            device_id_type=MESH,
        )

    for n in range(2):

        @pl.when(cases[n][0])
        def _():
            copy(n).start()

    def wait():
        for n in range(2):

            @pl.when(cases[n][0])
            def _():
                copy(n).wait_send()

            @pl.when(cases[n][1])
            def _():
                copy(n).wait_recv()

    return wait


def to_tokens_body(
    n_blk, n_head, out_ref, lse_ref, seq_ref, lse_lo_ref, lse_hi_ref, keep_sem, send_sem, recv_sem, lse_send, lse_recv
):
    blk, head = place()
    greet(n_blk, n_head)

    def part(h):
        return out_ref.at[h]

    def copy(step):
        to = lax.rem(head + step, n_head)
        return pltpu.make_async_remote_copy(
            src_ref=part(to), dst_ref=seq_ref.at[head], send_sem=send_sem.at[step], recv_sem=recv_sem.at[step],
            device_id=(blk, to), device_id_type=MESH,
        )

    for step in range(n_head - 1, 0, -1):
        copy(step).start()
    keep = pltpu.make_async_copy(part(head), seq_ref.at[head], keep_sem)
    keep.start()
    wait = to_neighbours(n_blk, n_head, lse_ref, lse_lo_ref, lse_hi_ref, lse_send, lse_recv)
    for step in range(1, n_head):
        copy(step).wait()
    wait()
    keep.wait()


def to_tokens(out, lse, n_blk, n_head):
    stat = jax.ShapeDtypeStruct(lse.shape, lse.dtype)
    return pl.pallas_call(
        functools.partial(to_tokens_body, n_blk, n_head),
        out_shape=(jax.ShapeDtypeStruct(out.shape, out.dtype), stat, stat),
        in_specs=[ANY, ANY],
        out_specs=(ANY,) * 3,
        scratch_shapes=[
            pltpu.SemaphoreType.DMA,
            pltpu.SemaphoreType.DMA((n_head,)),
            pltpu.SemaphoreType.DMA((n_head,)),
            pltpu.SemaphoreType.DMA((2,)),
            pltpu.SemaphoreType.DMA((2,)),
        ],
        compiler_params=pltpu.CompilerParams(collective_id=2, has_side_effects=True),
        name="to_tokens",
    )(in_hbm(out), in_hbm(lse))


def to_heads_body(
    n_blk, n_head, dseq_ref, dpart_ref, do_ref, delta_ref, delta_lo_ref, delta_hi_ref, keep_sem, send_sem, recv_sem, d_send,
    d_recv, n_send, n_recv
):
    blk, head = place()
    tok = dseq_ref.shape[2]
    greet(n_blk, n_head)
    at = pl.ds(pl.multiple_of(head * tok, tok), tok)

    def copy(step):
        to = lax.rem(head + step, n_head)
        return pltpu.make_async_remote_copy(
            src_ref=dseq_ref.at[to], dst_ref=do_ref.at[:, at], send_sem=send_sem.at[step], recv_sem=recv_sem.at[step],
            device_id=(blk, to), device_id_type=MESH,
        )

    def small_copy(step):
        to = lax.rem(head + step, n_head)
        return pltpu.make_async_remote_copy(
            src_ref=dpart_ref.at[to], dst_ref=delta_ref.at[head], send_sem=d_send.at[step], recv_sem=d_recv.at[step],
            device_id=(blk, to), device_id_type=MESH,
        )

    keep = (
        pltpu.make_async_copy(dseq_ref.at[head], do_ref.at[:, at], keep_sem.at[0]),
        pltpu.make_async_copy(dpart_ref.at[head], delta_ref.at[head], keep_sem.at[1]),
    )
    for step in range(n_head - 1, 0, -1):
        small_copy(step).start()
        copy(step).start()
    for local in keep:
        local.start()
    for step in range(1, n_head):
        small_copy(step).wait()
    keep[1].wait()
    wait = to_neighbours(n_blk, n_head, delta_ref, delta_lo_ref, delta_hi_ref, n_send, n_recv)
    for step in range(1, n_head):
        copy(step).wait()
    keep[0].wait()
    wait()


def to_heads(d_seq, d_part, n_blk, n_head):
    _, cut, tok = d_seq.shape
    stat = jax.ShapeDtypeStruct(d_part.shape, F32)
    return pl.pallas_call(
        functools.partial(to_heads_body, n_blk, n_head),
        out_shape=(jax.ShapeDtypeStruct((cut, n_head * tok), BF16), stat, stat, stat),
        in_specs=[ANY, ANY],
        out_specs=(ANY,) * 4,
        scratch_shapes=[
            pltpu.SemaphoreType.DMA((2,)),
            pltpu.SemaphoreType.DMA((n_head,)),
            pltpu.SemaphoreType.DMA((n_head,)),
            pltpu.SemaphoreType.DMA((n_head,)),
            pltpu.SemaphoreType.DMA((n_head,)),
            pltpu.SemaphoreType.DMA((2,)),
            pltpu.SemaphoreType.DMA((2,)),
        ],
        compiler_params=pltpu.CompilerParams(collective_id=3, has_side_effects=True),
        name="to_heads",
    )(in_hbm(d_seq), in_hbm(d_part))


def regroup(values, outer, inner, unit):
    if unit % 8:
        return values.reshape(-1, outer, inner, unit).transpose(0, 2, 1, 3).reshape(values.shape)
    at = lambda o, i: slice((o * inner + i) * unit, (o * inner + i + 1) * unit)
    return jnp.concatenate([values[:, at(o, i)] for i in range(inner) for o in range(outer)], axis=1)


def pack_body(*refs, count, blocks, n_head):
    (in_ref, mid_ref, down_ref, qkv_ref), vectors, (packed_ref, send_ref) = refs[:4], refs[4:-2], refs[-2:]
    unit, width = mid_ref.shape
    ff = blocks * width
    packed_ref[:, :ff] = regroup(in_ref[...].astype(F32), count, blocks, unit).astype(BF16)
    packed_ref[:, ff : ff + width] = mid_ref[...]
    for n in range(blocks):
        packed_ref[:, ff + width * (n + 1) : ff + width * (n + 2)] = down_ref[n * unit : (n + 1) * unit]

    cut = width // n_head
    vectors = [ref[...].astype(F32) for ref in vectors]
    joined = jnp.concatenate(vectors, axis=1)
    wide = 3 * cut
    pieces = jnp.concatenate([joined, jnp.zeros((1, wide - joined.shape[1]), F32)], axis=1)
    blk, head = place()
    me = blk * n_head + head
    spots = cut // unit

    def in_place(vec):
        return jnp.concatenate([jnp.where(lax.rem(me, spots) == n, vec, 0.0) for n in range(spots)], axis=1)

    placed = jnp.concatenate([in_place(vectors[0]), jnp.zeros((1, cut), F32), in_place(vectors[1])], axis=1)
    weights = qkv_ref[...].astype(F32)
    rest = jnp.zeros((BIAS_ROWS - 2, wide), F32)
    for h in range(n_head):
        columns = jnp.concatenate([weights[:, p * width + h * cut : p * width + (h + 1) * cut] for p in range(3)], axis=1)
        mine = jnp.where(me // spots == h, placed, 0.0)
        send_ref[h] = jnp.concatenate([columns, pieces, mine, rest], axis=0).astype(BF16)


def pack(w_in, w_out, w_down, w_qkv, vectors, count, n_head):
    unit, width = w_out.shape
    blocks = w_down.shape[0] // unit
    cut = width // n_head
    if unit % 8:
        down = w_down.reshape(blocks, unit, width).transpose(1, 0, 2).reshape(unit, -1)
        joined = jnp.concatenate(vectors)
        blk, head = place()
        me = blk * n_head + head
        spots = cut // unit
        zeros = jnp.zeros((cut,), BF16)
        at = lax.rem(me, spots) * unit
        placed = jnp.concatenate(
            [
                lax.dynamic_update_slice_in_dim(zeros, vectors[0], at, 0),
                zeros,
                lax.dynamic_update_slice_in_dim(zeros, vectors[1], at, 0),
            ]
        )
        owner = (jnp.arange(n_head) == me // spots)[:, None]
        rows = jnp.stack(
            [
                jnp.broadcast_to(jnp.pad(joined, (0, 3 * cut - joined.shape[0]))[None], (n_head, 3 * cut)),
                jnp.where(owner, placed[None], jnp.zeros((), BF16)),
            ]
            + [jnp.zeros((n_head, 3 * cut), BF16)] * (BIAS_ROWS - 2),
            axis=1,
        )
        columns = w_qkv.reshape(unit, 3, n_head, cut).transpose(2, 0, 1, 3).reshape(n_head, unit, 3 * cut)
        packed = jnp.concatenate([regroup(w_in, count, blocks, unit), w_out, down], axis=1)
        return packed, jnp.concatenate([columns, rows], axis=1)
    return pl.pallas_call(
        functools.partial(pack_body, count=count, blocks=blocks, n_head=n_head),
        out_shape=(
            jax.ShapeDtypeStruct((unit, 2 * w_in.shape[1] + width), BF16),
            jax.ShapeDtypeStruct((n_head, unit + BIAS_ROWS, 3 * cut), BF16),
        ),
        in_specs=[VMEM] * (4 + len(vectors)),
        out_specs=(VMEM, VMEM),
        name="pack",
    )(w_in, w_out, w_down, w_qkv, *(vec[None] for vec in vectors))


def unpack_body(packed_ref, in_ref, mid_ref, down_ref, *, count, blocks):
    unit, width = mid_ref.shape
    ff = blocks * width
    in_ref[...] = regroup(packed_ref[:, :ff].astype(F32), blocks, count, unit)
    mid_ref[...] = packed_ref[:, ff : ff + width].astype(F32)
    for n in range(blocks):
        down_ref[n * unit : (n + 1) * unit] = packed_ref[:, ff + width * (n + 1) : ff + width * (n + 2)].astype(F32)


def unpack(packed, width, count):
    unit = packed.shape[0]
    blocks = (packed.shape[1] // width - 1) // 2
    ff = blocks * width
    if unit % 8:
        packed = packed.astype(F32)
        down = packed[:, ff + width :].reshape(unit, blocks, width).transpose(1, 0, 2).reshape(-1, width)
        return regroup(packed[:, :ff], blocks, count, unit), packed[:, ff : ff + width], down
    return pl.pallas_call(
        functools.partial(unpack_body, count=count, blocks=blocks),
        out_shape=(
            jax.ShapeDtypeStruct((unit, ff), F32),
            jax.ShapeDtypeStruct((unit, width), F32),
            jax.ShapeDtypeStruct((unit * blocks, width), F32),
        ),
        in_specs=[VMEM],
        out_specs=(VMEM,) * 3,
        name="unpack",
    )(packed)


def normalize(values):
    centre = jnp.mean(values, axis=-1, keepdims=True)
    centered = values - centre
    r = lax.rsqrt(jnp.mean(centered * centered, axis=-1, keepdims=True) + 1e-05)
    return centered * r, r


def normalize_back(d_values, unit, r, gain):
    scaled = d_values * gain
    return r * (
        scaled - jnp.mean(scaled, axis=-1, keepdims=True) - unit * jnp.mean(scaled * unit, axis=-1, keepdims=True)
    )


def over_rows(values):
    return jnp.sum(values, axis=0, keepdims=True)


def dense_body(
    x_ref, seq_ref, cot_ref, vec_ref, inb_ref, w_hbm, out_ref, first_ref, dseq_ref, delta_ref, dvec_ref, dinb_ref, grad_hbm, bias_ref, dbias_ref, w, grad,
    unit_ref, r_ref, normed_ref, low_ref, acc_ref, slope_ref, act_ref, e_ref, w_sem, grad_sem, *, blocks, count
):
    width = x_ref.shape[1]
    out_at, down_at = blocks * width, (blocks + 1) * width

    def fetch(first, size, n):
        at = pl.ds(first, size)
        copy = pltpu.make_async_copy(w_hbm.at[:, at], w.at[:, at], w_sem.at[n])
        copy.start()
        return copy

    def cols(first, c):
        return pl.ds(pl.multiple_of(first + c * width, 128), width)

    def put(first, c, n):
        at = cols(first, c)
        return pltpu.make_async_copy(grad.at[:, at], grad_hbm.at[:, at], grad_sem.at[n])

    piece = width // count
    bias_ref[...] = inb_ref[...] if piece % 8 else regroup(inb_ref[...], count, blocks, piece)
    w_out_here = fetch(out_at, width, 0)
    w_in_here = fetch(0, out_at, 1)
    w_down_here = fetch(down_at, blocks * width, 2)
    out_bias, ln1_gain, ln1_bias, down_bias, ln2_gain, ln2_bias = (vec_ref[n : n + 1] for n in range(6))
    w_out_here.wait()
    unit, r = normalize(x_ref[...].astype(F32) + mm_tn(seq_ref[...], w[:, out_at:down_at]) + out_bias)
    unit_ref[...] = unit
    r_ref[...] = r
    normed = unit * ln1_gain + ln1_bias
    normed_ref[...] = normed
    low_ref[...] = normed.astype(BF16)
    acc_ref[...] = normed + down_bias
    w_in_here.wait()
    w_down_here.wait()

    def up_down(c, carry):
        at = cols(0, c)
        hidden = mm(low_ref[...], w[:, at]) + bias_ref[:, at]
        phi = 0.5 + 0.5 * lax.erf(hidden * (2.0**-0.5))
        act = (hidden * phi).astype(BF16)
        act_ref[:, at] = act
        slope_ref[:, at] = phi + hidden * (jnp.exp(-0.5 * hidden * hidden) * ((2.0 * math.pi) ** -0.5))
        acc_ref[...] += mm(act, w[:, cols(down_at, c)])
        return carry

    lax.fori_loop(0, blocks, up_down, 0, unroll=True)
    unit2, r2 = normalize(acc_ref[...])
    out_ref[...] = (unit2 * ln2_gain + ln2_bias).astype(BF16)
    dy = cot_ref[...].astype(F32)
    dvec_ref[4:5] = over_rows(dy * unit2)
    dvec_ref[5:6] = over_rows(dy)
    d_second = normalize_back(dy, unit2, r2, ln2_gain)
    e_ref[...] = d_second.astype(BF16)
    dvec_ref[3:4] = over_rows(e_ref[...].astype(F32))
    acc_ref[...] = d_second

    def back(c, carry):
        at, down = cols(0, c), cols(down_at, c)
        e = e_ref[...]
        d_hidden = (mm_nt(e, w[:, down]) * slope_ref[:, at]).astype(BF16)
        dbias_ref[:, at] = over_rows(d_hidden.astype(F32))
        acc_ref[...] += mm_nt(d_hidden, w[:, at])
        grad[:, at] = mm_tn(low_ref[...], d_hidden).astype(BF16)
        put(0, c, c).start()
        grad[:, down] = mm_tn(act_ref[:, at], e).astype(BF16)
        put(down_at, c, blocks + c).start()
        return carry

    lax.fori_loop(0, blocks, back, 0, unroll=2)
    d_normed = acc_ref[...]
    unit = unit_ref[...]
    dvec_ref[1:2] = over_rows(d_normed * unit)
    dvec_ref[2:3] = over_rows(d_normed)
    d_first = normalize_back(d_normed, unit, r_ref[...], ln1_gain)
    first_ref[...] = d_first
    e_first = d_first.astype(BF16)
    dvec_ref[0:1] = over_rows(e_first.astype(F32))
    grad[:, out_at:down_at] = mm(seq_ref[...], e_first).astype(BF16)
    put(out_at, 0, 2 * blocks).start()
    d_seq = mm_nt(w[:, out_at:down_at], e_first).astype(BF16)
    dseq_ref[...] = d_seq
    product = d_seq.astype(F32) * seq_ref[...].astype(F32)
    n_head, groups, _ = delta_ref.shape
    for n in range(n_head):
        for g in range(groups):
            first = (n * groups + g) * HEAD_DIM
            delta_ref[n, g : g + 1] = over_rows(product[first : first + HEAD_DIM])

    dinb_ref[...] = dbias_ref[...] if piece % 8 else regroup(dbias_ref[...], blocks, count, piece)

    def done(c, carry):
        put(0, c, c).wait()
        put(down_at, c, blocks + c).wait()
        return carry

    lax.fori_loop(0, blocks, done, 0)
    put(out_at, 0, 2 * blocks).wait()


def dense(x, seq_t, cotangent, vectors, in_bias, weights, blocks, n_head, count):
    tok, width = x.shape
    ff = blocks * width
    return pl.pallas_call(
        functools.partial(dense_body, blocks=blocks, count=count),
        out_shape=(
            jax.ShapeDtypeStruct((tok, width), BF16),
            jax.ShapeDtypeStruct((tok, width), F32),
            jax.ShapeDtypeStruct((width, tok), BF16),
            jax.ShapeDtypeStruct((n_head, width // n_head // HEAD_DIM, tok), F32),
            jax.ShapeDtypeStruct((8, width), F32),
            jax.ShapeDtypeStruct((1, ff), F32),
            jax.ShapeDtypeStruct(weights.shape, BF16),
        ),
        in_specs=[VMEM] * 5 + [ANY],
        out_specs=(VMEM,) * 6 + (ANY,),
        scratch_shapes=[
            pltpu.VMEM((1, ff), F32),
            pltpu.VMEM((1, ff), F32),
            pltpu.VMEM(weights.shape, BF16),
            pltpu.VMEM(weights.shape, BF16),
            pltpu.VMEM((tok, width), F32),
            pltpu.VMEM((tok, 1), F32),
            pltpu.VMEM((tok, width), F32),
            pltpu.VMEM((tok, width), BF16),
            pltpu.VMEM((tok, width), F32),
            pltpu.VMEM((tok, ff), F32),
            pltpu.VMEM((tok, ff), BF16),
            pltpu.VMEM((tok, width), BF16),
            pltpu.SemaphoreType.DMA((3,)),
            pltpu.SemaphoreType.DMA((2 * blocks + 1,)),
        ],
        compiler_params=pltpu.CompilerParams(vmem_limit_bytes=58 << 20),
        cost_estimate=pl.CostEstimate(flops=17_000_000_000, bytes_accessed=30_000_000, transcendentals=3_000_000),
        name="dense",
    )(x, seq_t, cotangent, vectors, in_bias, weights)


def window_of(segments, blk, rows, tile):
    padded = jnp.concatenate(
        [jnp.full((rows,), -1, jnp.int32), segments, jnp.full((rows,), 1 << 30, jnp.int32)]
    )
    seg = lax.dynamic_slice_in_dim(padded, blk * rows, 3 * rows, 0)
    own = seg[rows : 2 * rows]
    below = jnp.sum((seg[None, :] < own[::tile][:, None]).astype(jnp.int32), axis=1)
    upto = jnp.sum((seg[None, :] <= own[tile - 1 :: tile][:, None]).astype(jnp.int32), axis=1)
    return seg[None], below // tile, (upto - 1) // tile + 1


def shift(value, steps):
    count = lax.axis_size("blk")
    first, last = max(0, -steps), min(count, count - steps)
    return lax.ppermute(value, "blk", [(source, source + steps) for source in range(first, last)])


def body(
    inputs, segments, cotangent, w_qkv, q_bias, v_bias, w_out, out_bias, ln1_gain, ln1_bias, w_in, in_bias, w_down,
    down_bias, ln2_gain, ln2_bias
):
    n_blk, n_head = lax.axis_size("blk"), lax.axis_size("head")
    count = n_blk * n_head
    blk, head = place()
    tok, width = inputs.shape
    rows = tok * n_head
    per = w_qkv.shape[0]
    ff = w_in.shape[1]
    blocks = ff // width
    cut = width // n_head
    groups = cut // HEAD_DIM

    small = (q_bias, v_bias, out_bias, ln1_gain, ln1_bias, down_bias, ln2_gain, ln2_bias, in_bias)
    packed, to_send = pack(w_in, w_out, w_down, w_qkv, small, count, n_head)
    whole = lax.all_gather(packed, BOTH, axis=0, tiled=True)

    x_win, got, own_qkv, turned, qkv_bias, vectors, hidden_bias = collect(inputs, to_send, ff, n_blk, n_head)
    x_win = x_win.reshape(3 * rows, width)
    offsets = [0]
    for vec in small:
        offsets.append(offsets[-1] + vec.shape[0])
    if per % 8:
        got = got.reshape(count, *got.shape[2:])
        all_small = got[:, per, : offsets[-1]].astype(F32)
        full = [all_small[:, a:b].reshape(-1) for a, b in zip(offsets[:-1], offsets[1:])]
        vectors = jnp.stack(full[2:8] + full[2:4])
        hidden_bias = regroup(full[8][None], count, blocks, per)
    seg, lo, hi = window_of(segments, blk, rows, tok)
    attended, lse, qkv = attend(x_win, own_qkv, turned, qkv_bias, seg, lo, hi, groups, rows, tok)
    seq_t, lse_lo, lse_hi = to_tokens(attended, lse, n_blk, n_head)
    seq_t = seq_t.reshape(width, tok)

    outputs, d_first, d_seq_t, d_part, d_vectors, d_in_bias, grads = dense(
        inputs, seq_t, cotangent, vectors, hidden_bias, whole, blocks, n_head, count
    )
    d_out_bias, d_ln1_gain, d_ln1_bias, d_down_bias, d_ln2_gain, d_ln2_bias = (d_vectors[n] for n in range(6))
    if per % 8:
        d_in_bias = regroup(d_in_bias, blocks, count, per)
    d_in_bias = d_in_bias[0]
    d_out, delta, delta_lo, delta_hi = to_heads(d_seq_t.reshape(n_head, cut, tok), d_part, n_blk, n_head)
    delta, delta_lo, delta_hi = (a.transpose(1, 0, 2).reshape(groups, rows) for a in (delta, delta_lo, delta_hi))

    owned = lax.psum_scatter(grads, BOTH, scatter_dimension=0, tiled=True)

    do_lo, do_hi = shift(d_out, 1), shift(d_out, -1)
    dq, dk, dv = own_grads(qkv, d_out, lse, delta, seg, lo, hi, groups, rows, tok)
    d_w_qkv, d_part, d_biases = outer_grads(
        qkv, do_lo, do_hi, lse_lo, lse_hi, delta_lo, delta_hi, seg, dq, dk, dv, turned, x_win, lo, hi, groups, rows, tok
    )
    d_biases = d_biases[:, 0]
    place_own = lambda vec: lax.dynamic_update_slice_in_dim(jnp.zeros((width,), F32), vec, head * cut, 0)
    vectors = (
        place_own(d_biases[:cut]), place_own(d_biases[2 * cut :]), d_out_bias, d_ln1_gain, d_ln1_bias, d_down_bias, d_ln2_gain,
        d_ln2_bias, d_in_bias,
    )
    table = jnp.concatenate([vec.reshape(count, -1) for vec in vectors], axis=1)
    lanes = 128
    table_rows = -(-table.shape[1] // (8 * lanes)) * 8
    table = jnp.pad(table, ((0, 0), (0, table_rows * lanes - table.shape[1])))
    d_inputs, own_w_qkv, sums = finish(
        d_part.reshape(n_head, tok, width), d_first, d_w_qkv.reshape(n_blk, n_head, per, 3 * cut),
        table.reshape(n_blk, n_head, table_rows, lanes), n_blk, n_head,
    )
    sums = sums.reshape(-1)
    (o_q_bias, o_v_bias, o_out_bias, o_ln1_gain, o_ln1_bias, o_down_bias, o_ln2_gain, o_ln2_bias, o_in_bias) = (
        sums[a:b] for a, b in zip(offsets[:-1], offsets[1:])
    )
    own_w_in, own_w_out, own_w_down = unpack(owned, width, count)
    return (
        outputs, d_inputs, own_w_qkv, o_q_bias, o_v_bias, own_w_out, o_out_bias, o_ln1_gain, o_ln1_bias,
        own_w_in, o_in_bias, own_w_down, o_down_bias, o_ln2_gain, o_ln2_bias,
    )


def solution(mesh):
    rows, vec = P(BOTH, None), P(BOTH)
    placed = (rows, P(), rows, rows, vec, vec, rows, vec, vec, vec, rows, vec, rows, vec, vec, vec)
    return jax.shard_map(
        body,
        mesh=mesh,
        in_specs=placed,
        out_specs=(rows, rows, rows, vec, vec, rows, vec, vec, vec, rows, vec, rows, vec, vec, vec),
        check_vma=False,
    )
```
